32 devices in a mesh: gx: 8 (over y, x, core), gy: 4 (over z).
Axes of the slice: x: 2, y: 2, z: 4, core: 2. Of those that a mesh axis runs over, the one named last changes fastest.
Arguments:
- control: float32 [3, 64, 256, 1024], P(None, None, 'gy', 'gx')
- spread: float32 [3, 256, 1024], P(None, 'gy', 'gx'), may hold values from 0.5 to 2
- kernel_east: float32 [3, 9], replicated, may hold values from -1.5 to 1.5
- kernel_north: float32 [3, 9], replicated, may hold values from -1.5 to 1.5
- vertical: float32 [3, 64, 64], replicated, may hold values from -0.75 to 0.75
- tile_owner: int32 [16384], P(('gx', 'gy')), may hold values from 0 to 31, as said below
- gate_level: int32 [16384], P(('gx', 'gy')), may hold values from 0 to 63
- tile_row: int32 [16384], P(('gx', 'gy')), may hold values from 0 to 63
- beam_azimuth: int32 [16384], P(('gx', 'gy')), may hold values from 80 to 280, as said below
- innovation: float32 [16384, 2, 128], P(('gx', 'gy')), may hold values from -6 to 6
- obs_weight: float32 [16384, 2, 128], P(('gx', 'gy')), may hold values from 0.25 to 4
Outputs:
- gradient: float32 [3, 64, 256, 1024], P(None, None, 'gy', 'gx')
- cost: float32 [2], replicated
The draws below stay inside these ranges and needn't reach their ends.
Inputs may be any that keep to these rules, and one draw needn't show every extreme that they name: `tile_owner`: among the gate rows of one device no tile is named more than 32 times; one tile is named exactly 32 times by the rows of every device. `beam_azimuth`: every azimuth lies within 10 degrees of due east (90) or due west (270).
All inputs are finite; a program needn't handle non-finite values.
Results may differ from the reference program's by a relative error of at most 0.00009.
Values sent between devices are 32-bit elements; how exact they have to be, the bound alone decides.
A program may use at most 192 MiB of HBM per device.

```python
import math
import jax
import jax.numpy as jnp
from jax import lax

FIELDS = 3
NZ = 64
GATES = 128
W = 8
CY = 64
GROW_DEV = 512
CX = 128
TILES = 32
MOST = 32
NX = 1024
NY = 256
GROWS = 16384
N_GX = 8
N_GY = 4


def draw_control(key, part):
    shape = (FIELDS, NZ, NY, NX)
    east = jnp.arange(NX, dtype=jnp.float32) / NX
    north = jnp.arange(NY, dtype=jnp.float32) / NY
    ramp = (0.5 + east)[None, None, None, :] * (0.75 + 0.5 * north)[None, None, :, None]
    base = jax.random.normal(jax.random.fold_in(key, 5), shape, jnp.float32)
    return (base * ramp).astype(jnp.float32)


def draw_tile_owner(key, part):
    base = jax.random.fold_in(key, 11)
    favourite = jax.random.randint(jax.random.fold_in(base, 1), (), 0, TILES)
    block_keys = jax.random.split(jax.random.fold_in(base, 2), TILES)

    def one_block(block_key):
        size_key, order_key, mixing_key = jax.random.split(block_key, 3)
        sizes = jax.random.randint(size_key, (TILES,), MOST // 2, MOST + 1)
        sizes = sizes.at[0].set(MOST)
        bounds = jnp.cumsum(sizes)
        positions = jnp.arange(GROW_DEV, dtype=jnp.int32)
        group = jnp.sum((bounds[None, :] <= positions[:, None]).astype(jnp.int32), axis=1)
        others = jax.random.permutation(order_key, TILES - 1).astype(jnp.int32)
        others = others + (others >= favourite).astype(jnp.int32)
        order = jnp.concatenate([favourite[None].astype(jnp.int32), others])
        chosen = order[group]
        mixing = jax.random.permutation(mixing_key, GROW_DEV)
        return chosen[mixing]
    return jax.vmap(one_block)(block_keys).reshape(GROWS).astype(jnp.int32)


def draw_beam_azimuth(key, part):
    base = jax.random.fold_in(key, 23)
    side = jax.random.randint(jax.random.fold_in(base, 1), (GROWS,), 0, 2)
    offset = jax.random.randint(jax.random.fold_in(base, 2), (GROWS,), 0, 21)
    azimuth = 80 + 180 * side + offset
    azimuth = azimuth.at[0].set(80).at[1].set(280)
    return azimuth.astype(jnp.int32)


def plant(result, key, low, top_value):
    longest = result.shape.index(max(result.shape))
    spots = []
    for shift in (0, 1):
        where = [jax.random.randint(jax.random.fold_in(key, axis), (), 0, length) for axis, length in enumerate(result.shape)]
        where[longest] = (where[longest] + shift) % result.shape[longest]
        spots.append(tuple(where))
    return result.at[spots[0]].set(low).at[spots[1]].set(top_value)


def levels(stream_key, dims, shards, low, largest):
    factor_of = 1.0
    for position, blocks in shards:
        draws = jax.random.uniform(jax.random.fold_in(jax.random.fold_in(stream_key, 6), position), (blocks,), jnp.float32, low / len(shards), largest / len(shards))
        factor_of = factor_of * jnp.repeat(jnp.exp(draws), dims[position] // blocks).reshape((-1,) + (1,) * (len(dims) - 1 - position))
    return factor_of


def centred(key, shape, deviation, limit, cuts=(), kind=jnp.bfloat16):
    entries = jax.random.normal(key, shape, jnp.float32) * deviation
    if len(cuts) > 0:
        entries = levels(key, shape, cuts, -0.22, 0.18) * entries
    return jnp.clip(entries, min=-limit, max=limit).astype(kind)


def setup_inputs(seed: int = 0) -> dict:
    streams_of = jax.random.split(jax.random.key(seed), 12)
    return {
        "control": draw_control(jax.random.fold_in(streams_of[11], 71), 0),
        "spread": jnp.clip(jnp.exp(math.log(2.0) - 1.3862944 * jax.random.uniform(streams_of[1], (FIELDS, NY, NX), jnp.float32) ** levels(streams_of[1], (FIELDS, NY, NX), ((1, 4), (2, 8)), -0.2, 0.2)), 0.5, 2.0),
        "kernel_east": centred(streams_of[2], (FIELDS, W + 1), (2 * W + 1) ** -0.5, 1.5, (), jnp.float32),
        "kernel_north": centred(streams_of[3], (FIELDS, W + 1), (2 * W + 1) ** -0.5, 1.5, (), jnp.float32),
        "vertical": centred(streams_of[4], (FIELDS, NZ, NZ), NZ ** -0.5, 0.75, (), jnp.float32),
        "tile_owner": draw_tile_owner(jax.random.fold_in(streams_of[11], 71), 0),
        "gate_level": plant(jax.random.randint(streams_of[6], (GROWS,), 0, NZ), jax.random.fold_in(streams_of[6], 1), 0, NZ - 1).astype(jnp.int32),
        "tile_row": plant(jax.random.randint(streams_of[7], (GROWS,), 0, CY), jax.random.fold_in(streams_of[7], 1), 0, CY - 1).astype(jnp.int32),
        "beam_azimuth": draw_beam_azimuth(jax.random.fold_in(streams_of[11], 71), 0),
        "innovation": centred(streams_of[9], (GROWS, 2, GATES), 1.0, 6.0, ((0, 32),), jnp.float32),
        "obs_weight": jnp.clip(jnp.exp(math.log(4.0) - 2.7725887 * jax.random.uniform(streams_of[10], (GROWS, 2, GATES), jnp.float32) ** levels(streams_of[10], (GROWS, 2, GATES), ((0, 32),), -0.2, 0.2)), 0.25, 4.0),
    }


def full_taps(kernel):
    return jnp.concatenate([kernel[:, ::-1], kernel[:, 1:]], axis=1)


def filter_axis(field, kernel, axis):
    weights = full_taps(kernel)

    def one_field(pair):
        slab, taps = pair
        widths = [(0, 0), (0, 0), (0, 0)]
        widths[axis - 1] = (W, W)
        padded = jnp.pad(slab, widths)
        length = slab.shape[axis - 1]
        total = jnp.zeros_like(slab)
        for shift in range(2 * W + 1):
            total = total + taps[shift] * lax.slice_in_dim(padded, shift, shift + length, axis=axis - 1)
        return total

    return lax.map(one_field, (field, weights))


def reference(control, spread, kernel_east, kernel_north, vertical, tile_owner, gate_level, tile_row, beam_azimuth, innovation, obs_weight):
    smoothed = filter_axis(filter_axis(control, kernel_east, 3), kernel_north, 2)
    state_field = spread[:, None] * jnp.einsum("fkz,fzyx->fkyx", vertical, smoothed, precision=lax.Precision.HIGHEST)
    blocks = state_field.reshape(FIELDS, NZ, N_GY, CY, N_GX, CX)
    north_index = tile_owner % N_GY
    east_index = tile_owner // N_GY
    picked = blocks[:, gate_level, north_index, tile_row, east_index, :]
    angle = beam_azimuth.astype(jnp.float32) * (2.0 * math.pi / 360.0)
    cosine = jnp.cos(angle)[:, None]
    sine = jnp.sin(angle)[:, None]
    radial = picked[0] * cosine + picked[1] * sine
    modelled = jnp.stack([radial, picked[2]], axis=1)
    departure = modelled - innovation
    weighted = obs_weight * departure
    back_cost = 0.5 * jnp.sum(control * control) / (FIELDS * NZ * NY * NX)
    obs_cost = 0.5 * jnp.sum(weighted * departure) / (2 * GROWS * GATES)
    pushed = jnp.stack([weighted[:, 0] * cosine, weighted[:, 0] * sine, weighted[:, 1]], axis=0)
    adjoint = jnp.zeros((FIELDS, NZ, N_GY, CY, N_GX, CX), jnp.float32)
    adjoint = adjoint.at[:, gate_level, north_index, tile_row, east_index, :].add(pushed)
    adjoint = adjoint.reshape(FIELDS, NZ, NY, NX) * spread[:, None]
    lifted = jnp.einsum("fkz,fkyx->fzyx", vertical, adjoint, precision=lax.Precision.HIGHEST)
    gradient = control + filter_axis(filter_axis(lifted, kernel_east, 3), kernel_north, 2)
    return gradient, jnp.stack([back_cost, obs_cost])
```

```python
import functools
import math

import jax
import jax.numpy as jnp
from jax import lax
from jax.experimental import pallas as pl
from jax.experimental.pallas import tpu as pltpu
from jax.sharding import PartitionSpec as P

F32 = jnp.float32
BF16 = jnp.bfloat16
I32 = jnp.int32
VMEM_BYTES = 56 * 1024 * 1024
MESH = pl.DeviceIdType.MESH


def params():
    return pltpu.CompilerParams(vmem_limit_bytes=VMEM_BYTES)


def split(value):
    high = value.astype(BF16)
    low = (value - high.astype(F32)).astype(BF16)
    return high, low


def doubled(weights):
    high, low = split(weights)
    row = jnp.concatenate([high, low], axis=1)
    return jnp.concatenate([row, row], axis=0)


def times(rows, weights):
    high, low = split(rows)
    both = jnp.dot(
        jnp.concatenate([high, low], axis=1), weights, preferred_element_type=F32
    )
    half = both.shape[1] // 2
    return both[:, :half] + both[:, half:]


def taps_at(kernel_ref, f, distance, allowed):
    total = jnp.zeros(distance.shape, F32)
    for d in range(kernel_ref.shape[1]):
        total = jnp.where(distance == d, kernel_ref[f, d], total)
    return jnp.where(allowed, total, 0.0)


def main_band(kernel_ref, f):
    r = lax.broadcasted_iota(I32, (128, 128), 0)
    c = lax.broadcasted_iota(I32, (128, 128), 1)
    return doubled(taps_at(kernel_ref, f, jnp.abs(r - c), jnp.abs(r - c) <= 8))


def rim_band(kernel_ref, f, offset):
    r = (lax.broadcasted_iota(I32, (128, 128), 0) + (128 - offset)) & 127
    c = (lax.broadcasted_iota(I32, (128, 128), 1) + (128 - offset)) & 127
    distance = jnp.abs(r - c)
    fits = ((r >> 4) == (c >> 4)) & ((r & 8) != (c & 8)) & (distance <= 8)
    return doubled(taps_at(kernel_ref, f, distance, fits))


def north_band(kernel_ref, f, ys):
    reach = ys + 16
    r = lax.broadcasted_iota(I32, (ys, 3 * reach), 0)
    c = lax.broadcasted_iota(I32, (ys, 3 * reach), 1)
    j = jnp.where(c >= reach, c - reach, c)
    j = jnp.where(c >= 2 * reach, c - 2 * reach, j)
    distance = jnp.abs(r + 8 - j)
    taps = taps_at(kernel_ref, f, distance, distance <= 8)
    high = taps.astype(BF16).astype(F32)
    return jnp.where(c >= 2 * reach, taps - high, high).astype(BF16)


def north_times(band, x):
    high, low = split(x)
    return jnp.dot(
        band, jnp.concatenate([high, low, high], axis=0), preferred_element_type=F32
    )


def pack_rims(get, put_right, put_left, groups, b):
    lane = lax.broadcasted_iota(I32, (b, 128), 1)
    first = (lane & 8) == 0

    def one(g, carry):
        even = jnp.zeros((b, 128), F32)
        odd = jnp.zeros((b, 128), F32)
        for q in range(8):
            even = jnp.where(
                (lane >> 4) == q, pltpu.roll(get(16 * g + 2 * q), (16 * q + 8) % 128, 1), even
            )
            odd = jnp.where(
                (((lane + 120) & 127) >> 4) == q,
                pltpu.roll(get(16 * g + 2 * q + 1), (16 * q + 16) % 128, 1),
                odd,
            )
        put_right(g, jnp.where(first, even, odd))
        put_left(g, jnp.where(first, odd, even))
        return carry

    lax.fori_loop(0, groups, one, 0)


def east_filter(get, low_ref, high_ref, put, kernel_ref, f, groups, b):
    band = main_band(kernel_ref, f)
    rim_even = rim_band(kernel_ref, f, 0)
    rim_odd = rim_band(kernel_ref, f, 8)
    lane = lax.broadcasted_iota(I32, (b, 128), 1)
    first = (lane & 8) == 0
    edge = (lane < 8) | (lane >= 120)

    def one(g, carry):
        low = low_ref[f, g]
        high = high_ref[f, g]
        even = times(jnp.where(first, low, high), rim_even)
        odd = times(jnp.where(first, high, low), rim_odd)
        for part in range(2):
            many = jnp.concatenate([get(16 * g + 8 * part + j) for j in range(8)], axis=0)
            flat = times(many, band)
            for j in range(4):
                q = 4 * part + j
                at = 16 * g + 2 * q
                own = flat[2 * j * b : (2 * j + 1) * b]
                put(at, own + jnp.where(edge, pltpu.roll(even, (248 - 16 * q) % 128, 1), 0.0))
                own = flat[(2 * j + 1) * b : (2 * j + 2) * b]
                put(at + 1, own + jnp.where(edge, pltpu.roll(odd, (240 - 16 * q) % 128, 1), 0.0))
        return carry

    lax.fori_loop(0, groups, one, 0)


def mix_levels(parts, pair):
    high, low = split(pair)
    both = jnp.dot(parts, jnp.concatenate([high, low], axis=0), preferred_element_type=F32)
    half = both.shape[0] // 2
    return both[:half] + both[half:]


def fold_rows(x):
    return jnp.sum(x.reshape(-1, 8, 128), axis=0)


def rows_kernel(most, owner, level, row, azimuth, inn, wt, wind, refl, geo, count):
    rows = owner.shape[0]
    tiles = count.shape[0]
    wind[...] = jnp.zeros_like(wind)
    refl[...] = jnp.zeros_like(refl)
    geo[...] = jnp.zeros_like(geo)
    lane = lax.broadcasted_iota(I32, (1, 128), 1)

    def clear(t, carry):
        count[t] = 0
        return carry

    lax.fori_loop(0, tiles, clear, 0)

    def one(i, carry):
        for j in range(8):
            r = i * 8 + j
            o = owner[r]
            rank = count[o]
            count[o] = rank + 1
            label = jnp.where(lane == rank, level[r], geo[o])
            label = jnp.where(lane == rank + most, row[r], label)
            geo[o] = jnp.where(lane == rank + 2 * most, azimuth[r], label)
            at = pl.ds(rank, 1)
            wind[o, 0, at, :] = inn[r, 0:1, :]
            wind[o, 1, at, :] = wt[r, 0:1, :]
            refl[o, 0, at, :] = inn[r, 1:2, :]
            refl[o, 1, at, :] = wt[r, 1:2, :]
        return carry

    lax.fori_loop(0, rows // 8, one, 0)


def pack_rows(owner, level, row, azimuth, inn, wt, tiles, most):
    smem = pl.BlockSpec(memory_space=pltpu.SMEM)
    vmem = pl.BlockSpec(memory_space=pltpu.VMEM)
    w = inn.shape[2]
    block = jax.ShapeDtypeStruct((tiles, 2, most, w), F32)
    return pl.pallas_call(
        functools.partial(rows_kernel, most),
        out_shape=(block, block, jax.ShapeDtypeStruct((tiles, 1, 128), I32)),
        in_specs=[smem] * 4 + [vmem] * 2,
        out_specs=(vmem, vmem, vmem),
        scratch_shapes=[pltpu.SMEM((tiles,), I32)],
        compiler_params=params(),
        name="pack_rows",
    )(owner, level, row, azimuth, inn, wt)


def fused_kernel(
    nx, ny, most,
    control, wind, refl, geo, spread, vert, vert_back, east, north,
    slab, total_out, band_out,
    ext, tbuf, lift, state, right, left, low, high,
    windbuf, reflbuf, geobuf, m0, m1, cb, sb, rhs_wind, rhs_refl, label_v, wave_v, parts,
    cell_s, wave_s,
    fill_sem, rim_sem, edge_sem, row_sem, own_sem, sum_sem, put_sem, label_sem,
):
    fields, a, b, w = control.shape
    tiles = nx * ny
    slots = tiles * most
    reach = b + 16
    pitch = b + 8
    ix = lax.axis_index("gx")
    iy = lax.axis_index("gy")
    me = ix * ny + iy
    up_x, down_x = jnp.minimum(ix + 1, nx - 1), jnp.maximum(ix - 1, 0)
    up_y, down_y = jnp.minimum(iy + 1, ny - 1), jnp.maximum(iy - 1, 0)
    has_up_x, has_down_x = ix < nx - 1, ix > 0
    has_up_y, has_down_y = iy < ny - 1, iy > 0

    def place(t):
        return {"gx": t // ny, "gy": lax.rem(t, ny)}

    def fill(f):
        return pltpu.make_async_copy(
            control.at[f], ext.at[f, :, pl.ds(8, b)], fill_sem.at[f]
        )

    for f in range(fields):
        fill(f).start()

    barrier = pltpu.get_barrier_semaphore()

    def greet(j, carry):
        pl.semaphore_signal(
            barrier, inc=1, device_id=place(lax.rem(me + j, tiles)), device_id_type=MESH
        )
        return carry

    lax.fori_loop(1, tiles, greet, 0)
    pl.semaphore_wait(barrier, tiles - 1)

    def remote(src, dst, sems, sweep, which, f, axis, target):
        return pltpu.make_async_remote_copy(
            src_ref=src,
            dst_ref=dst,
            send_sem=sems.at[0, sweep, which, f],
            recv_sem=sems.at[1, sweep, which, f],
            device_id={axis: target},
            device_id_type=MESH,
        )

    def rim_up(f, sweep):
        return remote(right.at[sweep, f], low.at[sweep, f], rim_sem, sweep, 0, f, "gx", up_x)

    def rim_down(f, sweep):
        return remote(left.at[sweep, f], high.at[sweep, f], rim_sem, sweep, 1, f, "gx", down_x)

    def edge_up(f, sweep):
        if sweep == 0:
            src, dst = control.at[f, :, pl.ds(b - 8, 8)], ext.at[f, :, pl.ds(0, 8)]
        else:
            src, dst = tbuf.at[f, :, pl.ds(b - 8, 8)], slab.at[f, :, pl.ds(0, 8)]
        return remote(src, dst, edge_sem, sweep, 0, f, "gy", up_y)

    def edge_down(f, sweep):
        if sweep == 0:
            src, dst = control.at[f, :, pl.ds(0, 8)], ext.at[f, :, pl.ds(b + 8, 8)]
        else:
            src, dst = tbuf.at[f, :, pl.ds(0, 8)], slab.at[f, :, pl.ds(b + 8, 8)]
        return remote(src, dst, edge_sem, sweep, 1, f, "gy", down_y)

    def start_edges(f, sweep):
        @pl.when(has_up_y)
        def _():
            edge_up(f, sweep).start()

        @pl.when(has_down_y)
        def _():
            edge_down(f, sweep).start()

    def wait_edges(f, sweep):
        @pl.when(has_down_y)
        def _():
            edge_up(f, sweep).wait_recv()

        @pl.when(has_up_y)
        def _():
            edge_down(f, sweep).wait_recv()

    def start_rims(f, sweep):
        @pl.when(has_up_x)
        def _():
            rim_up(f, sweep).start()

        @pl.when(has_down_x)
        def _():
            rim_down(f, sweep).start()

    def wait_rims(f, sweep):
        @pl.when(has_down_x)
        def _():
            rim_up(f, sweep).wait_recv()

        @pl.when(has_up_x)
        def _():
            rim_down(f, sweep).wait_recv()

    kinds = (wind, refl, geo)

    def landing(kind, t):
        if kind == 2:
            return geobuf.at[t]
        buf = windbuf if kind == 0 else reflbuf
        return buf.at[:, pl.ds(pl.multiple_of(t * most, most), most)]

    def row_copy(kind, j):
        t = lax.rem(me + j, tiles)
        return pltpu.make_async_remote_copy(
            src_ref=kinds[kind].at[t],
            dst_ref=landing(kind, me),
            send_sem=row_sem.at[0, kind, j],
            recv_sem=row_sem.at[1, kind, j],
            device_id=place(t),
            device_id_type=MESH,
        )

    def row_arrival(kind, j):
        t = lax.rem(me + tiles - j, tiles)
        return pltpu.make_async_remote_copy(
            src_ref=kinds[kind].at[t],
            dst_ref=landing(kind, t),
            send_sem=row_sem.at[0, kind, j],
            recv_sem=row_sem.at[1, kind, j],
            device_id=place(t),
            device_id_type=MESH,
        )

    def own_rows(kind):
        return pltpu.make_async_copy(kinds[kind].at[me], landing(kind, me), own_sem.at[kind])

    def start_rows(kind):
        def one(j, carry):
            row_copy(kind, j).start()
            return carry

        lax.fori_loop(1, tiles, one, 0)
        own_rows(kind).start()

    def wait_rows(kind):
        def one(j, carry):
            row_arrival(kind, j).wait_recv()
            return carry

        lax.fori_loop(1, tiles, one, 0)
        own_rows(kind).wait()

    for f in range(fields):
        start_edges(f, 0)
    start_rows(2)
    start_rows(0)

    @pl.when(jnp.logical_not(has_down_x))
    def _():
        low[...] = jnp.zeros_like(low)

    @pl.when(jnp.logical_not(has_up_x))
    def _():
        high[...] = jnp.zeros_like(high)

    @pl.when(jnp.logical_not(has_down_y))
    def _():
        ext[:, :, 0:8] = jnp.zeros((fields, a, 8, w), F32)

    @pl.when(jnp.logical_not(has_up_y))
    def _():
        ext[:, :, b + 8 :] = jnp.zeros((fields, a, 8, w), F32)

    for f in range(fields):
        band_out[f] = north_band(north, f, b)

    total_square = jnp.zeros((8, w), F32)
    for f in range(fields):
        fill(f).wait()

        def square(i, total):
            v = ext[f, i, pl.ds(8, b), :]
            return total + fold_rows(v * v)

        total_square = lax.fori_loop(0, a, square, total_square)
    parts[0, ix, 0] = total_square

    def forward_north(f, carry):
        wait_edges(f, 0)
        band = band_out[f]

        def one(i, c):
            for j in range(2):
                p = 4 * i + 2 * j
                r = north_times(band, jnp.concatenate([ext[f, p], ext[f, p + 1]], axis=1))
                tbuf[f, p] = r[:, :w]
                tbuf[f, p + 1] = r[:, w:]
            return c

        lax.fori_loop(0, a // 4, one, 0)

        def put_right(g, v):
            right[0, f, g] = v

        def put_left(g, v):
            left[0, f, g] = v

        pack_rims(lambda s: tbuf[f, s], put_right, put_left, a // 16, b)
        start_rims(f, 0)
        return carry

    lax.fori_loop(0, fields, forward_north, 0)

    def forward_east(f, carry):
        wait_rims(f, 0)

        def put(s, v):
            lift[f, pl.ds(pl.multiple_of(s * pitch, 8), b), :] = v

        east_filter(
            lambda s: tbuf[f, s], low.at[0], high.at[0], put, east, f, a // 16, b
        )
        v = vert[f]

        def one(p, c):
            for j in range(4):
                y = p * 8 + 2 * j
                x = jnp.concatenate(
                    [lift[f, pl.ds(y, a, stride=pitch), :], lift[f, pl.ds(y + 1, a, stride=pitch), :]],
                    axis=1,
                )
                r = mix_levels(v, x)
                at = pl.multiple_of(y * a, 8)
                state[f, pl.ds(at, a), :] = r[:, :w] * spread[f, pl.ds(y, 1), :]
                at = pl.multiple_of(y * a + a, 8)
                state[f, pl.ds(at, a), :] = r[:, w:] * spread[f, pl.ds(y + 1, 1), :]
            return c

        lax.fori_loop(0, b // 8, one, 0)
        return carry

    lax.fori_loop(0, fields, forward_east, 0)

    wait_rows(2)
    per = 128 // most
    lane = lax.broadcasted_iota(I32, (8, 128), 1)

    def label(part):
        total = jnp.zeros((8, 128), I32)
        for q in range(per):
            piece = geobuf[pl.ds(q, 8, stride=per), 0, :]
            shift = ((q - part) * most) % 128
            piece = pltpu.roll(piece, shift, 1) if shift else piece
            total = jnp.where((lane >= q * most) & (lane < (q + 1) * most), piece, total)
        return total

    cell = label(1) * a + label(0)
    angle = label(2).astype(F32) * (2.0 * math.pi / 360.0)
    label_v[...] = cell
    wave_v[0] = jnp.cos(angle)
    wave_v[1] = jnp.sin(angle)
    to_cells = pltpu.make_async_copy(label_v, cell_s, label_sem.at[0])
    to_waves = pltpu.make_async_copy(wave_v, wave_s, label_sem.at[1])
    to_cells.start()
    to_waves.start()
    to_cells.wait()
    to_waves.wait()

    def pick(i, carry):
        for j in range(8):
            r = i * 8 + j
            high_part, low_part = r // 128, lax.rem(r, 128)
            at = cell_s[high_part, low_part]
            c = wave_s[0, high_part, low_part]
            s = wave_s[1, high_part, low_part]
            m0[pl.ds(r, 1), :] = c * state[0, pl.ds(at, 1), :] + s * state[1, pl.ds(at, 1), :]
            m1[pl.ds(r, 1), :] = state[2, pl.ds(at, 1), :]
            cb[pl.ds(r, 1), :] = jnp.full((1, w), c, F32)
            sb[pl.ds(r, 1), :] = jnp.full((1, w), s, F32)
        return carry

    lax.fori_loop(0, slots // 8, pick, 0)
    start_rows(1)
    wait_rows(0)

    def weigh_wind(i, total):
        at = pl.ds(pl.multiple_of(i * 16, 16), 16)
        d = m0[at, :] - windbuf[0, at, :]
        v = windbuf[1, at, :] * d
        for j, wave in enumerate((cb, sb)):
            one, two = split(v * wave[at, :])
            rhs_wind[at, 2 * j * w : (2 * j + 1) * w] = one
            rhs_wind[at, (2 * j + 1) * w : (2 * j + 2) * w] = two
        return total + fold_rows(v * d)

    def weigh_refl(i, total):
        at = pl.ds(pl.multiple_of(i * 16, 16), 16)
        d = m1[at, :] - reflbuf[0, at, :]
        v = reflbuf[1, at, :] * d
        one, two = split(v)
        rhs_refl[at, 0:w] = one
        rhs_refl[at, w : 2 * w] = two
        return total + fold_rows(v * d)

    def lower(rhs, which):
        chunk = 4 * a

        def one(i, carry):
            index = lax.broadcasted_iota(I32, (chunk, 128), 0) + i * chunk
            ones = jnp.concatenate(
                [
                    jnp.where(index == label_v[pl.ds(g, 1), :], 1.0, 0.0).astype(BF16)
                    for g in range(slots // 128)
                ],
                axis=1,
            )
            r = jnp.dot(ones, rhs[...], preferred_element_type=F32)
            for k, f in enumerate(which):
                grown = r[:, 2 * k * w : (2 * k + 1) * w] + r[:, (2 * k + 1) * w : (2 * k + 2) * w]
                v = vert_back[f]
                for j in range(2):
                    y = i * 4 + 2 * j
                    x = jnp.concatenate(
                        [grown[2 * j * a : (2 * j + 1) * a], grown[(2 * j + 1) * a : (2 * j + 2) * a]],
                        axis=1,
                    )
                    t = mix_levels(v, x)
                    lift[f, pl.ds(y, a, stride=pitch), :] = t[:, :w] * spread[f, pl.ds(y, 1), :]
                    lift[f, pl.ds(y + 1, a, stride=pitch), :] = (
                        t[:, w:] * spread[f, pl.ds(y + 1, 1), :]
                    )
            return carry

        lax.fori_loop(0, b // 4, one, 0)

    def back_rims(f):
        def put_right(g, v):
            right[1, f, g] = v

        def put_left(g, v):
            left[1, f, g] = v

        def get(s):
            return lift[f, pl.ds(pl.multiple_of(s * pitch, 8), b), :]

        pack_rims(get, put_right, put_left, a // 16, b)
        start_rims(f, 1)

    def to_slab(f):
        return pltpu.make_async_copy(
            tbuf.at[f], slab.at[f, :, pl.ds(8, b)], put_sem.at[0, f]
        )

    def blank(f, side):
        at = 0 if side == 0 else b + 8
        return pltpu.make_async_copy(
            ext.at[f, :, pl.ds(at, 8)], slab.at[f, :, pl.ds(at, 8)], put_sem.at[1 + side, f]
        )

    def back_east(f):
        wait_rims(f, 1)

        def get(s):
            return lift[f, pl.ds(pl.multiple_of(s * pitch, 8), b), :]

        def put(s, v):
            tbuf[f, s] = v

        east_filter(get, low.at[1], high.at[1], put, east, f, a // 16, b)
        start_edges(f, 1)
        to_slab(f).start()

        @pl.when(jnp.logical_not(has_down_y))
        def _():
            blank(f, 0).start()

        @pl.when(jnp.logical_not(has_up_y))
        def _():
            blank(f, 1).start()

    observed = lax.fori_loop(0, slots // 16, weigh_wind, jnp.zeros((8, w), F32))
    lower(rhs_wind, (0, 1))
    back_rims(0)
    back_rims(1)
    back_east(0)
    back_east(1)
    wait_rows(1)
    observed = lax.fori_loop(0, slots // 16, weigh_refl, observed)
    parts[0, ix, 1] = observed

    def share(axis, slot, peer, row):
        return pltpu.make_async_remote_copy(
            src_ref=parts.at[row, slot],
            dst_ref=parts.at[row, slot],
            send_sem=sum_sem.at[0, row, peer],
            recv_sem=sum_sem.at[1, row, slot],
            device_id={axis: peer},
            device_id_type=MESH,
        )

    def arrival(axis, peer, row):
        return pltpu.make_async_remote_copy(
            src_ref=parts.at[row, peer],
            dst_ref=parts.at[row, peer],
            send_sem=sum_sem.at[0, row, peer],
            recv_sem=sum_sem.at[1, row, peer],
            device_id={axis: peer},
            device_id_type=MESH,
        )

    for j in range(1, nx):
        share("gx", ix, lax.rem(ix + j, nx), 0).start()
    lower(rhs_refl, (2,))
    back_rims(2)
    for j in range(1, nx):
        arrival("gx", lax.rem(ix + j, nx), 0).wait_recv()
    row_sum = parts[0, 0]
    for j in range(1, nx):
        row_sum = row_sum + parts[0, j]
    parts[1, iy] = row_sum
    for j in range(1, ny):
        share("gy", iy, lax.rem(iy + j, ny), 1).start()
    back_east(2)
    for j in range(1, ny):
        arrival("gy", lax.rem(iy + j, ny), 1).wait_recv()
    all_sum = parts[1, 0]
    for j in range(1, ny):
        all_sum = all_sum + parts[1, j]
    total_out[...] = all_sum

    for f in range(fields):
        wait_edges(f, 1)
        to_slab(f).wait()

        @pl.when(jnp.logical_not(has_down_y))
        def _():
            blank(f, 0).wait()

        @pl.when(jnp.logical_not(has_up_y))
        def _():
            blank(f, 1).wait()

    for j in range(1, nx):
        share("gx", ix, lax.rem(ix + j, nx), 0).wait_send()
    for j in range(1, ny):
        share("gy", iy, lax.rem(iy + j, ny), 1).wait_send()

    for kind in range(3):

        def sent(j, carry):
            row_copy(kind, j).wait_send()
            return carry

        lax.fori_loop(1, tiles, sent, 0)

    for sweep in range(2):
        for f in range(fields):

            @pl.when(has_up_x)
            def _():
                rim_up(f, sweep).wait_send()

            @pl.when(has_down_x)
            def _():
                rim_down(f, sweep).wait_send()

            @pl.when(has_up_y)
            def _():
                edge_up(f, sweep).wait_send()

            @pl.when(has_down_y)
            def _():
                edge_down(f, sweep).wait_send()


def fused(control, wind, refl, geo, spread, vert, vert_back, east, north, most):
    f, a, b, w = control.shape
    nx, ny = lax.axis_size("gx"), lax.axis_size("gy")
    tiles = nx * ny
    slots = tiles * most
    smem = pl.BlockSpec(memory_space=pltpu.SMEM)
    vmem = pl.BlockSpec(memory_space=pltpu.VMEM)
    anywhere = pl.BlockSpec(memory_space=pl.ANY)
    rim = pltpu.VMEM((2, f, a // 16, b, w), F32)
    gates = pltpu.VMEM((slots, w), F32)
    dma = pltpu.SemaphoreType.DMA
    return pl.pallas_call(
        functools.partial(fused_kernel, nx, ny, most),
        in_specs=[anywhere] * 4 + [vmem] * 3 + [smem] * 2,
        out_specs=(anywhere, vmem, vmem),
        out_shape=(
            jax.ShapeDtypeStruct((f, a, b + 16, w), F32),
            jax.ShapeDtypeStruct((2, 8, w), F32),
            jax.ShapeDtypeStruct((f, b, 3 * (b + 16)), BF16),
        ),
        scratch_shapes=[
            pltpu.VMEM((f, a, b + 16, w), F32),
            pltpu.VMEM((f, a, b, w), F32),
            pltpu.VMEM((f, a * (b + 8), w), F32),
            pltpu.VMEM((f, a * b, w), F32),
            rim,
            rim,
            rim,
            rim,
            pltpu.VMEM((2, slots, w), F32),
            pltpu.VMEM((2, slots, w), F32),
            pltpu.VMEM((tiles, 1, 128), I32),
            gates,
            gates,
            gates,
            gates,
            pltpu.VMEM((slots, 4 * w), BF16),
            pltpu.VMEM((slots, 2 * w), BF16),
            pltpu.VMEM((8, 128), I32),
            pltpu.VMEM((2, 8, 128), F32),
            pltpu.VMEM((2, max(nx, ny), 2, 8, w), F32),
            pltpu.SMEM((8, 128), I32),
            pltpu.SMEM((2, 8, 128), F32),
            dma((f,)),
            dma((2, 2, 2, f)),
            dma((2, 2, 2, f)),
            dma((2, 3, tiles)),
            dma((3,)),
            dma((2, 2, max(nx, ny))),
            dma((3, f)),
            dma((2,)),
        ],
        compiler_params=pltpu.CompilerParams(
            vmem_limit_bytes=VMEM_BYTES, collective_id=0, has_side_effects=True
        ),
        name="fused",
    )(control, wind, refl, geo, spread, vert, vert_back, east, north)


def final_kernel(x_ref, c_ref, band, out):
    zs = x_ref.shape[1]
    w = x_ref.shape[3]
    for j in range(zs // 2):
        x = jnp.concatenate([x_ref[0, 2 * j], x_ref[0, 2 * j + 1]], axis=1)
        r = north_times(band[0], x)
        out[0, 2 * j] = c_ref[0, 2 * j] + r[:, :w]
        out[0, 2 * j + 1] = c_ref[0, 2 * j + 1] + r[:, w:]


def final(slab, control, band):
    f, a, b, w = control.shape
    zs = 16
    tile = pl.BlockSpec((1, zs, b, w), lambda i, j: (i, j, 0, 0))
    return pl.pallas_call(
        final_kernel,
        grid=(f, a // zs),
        in_specs=[
            pl.BlockSpec((1, zs, b + 16, w), lambda i, j: (i, j, 0, 0)),
            tile,
            pl.BlockSpec((1,) + band.shape[1:], lambda i, j: (i, 0, 0)),
        ],
        out_specs=tile,
        out_shape=jax.ShapeDtypeStruct(control.shape, F32),
        compiler_params=params(),
        name="final",
    )(slab, control, band)


def vertical_parts(v):
    high = lax.reduce_precision(v, 8, 7)
    low = lax.reduce_precision(v - high, 8, 7)
    both = jnp.concatenate([high, low], axis=1)
    return jnp.concatenate([both, both], axis=2).astype(BF16)


def body(
    control, spread, kernel_east, kernel_north, vertical,
    tile_owner, gate_level, tile_row, beam_azimuth, innovation, obs_weight,
):
    tiles = lax.axis_size("gx") * lax.axis_size("gy")
    most = 2 * tile_owner.shape[0] // tiles
    wind, refl, geo = pack_rows(
        tile_owner, gate_level, tile_row, beam_azimuth, innovation, obs_weight, tiles, most
    )
    vert = vertical_parts(vertical)
    vert_back = vertical_parts(jnp.swapaxes(vertical, 1, 2))
    slab, totals, band = fused(
        control, wind, refl, geo, spread, vert, vert_back, kernel_east, kernel_north, most
    )
    counts = jnp.array([control.size * tiles, innovation.size * tiles], F32)
    cost = 0.5 * jnp.sum(totals, axis=(1, 2)) / counts
    return final(slab, control, band), cost


def solution(mesh):
    both = ("gx", "gy")
    placed = (
        P(None, None, "gy", "gx"),
        P(None, "gy", "gx"),
        P(),
        P(),
        P(),
        P(both),
        P(both),
        P(both),
        P(both),
        P(both, None, None),
        P(both, None, None),
    )
    return jax.shard_map(
        body,
        mesh=mesh,
        in_specs=placed,
        out_specs=(P(None, None, "gy", "gx"), P()),
        check_vma=False,
    )
```

```python
import functools
import math

import jax
import jax.numpy as jnp
from jax import lax
from jax.experimental import pallas as pl
from jax.experimental.pallas import tpu as pltpu
from jax.sharding import PartitionSpec as P

F32 = jnp.float32
BF16 = jnp.bfloat16
I32 = jnp.int32
VMEM_BYTES = 58 * 1024 * 1024
MESH = pl.DeviceIdType.MESH


def split(value):
    high = value.astype(BF16)
    low = (value - high.astype(F32)).astype(BF16)
    return high, low


def doubled(weights):
    high, low = split(weights)
    row = jnp.concatenate([high, low], axis=1)
    return jnp.concatenate([row, row], axis=0)


def times(rows, weights):
    high, low = split(rows)
    both = jnp.dot(
        jnp.concatenate([high, low], axis=1), weights, preferred_element_type=F32
    )
    half = both.shape[1] // 2
    return both[:, :half] + both[:, half:]


def taps_at(kernel_ref, f, distance, allowed):
    total = jnp.zeros(distance.shape, F32)
    for d in range(kernel_ref.shape[1]):
        total = jnp.where(distance == d, kernel_ref[f, d], total)
    return jnp.where(allowed, total, 0.0)


def main_band(kernel_ref, f):
    r = lax.broadcasted_iota(I32, (128, 128), 0)
    c = lax.broadcasted_iota(I32, (128, 128), 1)
    return doubled(taps_at(kernel_ref, f, jnp.abs(r - c), jnp.abs(r - c) <= 8))


def rim_band(kernel_ref, f, offset):
    r = (lax.broadcasted_iota(I32, (128, 128), 0) + (128 - offset)) & 127
    c = (lax.broadcasted_iota(I32, (128, 128), 1) + (128 - offset)) & 127
    distance = jnp.abs(r - c)
    fits = ((r >> 4) == (c >> 4)) & ((r & 8) != (c & 8)) & (distance <= 8)
    return doubled(taps_at(kernel_ref, f, distance, fits))


def north_band(kernel_ref, f, ys, rim):
    reach = ys + 2 * rim
    r = lax.broadcasted_iota(I32, (ys, 3 * reach), 0)
    c = lax.broadcasted_iota(I32, (ys, 3 * reach), 1)
    j = jnp.where(c >= reach, c - reach, c)
    j = jnp.where(c >= 2 * reach, c - 2 * reach, j)
    distance = jnp.abs(r + rim - j)
    taps = taps_at(kernel_ref, f, distance, distance <= 8)
    high = taps.astype(BF16).astype(F32)
    return jnp.where(c >= 2 * reach, taps - high, high).astype(BF16)


def north_times(band, x):
    high, low = split(x)
    return jnp.dot(
        band, jnp.concatenate([high, low, high], axis=0), preferred_element_type=F32
    )


def pack_rims(get, put_right, put_left, groups, b):
    lane = lax.broadcasted_iota(I32, (b, 128), 1)
    first = (lane & 8) == 0

    def one(g, carry):
        even = jnp.zeros((b, 128), F32)
        odd = jnp.zeros((b, 128), F32)
        for q in range(8):
            even = jnp.where(
                (lane >> 4) == q, pltpu.roll(get(16 * g + 2 * q), (16 * q + 8) % 128, 1), even
            )
            odd = jnp.where(
                (((lane + 120) & 127) >> 4) == q,
                pltpu.roll(get(16 * g + 2 * q + 1), (16 * q + 16) % 128, 1),
                odd,
            )
        put_right(g, jnp.where(first, even, odd))
        put_left(g, jnp.where(first, odd, even))
        return carry

    lax.fori_loop(0, groups, one, 0)


def east_filter(get, low_ref, high_ref, put, kernel_ref, f, groups, b):
    band = main_band(kernel_ref, f)
    rim_even = rim_band(kernel_ref, f, 0)
    rim_odd = rim_band(kernel_ref, f, 8)
    lane = lax.broadcasted_iota(I32, (b, 128), 1)
    first = (lane & 8) == 0
    edge = (lane < 8) | (lane >= 120)

    def one(g, carry):
        low = low_ref[f, g]
        high = high_ref[f, g]
        even = times(jnp.where(first, low, high), rim_even)
        odd = times(jnp.where(first, high, low), rim_odd)
        for part in range(2):
            many = jnp.concatenate([get(16 * g + 8 * part + j) for j in range(8)], axis=0)
            flat = times(many, band)
            for j in range(4):
                q = 4 * part + j
                at = 16 * g + 2 * q
                own = flat[2 * j * b : (2 * j + 1) * b]
                put(at, own + jnp.where(edge, pltpu.roll(even, (248 - 16 * q) % 128, 1), 0.0))
                own = flat[(2 * j + 1) * b : (2 * j + 2) * b]
                put(at + 1, own + jnp.where(edge, pltpu.roll(odd, (240 - 16 * q) % 128, 1), 0.0))
        return carry

    lax.fori_loop(0, groups, one, 0)


def mix_levels(parts, pair):
    high, low = split(pair)
    both = jnp.dot(parts, jnp.concatenate([high, low], axis=0), preferred_element_type=F32)
    half = both.shape[0] // 2
    return both[:half] + both[half:]


def fold_rows(x):
    return jnp.sum(x.reshape(-1, 8, 128), axis=0)


def ones_at(index, labels, groups):
    return jnp.concatenate(
        [
            jnp.where(index == labels[pl.ds(g, 1), :], 1.0, 0.0).astype(BF16)
            for g in range(groups)
        ],
        axis=1,
    )


def level_parts(v):
    high = v.astype(BF16).astype(F32)
    both = jnp.concatenate([high, v - high], axis=0)
    return jnp.concatenate([both, both], axis=1).astype(BF16)


def fused_kernel(
    nx, ny, most,
    control, inn, wt, owner_in, level_in, row_in, azimuth_in, spread_in, vertical_in, east, north,
    near, halo, total_out,
    lanes_v, spread, vertical, total_v, ext, tbuf, lift, state, right, left, low, high,
    windbuf, reflbuf, geobuf, wind, refl, geo, rows_v, rows_rhs, slot_v, band_s, inner_s,
    vert, vert_back,
    m, waves, rhs_wind, rhs_refl, label_v, parts,
    cell_s,
    fill_sem, rim_sem, edge_sem, row_sem, own_sem, sum_sem, load_sem, label_sem, put_sem,
):
    fields, a, b, w = control.shape
    tiles = nx * ny
    slots = tiles * most
    rows = inn.shape[0]
    groups = rows // 128
    pitch = b + 8
    ix = lax.axis_index("gx")
    iy = lax.axis_index("gy")
    me = ix * ny + iy
    up_x, down_x = jnp.minimum(ix + 1, nx - 1), jnp.maximum(ix - 1, 0)
    up_y, down_y = jnp.minimum(iy + 1, ny - 1), jnp.maximum(iy - 1, 0)
    has_up_x, has_down_x = ix < nx - 1, ix > 0
    has_up_y, has_down_y = iy < ny - 1, iy > 0

    def place(t):
        return {"gx": t // ny, "gy": lax.rem(t, ny)}

    def fill(f):
        return pltpu.make_async_copy(
            control.at[f], ext.at[f, :, pl.ds(8, b)], fill_sem.at[f]
        )

    def load(k):
        src = (inn, wt)[k % 2]
        return pltpu.make_async_copy(src.at[:, k // 2], rows_v.at[k], load_sem.at[k])

    small = (
        (owner_in, lanes_v.at[0]),
        (level_in, lanes_v.at[1]),
        (row_in, lanes_v.at[2]),
        (azimuth_in, lanes_v.at[3]),
        (spread_in, spread),
        (vertical_in, vertical),
    )

    def fetch(k):
        return pltpu.make_async_copy(small[k][0], small[k][1], load_sem.at[4 + k])

    for k in range(len(small)):
        fetch(k).start()
    for k in range(4):
        load(k).start()
    for f in range(fields):
        fill(f).start()
    owner, level, row, azimuth = (lanes_v.at[k] for k in range(4))

    barrier = pltpu.get_barrier_semaphore()

    def greet(j, carry):
        pl.semaphore_signal(
            barrier, inc=1, device_id=place(lax.rem(me + j, tiles)), device_id_type=MESH
        )
        return carry

    lax.fori_loop(1, tiles, greet, 0)

    pl.semaphore_wait(barrier, tiles - 1)

    def remote(src, dst, sems, sweep, which, f, axis, target):
        return pltpu.make_async_remote_copy(
            src_ref=src,
            dst_ref=dst,
            send_sem=sems.at[0, sweep, which, f],
            recv_sem=sems.at[1, sweep, which, f],
            device_id={axis: target},
            device_id_type=MESH,
        )

    def rim_up(f, sweep):
        return remote(right.at[sweep, f], low.at[sweep, f], rim_sem, sweep, 0, f, "gx", up_x)

    def rim_down(f, sweep):
        return remote(left.at[sweep, f], high.at[sweep, f], rim_sem, sweep, 1, f, "gx", down_x)

    def edge_up(f, sweep):
        if sweep == 0:
            src, dst = control.at[f, :, pl.ds(b - 8, 8)], ext.at[f, :, pl.ds(0, 8)]
        else:
            src, dst = tbuf.at[f, :, pl.ds(b - 8, 8)], halo.at[f, :, pl.ds(0, 8)]
        return remote(src, dst, edge_sem, sweep, 0, f, "gy", up_y)

    def edge_down(f, sweep):
        if sweep == 0:
            src, dst = control.at[f, :, pl.ds(0, 8)], ext.at[f, :, pl.ds(b + 8, 8)]
        else:
            src, dst = tbuf.at[f, :, pl.ds(0, 8)], halo.at[f, :, pl.ds(8, 8)]
        return remote(src, dst, edge_sem, sweep, 1, f, "gy", down_y)

    def start_edges(f, sweep):
        @pl.when(has_up_y)
        def _():
            edge_up(f, sweep).start()

        @pl.when(has_down_y)
        def _():
            edge_down(f, sweep).start()

    def wait_edges(f, sweep):
        @pl.when(has_down_y)
        def _():
            edge_up(f, sweep).wait_recv()

        @pl.when(has_up_y)
        def _():
            edge_down(f, sweep).wait_recv()

    def start_rims(f, sweep):
        @pl.when(has_up_x)
        def _():
            rim_up(f, sweep).start()

        @pl.when(has_down_x)
        def _():
            rim_down(f, sweep).start()

    def wait_rims(f, sweep):
        @pl.when(has_down_x)
        def _():
            rim_up(f, sweep).wait_recv()

        @pl.when(has_up_x)
        def _():
            rim_down(f, sweep).wait_recv()

    kinds = (wind, refl, geo)

    def block(ref, kind, t):
        if kind == 2:
            return ref.at[pl.ds(t, 1)]
        return ref.at[:, pl.ds(pl.multiple_of(t * most, most), most)]

    def landing(kind, t):
        return block((windbuf, reflbuf, geobuf)[kind], kind, t)

    def row_copy(kind, j):
        t = lax.rem(me + j, tiles)
        return pltpu.make_async_remote_copy(
            src_ref=block(kinds[kind], kind, t),
            dst_ref=landing(kind, me),
            send_sem=row_sem.at[0, kind, j],
            recv_sem=row_sem.at[1, kind, j],
            device_id=place(t),
            device_id_type=MESH,
        )

    def row_arrival(kind, j):
        t = lax.rem(me + tiles - j, tiles)
        return pltpu.make_async_remote_copy(
            src_ref=block(kinds[kind], kind, t),
            dst_ref=landing(kind, t),
            send_sem=row_sem.at[0, kind, j],
            recv_sem=row_sem.at[1, kind, j],
            device_id=place(t),
            device_id_type=MESH,
        )

    def own_rows(kind):
        return pltpu.make_async_copy(
            block(kinds[kind], kind, me), landing(kind, me), own_sem.at[kind]
        )

    def start_rows(kind):
        def one(j, carry):
            row_copy(kind, j).start()
            return carry

        lax.fori_loop(1, tiles, one, 0)
        own_rows(kind).start()

    def wait_rows(kind):
        def one(j, carry):
            row_arrival(kind, j).wait_recv()
            return carry

        lax.fori_loop(1, tiles, one, 0)
        own_rows(kind).wait()

    for f in range(fields):
        start_edges(f, 0)

    for k in range(len(small)):
        fetch(k).wait()

    tile_index = lax.broadcasted_iota(I32, (tiles, 128), 0)
    member = ones_at(tile_index, owner, groups)
    before = jnp.concatenate(
        [
            jnp.where(
                lax.broadcasted_iota(I32, (rows, 128), 0)
                < lax.broadcasted_iota(I32, (rows, 128), 1) + 128 * g,
                1.0,
                0.0,
            ).astype(BF16)
            for g in range(groups)
        ],
        axis=1,
    )
    ahead = jnp.dot(member, before, preferred_element_type=F32)
    ranks = []
    for g in range(groups):
        here = jnp.where(tile_index == owner[pl.ds(g, 1), :], ahead[:, 128 * g : 128 * g + 128], 0.0)
        ranks.append(jnp.sum(here, axis=0, keepdims=True).astype(I32))
        slot_v[pl.ds(g, 1), :] = owner[pl.ds(g, 1), :] * most + ranks[g]
    k_index = lax.broadcasted_iota(I32, (128, 128), 0)
    told = []
    for g in range(groups):
        total = jnp.zeros((128, 128), F32)
        values = (
            level[pl.ds(g, 1), :],
            row[pl.ds(g, 1), :],
            azimuth[pl.ds(g, 1), :] - 180,
        )
        for part, value in enumerate(values):
            total = jnp.where(k_index == ranks[g] + part * most, value.astype(F32), total)
        told.append(total.astype(BF16))
    geo[...] = lax.dot_general(
        member,
        jnp.concatenate(told, axis=1),
        (((1,), (1,)), ((), ())),
        preferred_element_type=F32,
    ).astype(I32)
    start_rows(2)

    def pack(kind):
        target = kinds[kind]
        for k in range(2):
            one, two = split(rows_v[2 * kind + k])
            rows_rhs[kind, :, k * w : (k + 1) * w] = one
            rows_rhs[kind, :, (2 + k) * w : (3 + k) * w] = two

        def one(i, carry):
            index = lax.broadcasted_iota(I32, (256, 128), 0) + i * 256
            r = jnp.dot(
                ones_at(index, slot_v, groups), rows_rhs[kind], preferred_element_type=F32
            )
            at = pl.ds(pl.multiple_of(i * 256, 256), 256)
            target[0, at, :] = r[:, :w] + r[:, 2 * w : 3 * w]
            target[1, at, :] = r[:, w : 2 * w] + r[:, 3 * w :]
            return carry

        lax.fori_loop(0, slots // 256, one, 0)

    for k in range(4):
        load(k).wait()
    pack(0)

    @pl.when(jnp.logical_not(has_down_x))
    def _():
        low[...] = jnp.zeros_like(low)

    @pl.when(jnp.logical_not(has_up_x))
    def _():
        high[...] = jnp.zeros_like(high)

    @pl.when(jnp.logical_not(has_down_y))
    def _():
        ext[:, :, 0:8] = jnp.zeros((fields, a, 8, w), F32)

    @pl.when(jnp.logical_not(has_up_y))
    def _():
        ext[:, :, b + 8 :] = jnp.zeros((fields, a, 8, w), F32)

    for f in range(fields):
        band_s[f] = north_band(north, f, b, 8)
        inner_s[f] = north_band(north, f, b, 0)
        vert[f] = level_parts(vertical[f])
        vert_back[f] = level_parts(vertical[f].T)

    total_square = jnp.zeros((8, w), F32)
    for f in range(fields):
        fill(f).wait()

        def square(i, total):
            v = ext[f, i, pl.ds(8, b), :]
            return total + fold_rows(v * v)

        total_square = lax.fori_loop(0, a, square, total_square)
    parts[0, ix, 0] = total_square

    def forward_north(f, carry):
        wait_edges(f, 0)
        band = band_s[f]

        def one(i, c):
            for j in range(2):
                p = 4 * i + 2 * j
                r = north_times(band, jnp.concatenate([ext[f, p], ext[f, p + 1]], axis=1))
                tbuf[f, p] = r[:, :w]
                tbuf[f, p + 1] = r[:, w:]
            return c

        lax.fori_loop(0, a // 4, one, 0)

        def put_right(g, v):
            right[0, f, g] = v

        def put_left(g, v):
            left[0, f, g] = v

        pack_rims(lambda s: tbuf[f, s], put_right, put_left, a // 16, b)
        start_rims(f, 0)
        return carry

    def forward_east(f, carry):
        wait_rims(f, 0)

        def put(s, v):
            lift[f, pl.ds(pl.multiple_of(s * pitch, 8), b), :] = v

        east_filter(
            lambda s: tbuf[f, s], low.at[0], high.at[0], put, east, f, a // 16, b
        )
        v = vert[f]

        def one(p, c):
            for j in range(4):
                y = p * 8 + 2 * j
                x = jnp.concatenate(
                    [lift[f, pl.ds(y, a, stride=pitch), :], lift[f, pl.ds(y + 1, a, stride=pitch), :]],
                    axis=1,
                )
                r = mix_levels(v, x)
                at = pl.multiple_of(y * a, 8)
                state[f, pl.ds(at, a), :] = r[:, :w] * spread[f, pl.ds(y, 1), :]
                at = pl.multiple_of(y * a + a, 8)
                state[f, pl.ds(at, a), :] = r[:, w:] * spread[f, pl.ds(y + 1, 1), :]
            return c

        lax.fori_loop(0, b // 8, one, 0)
        return carry

    forward_north(0, 0)
    forward_north(1, 0)
    start_rows(0)
    pack(1)
    forward_east(0, 0)
    forward_north(2, 0)
    lax.fori_loop(1, fields, forward_east, 0)
    start_rows(1)

    wait_rows(2)
    per = 128 // most
    lane = lax.broadcasted_iota(I32, (8, 128), 1)

    def label(part):
        total = jnp.zeros((8, 128), I32)
        for q in range(per):
            piece = geobuf[pl.ds(q, 8, stride=per), :]
            shift = ((q - part) * most) % 128
            piece = pltpu.roll(piece, shift, 1) if shift else piece
            total = jnp.where((lane >= q * most) & (lane < (q + 1) * most), piece, total)
        return total

    cell = label(1) * a + label(0)
    angle = (label(2) + 180).astype(F32) * (2.0 * math.pi / 360.0)
    label_v[...] = cell
    to_cells = pltpu.make_async_copy(label_v, cell_s, label_sem.at[0])
    to_cells.start()
    for k, wave in enumerate((jnp.cos(angle), jnp.sin(angle))):
        for g in range(8):
            waves[k, g * 128 : (g + 1) * 128, :] = jnp.broadcast_to(
                wave[g : g + 1], (128, 128)
            ).T
    to_cells.wait()

    def pick(i, carry):
        block_at, first = i // 8, lax.rem(i, 8) * 16
        for j in range(16):
            at = jnp.clip(cell_s[block_at, first + j], 0, a * b - 1)
            for f in range(fields):
                m[f, pl.ds(i * 16 + j, 1), :] = state[f, pl.ds(at, 1), :]
        return carry

    lax.fori_loop(0, slots // 16, pick, 0)
    wait_rows(0)

    def weigh_wind(i, total):
        at = pl.ds(pl.multiple_of(i * 16, 16), 16)
        d = waves[0, at, :] * m[0, at, :] + waves[1, at, :] * m[1, at, :] - windbuf[0, at, :]
        v = windbuf[1, at, :] * d
        for j in range(2):
            one, two = split(v * waves[j, at, :])
            rhs_wind[at, 2 * j * w : (2 * j + 1) * w] = one
            rhs_wind[at, (2 * j + 1) * w : (2 * j + 2) * w] = two
        return total + fold_rows(v * d)

    def weigh_refl(i, total):
        at = pl.ds(pl.multiple_of(i * 16, 16), 16)
        d = m[2, at, :] - reflbuf[0, at, :]
        v = reflbuf[1, at, :] * d
        one, two = split(v)
        rhs_refl[at, 0:w] = one
        rhs_refl[at, w : 2 * w] = two
        return total + fold_rows(v * d)

    def lower(rhs, which):
        many = 8
        chunk = many * a

        def one(i, carry):
            index = lax.broadcasted_iota(I32, (chunk, 128), 0) + i * chunk
            ones = ones_at(index, label_v, slots // 128)
            r = jnp.dot(ones, rhs[...], preferred_element_type=F32)
            for k, f in enumerate(which):
                grown = r[:, 2 * k * w : (2 * k + 1) * w] + r[:, (2 * k + 1) * w : (2 * k + 2) * w]
                v = vert_back[f]
                for j in range(many // 2):
                    y = i * many + 2 * j
                    x = jnp.concatenate(
                        [grown[2 * j * a : (2 * j + 1) * a], grown[(2 * j + 1) * a : (2 * j + 2) * a]],
                        axis=1,
                    )
                    t = mix_levels(v, x)
                    lift[f, pl.ds(y, a, stride=pitch), :] = t[:, :w] * spread[f, pl.ds(y, 1), :]
                    lift[f, pl.ds(y + 1, a, stride=pitch), :] = (
                        t[:, w:] * spread[f, pl.ds(y + 1, 1), :]
                    )
            return carry

        lax.fori_loop(0, b // many, one, 0)

    def back_rims(f):
        def put_right(g, v):
            right[1, f, g] = v

        def put_left(g, v):
            left[1, f, g] = v

        def get(s):
            return lift[f, pl.ds(pl.multiple_of(s * pitch, 8), b), :]

        pack_rims(get, put_right, put_left, a // 16, b)
        start_rims(f, 1)

    def back_east(f):
        wait_rims(f, 1)

        def get(s):
            return lift[f, pl.ds(pl.multiple_of(s * pitch, 8), b), :]

        def put(s, v):
            tbuf[f, s] = v

        east_filter(get, low.at[1], high.at[1], put, east, f, a // 16, b)
        start_edges(f, 1)

    def keep(f):
        return pltpu.make_async_copy(ext.at[f, :, pl.ds(8, b)], near.at[f], put_sem.at[0, f])

    def blank(f, side):
        return pltpu.make_async_copy(
            ext.at[f, :, pl.ds(side * (b + 8), 8)],
            halo.at[f, :, pl.ds(8 * side, 8)],
            put_sem.at[1 + side, f],
        )

    def blanks(act):
        for side, there in ((0, has_down_y), (1, has_up_y)):

            @pl.when(jnp.logical_not(there))
            def _():
                for f in range(fields):
                    act(blank(f, side))

    def back_inner(f, carry):
        band = inner_s[f]

        def one(i, c):
            for j in range(2):
                p = 4 * i + 2 * j
                r = north_times(band, jnp.concatenate([tbuf[f, p], tbuf[f, p + 1]], axis=1))
                at = pl.ds(8, b)
                ext[f, p, at, :] = ext[f, p, at, :] + r[:, :w]
                ext[f, p + 1, at, :] = ext[f, p + 1, at, :] + r[:, w:]
            return c

        lax.fori_loop(0, a // 4, one, 0)
        keep(f).start()
        return carry

    blanks(lambda copy: copy.start())
    observed = lax.fori_loop(0, slots // 16, weigh_wind, jnp.zeros((8, w), F32))
    lower(rhs_wind, (0, 1))
    back_rims(0)
    back_rims(1)
    back_east(0)
    back_east(1)
    wait_rows(1)
    observed = lax.fori_loop(0, slots // 16, weigh_refl, observed)
    parts[0, ix, 1] = observed

    def share(axis, slot, peer, row):
        return pltpu.make_async_remote_copy(
            src_ref=parts.at[row, slot],
            dst_ref=parts.at[row, slot],
            send_sem=sum_sem.at[0, row, peer],
            recv_sem=sum_sem.at[1, row, slot],
            device_id={axis: peer},
            device_id_type=MESH,
        )

    def arrival(axis, peer, row):
        return pltpu.make_async_remote_copy(
            src_ref=parts.at[row, peer],
            dst_ref=parts.at[row, peer],
            send_sem=sum_sem.at[0, row, peer],
            recv_sem=sum_sem.at[1, row, peer],
            device_id={axis: peer},
            device_id_type=MESH,
        )

    for j in range(1, nx):
        share("gx", ix, lax.rem(ix + j, nx), 0).start()
    lower(rhs_refl, (2,))
    back_rims(2)
    back_inner(0, 0)
    for j in range(1, nx):
        arrival("gx", lax.rem(ix + j, nx), 0).wait_recv()
    row_sum = parts[0, 0]
    for j in range(1, nx):
        row_sum = row_sum + parts[0, j]
    parts[1, iy] = row_sum
    for j in range(1, ny):
        share("gy", iy, lax.rem(iy + j, ny), 1).start()
    back_east(2)
    for j in range(1, ny):
        arrival("gy", lax.rem(iy + j, ny), 1).wait_recv()
    all_sum = parts[1, 0]
    for j in range(1, ny):
        all_sum = all_sum + parts[1, j]
    total_v[...] = all_sum
    totals = pltpu.make_async_copy(total_v, total_out, label_sem.at[1])
    totals.start()
    lax.fori_loop(1, fields, back_inner, 0)
    for f in range(fields):
        wait_edges(f, 1)
        keep(f).wait()
    blanks(lambda copy: copy.wait())
    totals.wait()

    for j in range(1, nx):
        share("gx", ix, lax.rem(ix + j, nx), 0).wait_send()
    for j in range(1, ny):
        share("gy", iy, lax.rem(iy + j, ny), 1).wait_send()

    for kind in range(3):

        def sent(j, carry):
            row_copy(kind, j).wait_send()
            return carry

        lax.fori_loop(1, tiles, sent, 0)

    for sweep in range(2):
        for f in range(fields):

            @pl.when(has_up_x)
            def _():
                rim_up(f, sweep).wait_send()

            @pl.when(has_down_x)
            def _():
                rim_down(f, sweep).wait_send()

            @pl.when(has_up_y)
            def _():
                edge_up(f, sweep).wait_send()

            @pl.when(has_down_y)
            def _():
                edge_down(f, sweep).wait_send()


def fused(
    control, inn, wt, owner, level, row, azimuth, spread, vertical, east, north, most
):
    f, a, b, w = control.shape
    nx, ny = lax.axis_size("gx"), lax.axis_size("gy")
    tiles = nx * ny
    slots = tiles * most
    rows = inn.shape[0]
    smem = pl.BlockSpec(memory_space=pltpu.SMEM)
    anywhere = pl.BlockSpec(memory_space=pl.ANY)
    rim = pltpu.VMEM((2, f, a // 16, b, w), F32)
    gates = pltpu.VMEM((2, slots, w), F32)
    told = pltpu.VMEM((tiles, 128), I32)
    dma = pltpu.SemaphoreType.DMA
    return pl.pallas_call(
        functools.partial(fused_kernel, nx, ny, most),
        in_specs=[anywhere] * 9 + [smem] * 2,
        out_specs=(anywhere, anywhere, anywhere),
        out_shape=(
            jax.ShapeDtypeStruct((f, a, b, w), F32),
            jax.ShapeDtypeStruct((f, a, 16, w), F32),
            jax.ShapeDtypeStruct((2, 8, w), F32),
        ),
        scratch_shapes=[
            pltpu.VMEM((4, rows // 128, 128), I32),
            pltpu.VMEM((f, b, w), F32),
            pltpu.VMEM((f, a, a), F32),
            pltpu.VMEM((2, 8, w), F32),
            pltpu.VMEM((f, a, b + 16, w), F32),
            pltpu.VMEM((f, a, b, w), F32),
            pltpu.VMEM((f, a * (b + 8), w), F32),
            pltpu.VMEM((f, a * b, w), F32),
            rim,
            rim,
            rim,
            rim,
            gates,
            gates,
            told,
            gates,
            gates,
            told,
            pltpu.VMEM((4, rows, w), F32),
            pltpu.VMEM((2, rows, 4 * w), BF16),
            pltpu.VMEM((rows // 128, 128), I32),
            pltpu.VMEM((f, b, 3 * (b + 16)), BF16),
            pltpu.VMEM((f, b, 3 * b), BF16),
            pltpu.VMEM((f, 2 * a, 2 * a), BF16),
            pltpu.VMEM((f, 2 * a, 2 * a), BF16),
            pltpu.VMEM((f, slots, w), F32),
            gates,
            pltpu.VMEM((slots, 4 * w), BF16),
            pltpu.VMEM((slots, 2 * w), BF16),
            pltpu.VMEM((8, 128), I32),
            pltpu.VMEM((2, max(nx, ny), 2, 8, w), F32),
            pltpu.SMEM((8, 128), I32),
            dma((f,)),
            dma((2, 2, 2, f)),
            dma((2, 2, 2, f)),
            dma((2, 3, tiles)),
            dma((3,)),
            dma((2, 2, max(nx, ny))),
            dma((10,)),
            dma((2,)),
            dma((3, f)),
        ],
        compiler_params=pltpu.CompilerParams(
            vmem_limit_bytes=VMEM_BYTES, collective_id=0, has_side_effects=True
        ),
        name="fused",
    )(control, inn, wt, owner, level, row, azimuth, spread, vertical, east, north)


def final_kernel(
    scales, near, halo, totals, north, out, cost,
    buf, halo_v, totals_v, in_sem, out_sem, halo_sem, total_sem,
):
    fields, a, b, w = out.shape
    parts = in_sem.shape[1]
    zs = a // parts

    def rim(f):
        return pltpu.make_async_copy(halo.at[f], halo_v.at[f], halo_sem.at[f])

    def fetch(f, p):
        at = pl.ds(p * zs, zs)
        return pltpu.make_async_copy(near.at[f, at], buf.at[f, at], in_sem.at[f, p])

    def put(f, p):
        at = pl.ds(p * zs, zs)
        return pltpu.make_async_copy(buf.at[f, at], out.at[f, at], out_sem.at[f, p])

    total = pltpu.make_async_copy(totals, totals_v, total_sem.at[0])
    for f in range(fields):
        rim(f).start()
        for p in range(parts):
            fetch(f, p).start()
    total.start()
    r = lax.broadcasted_iota(I32, (16, 48), 0)
    c = lax.broadcasted_iota(I32, (16, 48), 1)
    j = c & 15
    distance = jnp.where(r < 8, r + 8 - j, 8 + j - r)
    fits = ((r >> 3) == (j >> 3)) & (distance <= 8)

    for f in range(fields):
        taps = taps_at(north, f, distance, fits)
        high = taps.astype(BF16).astype(F32)
        band = jnp.where(c >= 32, taps - high, high).astype(BF16)
        rim(f).wait()
        for part in range(parts):
            fetch(f, part).wait()
            for i in range(zs // 8):
                first = part * zs + i * 8
                x = jnp.concatenate([halo_v[f, first + z] for z in range(8)], axis=1)
                t = north_times(band, x)
                for z in range(8):
                    here = t[:, z * w : (z + 1) * w]
                    buf[f, first + z, 0:8] = buf[f, first + z, 0:8] + here[0:8]
                    buf[f, first + z, b - 8 : b] = buf[f, first + z, b - 8 : b] + here[8:16]
            put(f, part).start()
    total.wait()
    for k in range(2):
        cost[k] = jnp.sum(totals_v[k]) * scales[k]
    for f in range(fields):
        for p in range(parts):
            put(f, p).wait()


def final(scales, near, halo, totals, north):
    f, a, b, w = near.shape
    smem = pl.BlockSpec(memory_space=pltpu.SMEM)
    anywhere = pl.BlockSpec(memory_space=pl.ANY)
    return pl.pallas_call(
        functools.partial(final_kernel, scales),
        in_specs=[anywhere, anywhere, anywhere, smem],
        out_specs=(anywhere, smem),
        out_shape=(
            jax.ShapeDtypeStruct(near.shape, F32),
            jax.ShapeDtypeStruct((2,), F32),
        ),
        scratch_shapes=[
            pltpu.VMEM((f, a, b, w), F32),
            pltpu.VMEM((f, a, 16, w), F32),
            pltpu.VMEM(totals.shape, F32),
            pltpu.SemaphoreType.DMA((f, 4)),
            pltpu.SemaphoreType.DMA((f, 4)),
            pltpu.SemaphoreType.DMA((f,)),
            pltpu.SemaphoreType.DMA((1,)),
        ],
        compiler_params=pltpu.CompilerParams(vmem_limit_bytes=VMEM_BYTES),
        name="final",
    )(near, halo, totals, north)


def body(
    control, spread, kernel_east, kernel_north, vertical,
    tile_owner, gate_level, tile_row, beam_azimuth, innovation, obs_weight,
):
    tiles = lax.axis_size("gx") * lax.axis_size("gy")
    most = 2 * tile_owner.shape[0] // tiles
    lanes = [x.reshape(-1, 128) for x in (tile_owner, gate_level, tile_row, beam_azimuth)]
    near, halo, totals = fused(
        control, innovation, obs_weight, *lanes, spread, vertical, kernel_east, kernel_north, most
    )
    scales = [0.5 / (control.size * tiles), 0.5 / (innovation.size * tiles)]
    return final(scales, near, halo, totals, kernel_north)


def solution(mesh):
    both = ("gx", "gy")
    placed = (
        P(None, None, "gy", "gx"),
        P(None, "gy", "gx"),
        P(),
        P(),
        P(),
        P(both),
        P(both),
        P(both),
        P(both),
        P(both, None, None),
        P(both, None, None),
    )
    return jax.shard_map(
        body,
        mesh=mesh,
        in_specs=placed,
        out_specs=(P(None, None, "gy", "gx"), P()),
        check_vma=False,
    )
```

```python
import functools
import math

import jax
import jax.numpy as jnp
from jax import lax
from jax.experimental import pallas as pl
from jax.experimental.pallas import tpu as pltpu
from jax.sharding import PartitionSpec as P

F32 = jnp.float32
BF16 = jnp.bfloat16
I32 = jnp.int32
VMEM_BYTES = 58 * 1024 * 1024
MESH = pl.DeviceIdType.MESH


def split(value):
    high = value.astype(BF16)
    low = (value - high.astype(F32)).astype(BF16)
    return high, low


def doubled(weights):
    high, low = split(weights)
    row = jnp.concatenate([high, low], axis=1)
    return jnp.concatenate([row, row], axis=0)


def times(rows, weights):
    high, low = split(rows)
    both = jnp.dot(
        jnp.concatenate([high, low], axis=1), weights, preferred_element_type=F32
    )
    half = both.shape[1] // 2
    return both[:, :half] + both[:, half:]


def taps_at(kernel_ref, f, distance, allowed):
    total = jnp.zeros(distance.shape, F32)
    for d in range(kernel_ref.shape[1]):
        total = jnp.where(distance == d, kernel_ref[f, d], total)
    return jnp.where(allowed, total, 0.0)


def main_band(kernel_ref, f):
    r = lax.broadcasted_iota(I32, (128, 128), 0)
    c = lax.broadcasted_iota(I32, (128, 128), 1)
    return doubled(taps_at(kernel_ref, f, jnp.abs(r - c), jnp.abs(r - c) <= 8))


def rim_band(kernel_ref, f, offset):
    r = (lax.broadcasted_iota(I32, (128, 128), 0) + (128 - offset)) & 127
    c = (lax.broadcasted_iota(I32, (128, 128), 1) + (128 - offset)) & 127
    distance = jnp.abs(r - c)
    fits = ((r >> 4) == (c >> 4)) & ((r & 8) != (c & 8)) & (distance <= 8)
    return doubled(taps_at(kernel_ref, f, distance, fits))


def north_band(kernel_ref, f, ys, rim):
    reach = ys + 2 * rim
    r = lax.broadcasted_iota(I32, (ys, 3 * reach), 0)
    c = lax.broadcasted_iota(I32, (ys, 3 * reach), 1)
    j = jnp.where(c >= reach, c - reach, c)
    j = jnp.where(c >= 2 * reach, c - 2 * reach, j)
    distance = jnp.abs(r + rim - j)
    taps = taps_at(kernel_ref, f, distance, distance <= 8)
    high = taps.astype(BF16).astype(F32)
    return jnp.where(c >= 2 * reach, taps - high, high).astype(BF16)


def north_times(band, x):
    high, low = split(x)
    return jnp.dot(
        band, jnp.concatenate([high, low, high], axis=0), preferred_element_type=F32
    )


def pack_rims(get, put_right, put_left, groups, b):
    lane = lax.broadcasted_iota(I32, (b, 128), 1)
    first = (lane & 8) == 0

    def one(g, carry):
        even = jnp.zeros((b, 128), F32)
        odd = jnp.zeros((b, 128), F32)
        for q in range(8):
            even = jnp.where(
                (lane >> 4) == q, pltpu.roll(get(16 * g + 2 * q), (16 * q + 8) % 128, 1), even
            )
            odd = jnp.where(
                (((lane + 120) & 127) >> 4) == q,
                pltpu.roll(get(16 * g + 2 * q + 1), (16 * q + 16) % 128, 1),
                odd,
            )
        put_right(g, jnp.where(first, even, odd))
        put_left(g, jnp.where(first, odd, even))
        return carry

    lax.fori_loop(0, groups, one, 0)


def east_filter(get, low_ref, high_ref, put, bands, f, groups, spans):
    n = sum(count for _, count in spans)
    lane = lax.broadcasted_iota(I32, (n, 128), 1)
    first = (lane & 8) == 0
    edge = (lane < 8) | (lane >= 120)

    def side(ref, g):
        return jnp.concatenate([ref[f, g, at : at + count, :] for at, count in spans], axis=0)

    def one(g, carry):
        low = side(low_ref, g)
        high = side(high_ref, g)
        even = times(jnp.where(first, low, high), bands[f, 1])
        odd = times(jnp.where(first, high, low), bands[f, 2])
        for part in range(2):
            many = jnp.concatenate(
                [get(16 * g + 8 * part + j, *span) for j in range(8) for span in spans], axis=0
            )
            flat = times(many, bands[f, 0])
            for j in range(4):
                q = 4 * part + j
                at = 16 * g + 2 * q
                own = flat[2 * j * n : (2 * j + 1) * n]
                put(at, own + jnp.where(edge, pltpu.roll(even, (248 - 16 * q) % 128, 1), 0.0))
                own = flat[(2 * j + 1) * n : (2 * j + 2) * n]
                put(at + 1, own + jnp.where(edge, pltpu.roll(odd, (240 - 16 * q) % 128, 1), 0.0))
        return carry

    lax.fori_loop(0, groups, one, 0)


def mix_levels(parts, pair):
    high, low = split(pair)
    both = jnp.dot(parts, jnp.concatenate([high, low], axis=0), preferred_element_type=F32)
    half = both.shape[0] // 2
    return both[:half] + both[half:]


def fold_rows(x):
    return jnp.sum(x.reshape(-1, 8, 128), axis=0)


def ones_at(index, labels, groups):
    return jnp.concatenate(
        [
            jnp.where(index == labels[pl.ds(g, 1), :], 1.0, 0.0).astype(BF16)
            for g in range(groups)
        ],
        axis=1,
    )


def level_parts(v):
    high = v.astype(BF16).astype(F32)
    both = jnp.concatenate([high, v - high], axis=0)
    return jnp.concatenate([both, both], axis=1).astype(BF16)


def fused_kernel(
    nx, ny, most,
    control, inn, wt, owner_in, level_in, row_in, azimuth_in, spread_in, vertical_in, east_in, north_in,
    near, halo, total_out,
    lanes_v, spread, vertical, total_v, ext, tbuf, lift, state, right, left, low, high,
    windbuf, reflbuf, geobuf, wind, refl, geo, rows_v, rows_rhs, slot_v, band_s, inner_s,
    vert, vert_back, bands, east, north,
    m, waves, rhs, label_v, parts,
    cell_s,
    fill_sem, rim_sem, edge_sem, row_sem, own_sem, sum_sem, load_sem, label_sem, put_sem, ready,
):
    fields, a, b, w = control.shape
    tiles = nx * ny
    slots = tiles * most
    rows = inn.shape[0]
    groups = rows // 128
    pitch = b + 8
    ix = lax.axis_index("gx")
    iy = lax.axis_index("gy")
    me = ix * ny + iy
    up_x, down_x = jnp.minimum(ix + 1, nx - 1), jnp.maximum(ix - 1, 0)
    up_y, down_y = jnp.minimum(iy + 1, ny - 1), jnp.maximum(iy - 1, 0)
    has_up_x, has_down_x = ix < nx - 1, ix > 0
    has_up_y, has_down_y = iy < ny - 1, iy > 0

    def place(t):
        return {"gx": t // ny, "gy": lax.rem(t, ny)}

    def fill(f):
        return pltpu.make_async_copy(
            control.at[f], ext.at[f, :, pl.ds(8, b)], fill_sem.at[f]
        )

    def load(k):
        src = (inn, wt)[k % 2]
        return pltpu.make_async_copy(src.at[:, k // 2], rows_v.at[k], load_sem.at[k])

    small = (
        (owner_in, lanes_v.at[0]),
        (level_in, lanes_v.at[1]),
        (row_in, lanes_v.at[2]),
        (azimuth_in, lanes_v.at[3]),
        (spread_in, spread),
        (vertical_in, vertical),
        (east_in, east),
        (north_in, north),
    )

    def fetch(k):
        return pltpu.make_async_copy(small[k][0], small[k][1], load_sem.at[4 + k])

    for k in range(len(small)):
        fetch(k).start()
    for k in range(4):
        load(k).start()
    for f in range(fields):
        fill(f).start()
    owner, level, row, azimuth = (lanes_v.at[k] for k in range(4))

    barrier = pltpu.get_barrier_semaphore()

    for axis, at, n in (("gx", ix, nx), ("gy", iy, ny)):
        for j in range(1, n):
            pl.semaphore_signal(
                barrier, inc=1, device_id={axis: lax.rem(at + j, n)}, device_id_type=MESH
            )

    pl.semaphore_wait(barrier, nx + ny - 2)
    for j in range(1, ny):
        pl.semaphore_signal(
            ready, inc=1, device_id={"gy": lax.rem(iy + j, ny)}, device_id_type=MESH
        )

    def remote(src, dst, sems, sweep, which, f, axis, target):
        return pltpu.make_async_remote_copy(
            src_ref=src,
            dst_ref=dst,
            send_sem=sems.at[0, sweep, which, f],
            recv_sem=sems.at[1, sweep, which, f],
            device_id={axis: target},
            device_id_type=MESH,
        )

    def rim_up(f, sweep):
        return remote(right.at[sweep, f], low.at[sweep, f], rim_sem, sweep, 0, f, "gx", up_x)

    def rim_down(f, sweep):
        return remote(left.at[sweep, f], high.at[sweep, f], rim_sem, sweep, 1, f, "gx", down_x)

    def edge_up(f, sweep):
        if sweep == 0:
            src, dst = control.at[f, :, pl.ds(b - 8, 8)], ext.at[f, :, pl.ds(0, 8)]
        else:
            src, dst = tbuf.at[f, :, pl.ds(b - 8, 8)], halo.at[f, :, pl.ds(0, 8)]
        return remote(src, dst, edge_sem, sweep, 0, f, "gy", up_y)

    def edge_down(f, sweep):
        if sweep == 0:
            src, dst = control.at[f, :, pl.ds(0, 8)], ext.at[f, :, pl.ds(b + 8, 8)]
        else:
            src, dst = tbuf.at[f, :, pl.ds(0, 8)], halo.at[f, :, pl.ds(8, 8)]
        return remote(src, dst, edge_sem, sweep, 1, f, "gy", down_y)

    def start_edges(f, sweep):
        @pl.when(has_up_y)
        def _():
            edge_up(f, sweep).start()

        @pl.when(has_down_y)
        def _():
            edge_down(f, sweep).start()

    def wait_edges(f, sweep):
        @pl.when(has_down_y)
        def _():
            edge_up(f, sweep).wait_recv()

        @pl.when(has_up_y)
        def _():
            edge_down(f, sweep).wait_recv()

    def start_rims(f, sweep):
        @pl.when(has_up_x)
        def _():
            rim_up(f, sweep).start()

        @pl.when(has_down_x)
        def _():
            rim_down(f, sweep).start()

    def wait_rims(f, sweep):
        @pl.when(has_down_x)
        def _():
            rim_up(f, sweep).wait_recv()

        @pl.when(has_up_x)
        def _():
            rim_down(f, sweep).wait_recv()

    kinds = (wind, refl, geo)

    def block(ref, kind, t):
        if kind == 2:
            return ref.at[pl.ds(t, 1)]
        return ref.at[:, pl.ds(pl.multiple_of(t * most, most), most)]

    def landing(kind, t):
        return block((windbuf, reflbuf, geobuf)[kind], kind, t)

    def row_copy(kind, j):
        t = lax.rem(me + j, tiles)
        return pltpu.make_async_remote_copy(
            src_ref=block(kinds[kind], kind, t),
            dst_ref=landing(kind, me),
            send_sem=row_sem.at[0, kind, j],
            recv_sem=row_sem.at[1, kind, j],
            device_id=place(t),
            device_id_type=MESH,
        )

    def row_arrival(kind, j):
        t = lax.rem(me + tiles - j, tiles)
        return pltpu.make_async_remote_copy(
            src_ref=block(kinds[kind], kind, t),
            dst_ref=landing(kind, t),
            send_sem=row_sem.at[0, kind, j],
            recv_sem=row_sem.at[1, kind, j],
            device_id=place(t),
            device_id_type=MESH,
        )

    def own_rows(kind):
        return pltpu.make_async_copy(
            block(kinds[kind], kind, me), landing(kind, me), own_sem.at[kind]
        )

    def start_rows(kind):
        def one(j, carry):
            row_copy(kind, j).start()
            return carry

        lax.fori_loop(1, tiles, one, 0)
        own_rows(kind).start()

    def wait_rows(kind):
        def one(j, carry):
            row_arrival(kind, j).wait_recv()
            return carry

        lax.fori_loop(1, tiles, one, 0)
        own_rows(kind).wait()

    for f in range(fields):
        start_edges(f, 0)

    for k in range(len(small)):
        fetch(k).wait()

    tile_index = lax.broadcasted_iota(I32, (tiles, 128), 0)
    member = ones_at(tile_index, owner, groups)
    before = jnp.concatenate(
        [
            jnp.where(
                lax.broadcasted_iota(I32, (rows, 128), 0)
                < lax.broadcasted_iota(I32, (rows, 128), 1) + 128 * g,
                1.0,
                0.0,
            ).astype(BF16)
            for g in range(groups)
        ],
        axis=1,
    )
    ahead = jnp.dot(member, before, preferred_element_type=F32)
    ranks = []
    for g in range(groups):
        here = jnp.where(tile_index == owner[pl.ds(g, 1), :], ahead[:, 128 * g : 128 * g + 128], 0.0)
        ranks.append(jnp.sum(here, axis=0, keepdims=True).astype(I32))
        slot_v[pl.ds(g, 1), :] = owner[pl.ds(g, 1), :] * most + ranks[g]
    k_index = lax.broadcasted_iota(I32, (128, 128), 0)
    told = []
    for g in range(groups):
        total = jnp.zeros((128, 128), F32)
        values = (
            level[pl.ds(g, 1), :],
            row[pl.ds(g, 1), :],
            azimuth[pl.ds(g, 1), :] - 180,
        )
        for part, value in enumerate(values):
            total = jnp.where(k_index == ranks[g] + part * most, value.astype(F32), total)
        told.append(total.astype(BF16))
    geo[...] = lax.dot_general(
        member,
        jnp.concatenate(told, axis=1),
        (((1,), (1,)), ((), ())),
        preferred_element_type=F32,
    ).astype(I32)
    pl.semaphore_wait(ready, ny - 1)
    start_rows(2)

    def pack(kind):
        target = kinds[kind]
        for k in range(2):
            one, two = split(rows_v[2 * kind + k])
            rows_rhs[kind, :, k * w : (k + 1) * w] = one
            rows_rhs[kind, :, (2 + k) * w : (3 + k) * w] = two

        def one(i, carry):
            index = lax.broadcasted_iota(I32, (256, 128), 0) + i * 256
            r = jnp.dot(
                ones_at(index, slot_v, groups), rows_rhs[kind], preferred_element_type=F32
            )
            at = pl.ds(pl.multiple_of(i * 256, 256), 256)
            target[0, at, :] = r[:, :w] + r[:, 2 * w : 3 * w]
            target[1, at, :] = r[:, w : 2 * w] + r[:, 3 * w :]
            return carry

        lax.fori_loop(0, slots // 256, one, 0)

    for k in range(4):
        load(k).wait()
    pack(0)

    @pl.when(jnp.logical_not(has_down_x))
    def _():
        low[...] = jnp.zeros_like(low)

    @pl.when(jnp.logical_not(has_up_x))
    def _():
        high[...] = jnp.zeros_like(high)

    @pl.when(jnp.logical_not(has_down_y))
    def _():
        ext[:, :, 0:8] = jnp.zeros((fields, a, 8, w), F32)

    @pl.when(jnp.logical_not(has_up_y))
    def _():
        ext[:, :, b + 8 :] = jnp.zeros((fields, a, 8, w), F32)

    for f in range(fields):
        band_s[f] = north_band(north, f, b, 8)
        inner_s[f] = north_band(north, f, b, 0)
        vert[f] = level_parts(vertical[f])
        vert_back[f] = level_parts(vertical[f].T)
        bands[f, 0] = main_band(east, f)
        bands[f, 1] = rim_band(east, f, 0)
        bands[f, 2] = rim_band(east, f, 8)

    total_square = jnp.zeros((8, w), F32)
    for f in range(fields):
        fill(f).wait()

        def square(i, total):
            v = ext[f, i, pl.ds(8, b), :]
            return total + fold_rows(v * v)

        total_square = lax.fori_loop(0, a, square, total_square)
    parts[0, ix, 0] = total_square

    def forward_north(f, carry):
        wait_edges(f, 0)
        band = band_s[f]

        def one(i, c):
            for j in range(8):
                p = 16 * i + 2 * j
                r = north_times(band, jnp.concatenate([ext[f, p], ext[f, p + 1]], axis=1))
                tbuf[f, p] = r[:, :w]
                tbuf[f, p + 1] = r[:, w:]
            return c

        lax.fori_loop(0, a // 16, one, 0)

        def put_right(g, v):
            right[0, f, g] = v

        def put_left(g, v):
            left[0, f, g] = v

        pack_rims(lambda s: tbuf[f, s], put_right, put_left, a // 16, b)
        start_rims(f, 0)
        return carry

    def forward_east(f, carry):
        wait_rims(f, 0)

        def put(s, v):
            lift[f, pl.ds(pl.multiple_of(s * pitch, 8), b), :] = v

        east_filter(
            lambda s, at, count: tbuf[f, s], low.at[0], high.at[0], put, bands, f, a // 16, ((0, b),)
        )
        v = vert[f]

        def one(p, c):
            for j in range(8):
                y = p * 16 + 2 * j
                x = jnp.concatenate(
                    [lift[f, pl.ds(y, a, stride=pitch), :], lift[f, pl.ds(y + 1, a, stride=pitch), :]],
                    axis=1,
                )
                r = mix_levels(v, x)
                at = pl.multiple_of(y * a, 8)
                state[f, pl.ds(at, a), :] = r[:, :w] * spread[f, pl.ds(y, 1), :]
                at = pl.multiple_of(y * a + a, 8)
                state[f, pl.ds(at, a), :] = r[:, w:] * spread[f, pl.ds(y + 1, 1), :]
            return c

        lax.fori_loop(0, b // 16, one, 0)
        return carry

    forward_north(0, 0)
    forward_north(1, 0)
    start_rows(0)
    pack(1)
    forward_east(0, 0)
    forward_north(2, 0)
    lax.fori_loop(1, fields, forward_east, 0)
    start_rows(1)

    wait_rows(2)
    per = 128 // most
    lane = lax.broadcasted_iota(I32, (8, 128), 1)

    def label(part):
        total = jnp.zeros((8, 128), I32)
        for q in range(per):
            piece = geobuf[pl.ds(q, 8, stride=per), :]
            shift = ((q - part) * most) % 128
            piece = pltpu.roll(piece, shift, 1) if shift else piece
            total = jnp.where((lane >= q * most) & (lane < (q + 1) * most), piece, total)
        return total

    cell = label(1) * a + label(0)
    angle = (label(2) + 180).astype(F32) * (2.0 * math.pi / 360.0)
    label_v[...] = cell
    to_cells = pltpu.make_async_copy(label_v, cell_s, label_sem.at[0])
    to_cells.start()
    for k, wave in enumerate((jnp.cos(angle), jnp.sin(angle))):
        for g in range(8):
            waves[k, g * 128 : (g + 1) * 128, :] = jnp.broadcast_to(
                wave[g : g + 1], (128, 128)
            ).T
    to_cells.wait()

    def pick(i, carry):
        block_at, first = i // 8, lax.rem(i, 8) * 16
        for j in range(16):
            at = jnp.clip(cell_s[block_at, first + j], 0, a * b - 1)
            for f in range(fields):
                m[f, pl.ds(i * 16 + j, 1), :] = state[f, pl.ds(at, 1), :]
        return carry

    lax.fori_loop(0, slots // 16, pick, 0)
    wait_rows(0)

    def weigh_wind(i, total):
        at = pl.ds(pl.multiple_of(i * 16, 16), 16)
        d = waves[0, at, :] * m[0, at, :] + waves[1, at, :] * m[1, at, :] - windbuf[0, at, :]
        v = windbuf[1, at, :] * d
        for j in range(2):
            one, two = split(v * waves[j, at, :])
            rhs[j, at, 0:w] = one
            rhs[j, at, w : 2 * w] = two
        return total + fold_rows(v * d)

    def weigh_refl(i, total):
        at = pl.ds(pl.multiple_of(i * 16, 16), 16)
        d = m[2, at, :] - reflbuf[0, at, :]
        v = reflbuf[1, at, :] * d
        one, two = split(v)
        rhs[2, at, 0:w] = one
        rhs[2, at, w : 2 * w] = two
        return total + fold_rows(v * d)

    def lower(f):
        many = 16
        chunk = many * a
        v = vert_back[f]

        def one(i, carry):
            index = lax.broadcasted_iota(I32, (chunk, 128), 0) + i * chunk
            ones = ones_at(index, label_v, slots // 128)
            r = jnp.dot(ones, rhs[f], preferred_element_type=F32)
            grown = r[:, :w] + r[:, w:]
            for j in range(many // 2):
                y = i * many + 2 * j
                x = jnp.concatenate(
                    [grown[2 * j * a : (2 * j + 1) * a], grown[(2 * j + 1) * a : (2 * j + 2) * a]],
                    axis=1,
                )
                t = mix_levels(v, x)
                lift[f, pl.ds(y, a, stride=pitch), :] = t[:, :w] * spread[f, pl.ds(y, 1), :]
                lift[f, pl.ds(y + 1, a, stride=pitch), :] = t[:, w:] * spread[f, pl.ds(y + 1, 1), :]
            return carry

        lax.fori_loop(0, b // many, one, 0)

    def back_rims(f):
        def put_right(g, v):
            right[1, f, g] = v

        def put_left(g, v):
            left[1, f, g] = v

        def get(s):
            return lift[f, pl.ds(pl.multiple_of(s * pitch, 8), b), :]

        pack_rims(get, put_right, put_left, a // 16, b)
        start_rims(f, 1)

    def back_get(f):
        def get(s, at, count):
            return lift[f, pl.ds(pl.multiple_of(s * pitch + at, 8), count), :]

        return get

    def back_edges(f):
        wait_rims(f, 1)

        def put(s, v):
            tbuf[f, s, 0:8, :] = v[0:8]
            tbuf[f, s, b - 8 : b, :] = v[8:16]

        spans = ((0, 8), (b - 8, 8))
        east_filter(back_get(f), low.at[1], high.at[1], put, bands, f, a // 16, spans)
        start_edges(f, 1)

    def back_east(f):
        def put(s, v):
            tbuf[f, s, 8 : b - 8, :] = v

        east_filter(back_get(f), low.at[1], high.at[1], put, bands, f, a // 16, ((8, b - 16),))

    def keep(f):
        return pltpu.make_async_copy(ext.at[f, :, pl.ds(8, b)], near.at[f], put_sem.at[0, f])

    def blank(f, side):
        return pltpu.make_async_copy(
            ext.at[f, :, pl.ds(side * (b + 8), 8)],
            halo.at[f, :, pl.ds(8 * side, 8)],
            put_sem.at[1 + side, f],
        )

    def blanks(act):
        for side, there in ((0, has_down_y), (1, has_up_y)):

            @pl.when(jnp.logical_not(there))
            def _():
                for f in range(fields):
                    act(blank(f, side))

    def back_inner(f, carry):
        band = inner_s[f]

        def one(i, c):
            for j in range(8):
                p = 16 * i + 2 * j
                r = north_times(band, jnp.concatenate([tbuf[f, p], tbuf[f, p + 1]], axis=1))
                at = pl.ds(8, b)
                ext[f, p, at, :] = ext[f, p, at, :] + r[:, :w]
                ext[f, p + 1, at, :] = ext[f, p + 1, at, :] + r[:, w:]
            return c

        lax.fori_loop(0, a // 16, one, 0)
        keep(f).start()
        return carry

    blanks(lambda copy: copy.start())
    observed = lax.fori_loop(0, slots // 16, weigh_wind, jnp.zeros((8, w), F32))

    def each(part, first, last):
        def one(f, carry):
            part(f)
            return carry

        lax.fori_loop(first, last, one, 0)

    def scatter(f):
        lower(f)
        back_rims(f)

    each(scatter, 0, 2)
    each(back_edges, 0, 2)
    wait_rows(1)
    observed = lax.fori_loop(0, slots // 16, weigh_refl, observed)
    parts[0, ix, 1] = observed

    def share(axis, slot, peer, row):
        return pltpu.make_async_remote_copy(
            src_ref=parts.at[row, slot],
            dst_ref=parts.at[row, slot],
            send_sem=sum_sem.at[0, row, peer],
            recv_sem=sum_sem.at[1, row, slot],
            device_id={axis: peer},
            device_id_type=MESH,
        )

    def arrival(axis, peer, row):
        return pltpu.make_async_remote_copy(
            src_ref=parts.at[row, peer],
            dst_ref=parts.at[row, peer],
            send_sem=sum_sem.at[0, row, peer],
            recv_sem=sum_sem.at[1, row, peer],
            device_id={axis: peer},
            device_id_type=MESH,
        )

    for j in range(1, nx):
        share("gx", ix, lax.rem(ix + j, nx), 0).start()
    scatter(2)
    each(back_east, 0, 2)
    back_inner(0, 0)
    for j in range(1, nx):
        arrival("gx", lax.rem(ix + j, nx), 0).wait_recv()
    row_sum = parts[0, 0]
    for j in range(1, nx):
        row_sum = row_sum + parts[0, j]
    parts[1, iy] = row_sum
    for j in range(1, ny):
        share("gy", iy, lax.rem(iy + j, ny), 1).start()
    back_edges(2)
    back_inner(1, 0)
    back_east(2)
    for j in range(1, ny):
        arrival("gy", lax.rem(iy + j, ny), 1).wait_recv()
    all_sum = parts[1, 0]
    for j in range(1, ny):
        all_sum = all_sum + parts[1, j]
    total_v[...] = all_sum
    totals = pltpu.make_async_copy(total_v, total_out, label_sem.at[1])
    totals.start()
    back_inner(2, 0)
    for f in range(fields):
        wait_edges(f, 1)
        keep(f).wait()
    blanks(lambda copy: copy.wait())
    totals.wait()

    for j in range(1, nx):
        share("gx", ix, lax.rem(ix + j, nx), 0).wait_send()
    for j in range(1, ny):
        share("gy", iy, lax.rem(iy + j, ny), 1).wait_send()

    for kind in range(3):

        def sent(j, carry):
            row_copy(kind, j).wait_send()
            return carry

        lax.fori_loop(1, tiles, sent, 0)

    for sweep in range(2):
        for f in range(fields):

            @pl.when(has_up_x)
            def _():
                rim_up(f, sweep).wait_send()

            @pl.when(has_down_x)
            def _():
                rim_down(f, sweep).wait_send()

            @pl.when(has_up_y)
            def _():
                edge_up(f, sweep).wait_send()

            @pl.when(has_down_y)
            def _():
                edge_down(f, sweep).wait_send()


def fused(
    control, inn, wt, owner, level, row, azimuth, spread, vertical, east, north, most
):
    f, a, b, w = control.shape
    nx, ny = lax.axis_size("gx"), lax.axis_size("gy")
    tiles = nx * ny
    slots = tiles * most
    rows = inn.shape[0]
    anywhere = pl.BlockSpec(memory_space=pl.ANY)
    rim = pltpu.VMEM((2, f, a // 16, b, w), F32)
    gates = pltpu.VMEM((2, slots, w), F32)
    told = pltpu.VMEM((tiles, 128), I32)
    dma = pltpu.SemaphoreType.DMA
    return pl.pallas_call(
        functools.partial(fused_kernel, nx, ny, most),
        in_specs=[anywhere] * 11,
        out_specs=(anywhere, anywhere, anywhere),
        out_shape=(
            jax.ShapeDtypeStruct((f, a, b, w), F32),
            jax.ShapeDtypeStruct((f, a, 16, w), F32),
            jax.ShapeDtypeStruct((2, 8, w), F32),
        ),
        scratch_shapes=[
            pltpu.VMEM((4, rows // 128, 128), I32),
            pltpu.VMEM((f, b, w), F32),
            pltpu.VMEM((f, a, a), F32),
            pltpu.VMEM((2, 8, w), F32),
            pltpu.VMEM((f, a, b + 16, w), F32),
            pltpu.VMEM((f, a, b, w), F32),
            pltpu.VMEM((f, a * (b + 8), w), F32),
            pltpu.VMEM((f, a * b, w), F32),
            rim,
            rim,
            rim,
            rim,
            gates,
            gates,
            told,
            gates,
            gates,
            told,
            pltpu.VMEM((4, rows, w), F32),
            pltpu.VMEM((2, rows, 4 * w), BF16),
            pltpu.VMEM((rows // 128, 128), I32),
            pltpu.VMEM((f, b, 3 * (b + 16)), BF16),
            pltpu.VMEM((f, b, 3 * b), BF16),
            pltpu.VMEM((f, 2 * a, 2 * a), BF16),
            pltpu.VMEM((f, 2 * a, 2 * a), BF16),
            pltpu.VMEM((f, 3, 2 * w, 2 * w), BF16),
            pltpu.SMEM(east.shape, F32),
            pltpu.SMEM(north.shape, F32),
            pltpu.VMEM((f, slots, w), F32),
            gates,
            pltpu.VMEM((f, slots, 2 * w), BF16),
            pltpu.VMEM((8, 128), I32),
            pltpu.VMEM((2, max(nx, ny), 2, 8, w), F32),
            pltpu.SMEM((8, 128), I32),
            dma((f,)),
            dma((2, 2, 2, f)),
            dma((2, 2, 2, f)),
            dma((2, 3, tiles)),
            dma((3,)),
            dma((2, 2, max(nx, ny))),
            dma((12,)),
            dma((2,)),
            dma((3, f)),
            pltpu.SemaphoreType.REGULAR,
        ],
        compiler_params=pltpu.CompilerParams(
            vmem_limit_bytes=VMEM_BYTES, collective_id=0, has_side_effects=True
        ),
        name="fused",
    )(control, inn, wt, owner, level, row, azimuth, spread, vertical, east, north)


def final_kernel(
    scales, near, halo, totals, north_in, out, cost,
    buf, halo_v, totals_v, north, in_sem, out_sem, halo_sem, total_sem,
):
    fields, a, b, w = out.shape
    parts = in_sem.shape[1]
    zs = a // parts

    def rim(f):
        return pltpu.make_async_copy(halo.at[f], halo_v.at[f], halo_sem.at[f])

    def fetch(f, p):
        at = pl.ds(p * zs, zs)
        return pltpu.make_async_copy(near.at[f, at], buf.at[f, at], in_sem.at[f, p])

    def put(f, p):
        at = pl.ds(p * zs, zs)
        return pltpu.make_async_copy(buf.at[f, at], out.at[f, at], out_sem.at[f, p])

    total = pltpu.make_async_copy(totals, totals_v, total_sem.at[0])
    taps_in = pltpu.make_async_copy(north_in, north, total_sem.at[1])
    taps_in.start()
    for f in range(fields):
        rim(f).start()
        for p in range(parts):
            fetch(f, p).start()
    total.start()
    r = lax.broadcasted_iota(I32, (16, 48), 0)
    c = lax.broadcasted_iota(I32, (16, 48), 1)
    j = c & 15
    distance = jnp.where(r < 8, r + 8 - j, 8 + j - r)
    fits = ((r >> 3) == (j >> 3)) & (distance <= 8)
    taps_in.wait()

    for f in range(fields):
        taps = taps_at(north, f, distance, fits)
        high = taps.astype(BF16).astype(F32)
        band = jnp.where(c >= 32, taps - high, high).astype(BF16)
        rim(f).wait()
        for part in range(parts):
            fetch(f, part).wait()
            for i in range(zs // 8):
                first = part * zs + i * 8
                x = jnp.concatenate([halo_v[f, first + z] for z in range(8)], axis=1)
                t = north_times(band, x)
                for z in range(8):
                    here = t[:, z * w : (z + 1) * w]
                    buf[f, first + z, 0:8] = buf[f, first + z, 0:8] + here[0:8]
                    buf[f, first + z, b - 8 : b] = buf[f, first + z, b - 8 : b] + here[8:16]
            put(f, part).start()
    total.wait()
    for k in range(2):
        cost[k] = jnp.sum(totals_v[k]) * scales[k]
    for f in range(fields):
        for p in range(parts):
            put(f, p).wait()


def final(scales, near, halo, totals, north):
    f, a, b, w = near.shape
    smem = pl.BlockSpec(memory_space=pltpu.SMEM)
    anywhere = pl.BlockSpec(memory_space=pl.ANY)
    return pl.pallas_call(
        functools.partial(final_kernel, scales),
        in_specs=[anywhere] * 4,
        out_specs=(anywhere, smem),
        out_shape=(
            jax.ShapeDtypeStruct(near.shape, F32),
            jax.ShapeDtypeStruct((2,), F32),
        ),
        scratch_shapes=[
            pltpu.VMEM((f, a, b, w), F32),
            pltpu.VMEM((f, a, 16, w), F32),
            pltpu.VMEM(totals.shape, F32),
            pltpu.SMEM(north.shape, F32),
            pltpu.SemaphoreType.DMA((f, 4)),
            pltpu.SemaphoreType.DMA((f, 4)),
            pltpu.SemaphoreType.DMA((f,)),
            pltpu.SemaphoreType.DMA((2,)),
        ],
        compiler_params=pltpu.CompilerParams(vmem_limit_bytes=VMEM_BYTES),
        name="final",
    )(near, halo, totals, north)


def body(
    control, spread, kernel_east, kernel_north, vertical,
    tile_owner, gate_level, tile_row, beam_azimuth, innovation, obs_weight,
):
    tiles = lax.axis_size("gx") * lax.axis_size("gy")
    most = 2 * tile_owner.shape[0] // tiles
    lanes = [x.reshape(-1, 128) for x in (tile_owner, gate_level, tile_row, beam_azimuth)]
    near, halo, totals = fused(
        control, innovation, obs_weight, *lanes, spread, vertical, kernel_east, kernel_north, most
    )
    scales = [0.5 / (control.size * tiles), 0.5 / (innovation.size * tiles)]
    return final(scales, near, halo, totals, kernel_north)


def solution(mesh):
    both = ("gx", "gy")
    placed = (
        P(None, None, "gy", "gx"),
        P(None, "gy", "gx"),
        P(),
        P(),
        P(),
        P(both),
        P(both),
        P(both),
        P(both),
        P(both, None, None),
        P(both, None, None),
    )
    return jax.shard_map(
        body,
        mesh=mesh,
        in_specs=placed,
        out_specs=(P(None, None, "gy", "gx"), P()),
        check_vma=False,
    )
```

```python
import functools
import math

import jax
import jax.numpy as jnp
from jax import lax
from jax.experimental import pallas as pl
from jax.experimental.pallas import tpu as pltpu
from jax.sharding import PartitionSpec as P

F32 = jnp.float32
BF16 = jnp.bfloat16
I32 = jnp.int32
VMEM_BYTES = 58 * 1024 * 1024
MESH = pl.DeviceIdType.MESH


def split(value):
    high = value.astype(BF16)
    low = (value - high.astype(F32)).astype(BF16)
    return high, low


def doubled(weights):
    high, low = split(weights)
    row = jnp.concatenate([high, low], axis=1)
    return jnp.concatenate([row, row], axis=0)


def times(rows, weights):
    high, low = split(rows)
    both = jnp.dot(
        jnp.concatenate([high, low], axis=1), weights, preferred_element_type=F32
    )
    half = both.shape[1] // 2
    return both[:, :half] + both[:, half:]


def taps_at(kernel_ref, f, distance, allowed):
    total = jnp.zeros(distance.shape, F32)
    for d in range(kernel_ref.shape[1]):
        total = jnp.where(distance == d, kernel_ref[f, d], total)
    return jnp.where(allowed, total, 0.0)


def main_band(kernel_ref, f):
    r = lax.broadcasted_iota(I32, (128, 128), 0)
    c = lax.broadcasted_iota(I32, (128, 128), 1)
    return doubled(taps_at(kernel_ref, f, jnp.abs(r - c), jnp.abs(r - c) <= 8))


def rim_band(kernel_ref, f, offset):
    r = (lax.broadcasted_iota(I32, (128, 128), 0) + (128 - offset)) & 127
    c = (lax.broadcasted_iota(I32, (128, 128), 1) + (128 - offset)) & 127
    distance = jnp.abs(r - c)
    fits = ((r >> 4) == (c >> 4)) & ((r & 8) != (c & 8)) & (distance <= 8)
    return doubled(taps_at(kernel_ref, f, distance, fits))


def north_band(kernel_ref, f, ys, rim):
    reach = ys + 2 * rim
    r = lax.broadcasted_iota(I32, (ys, 3 * reach), 0)
    c = lax.broadcasted_iota(I32, (ys, 3 * reach), 1)
    j = jnp.where(c >= reach, c - reach, c)
    j = jnp.where(c >= 2 * reach, c - 2 * reach, j)
    distance = jnp.abs(r + rim - j)
    taps = taps_at(kernel_ref, f, distance, distance <= 8)
    high = taps.astype(BF16).astype(F32)
    return jnp.where(c >= 2 * reach, taps - high, high).astype(BF16)


def north_times(band, x):
    high, low = split(x)
    return jnp.dot(
        band, jnp.concatenate([high, low, high], axis=0), preferred_element_type=F32
    )


def pack_rims(get, put_right, put_left, groups, b):
    lane = lax.broadcasted_iota(I32, (b, 128), 1)
    first = (lane & 8) == 0

    def one(g, carry):
        even = jnp.zeros((b, 128), F32)
        odd = jnp.zeros((b, 128), F32)
        for q in range(8):
            even = jnp.where(
                (lane >> 4) == q, pltpu.roll(get(16 * g + 2 * q), (16 * q + 8) % 128, 1), even
            )
            odd = jnp.where(
                (((lane + 120) & 127) >> 4) == q,
                pltpu.roll(get(16 * g + 2 * q + 1), (16 * q + 16) % 128, 1),
                odd,
            )
        put_right(g, jnp.where(first, even, odd))
        put_left(g, jnp.where(first, odd, even))
        return carry

    lax.fori_loop(0, groups, one, 0)


def east_filter(get, low_ref, high_ref, put, bands, f, groups, spans):
    n = sum(count for _, count in spans)
    lane = lax.broadcasted_iota(I32, (n, 128), 1)
    first = (lane & 8) == 0
    edge = (lane < 8) | (lane >= 120)

    def side(ref, g):
        return jnp.concatenate([ref[f, g, at : at + count, :] for at, count in spans], axis=0)

    def one(g, carry):
        low = side(low_ref, g)
        high = side(high_ref, g)
        even = times(jnp.where(first, low, high), bands[f, 1])
        odd = times(jnp.where(first, high, low), bands[f, 2])
        for part in range(2):
            many = jnp.concatenate(
                [get(16 * g + 8 * part + j, *span) for j in range(8) for span in spans], axis=0
            )
            flat = times(many, bands[f, 0])
            for j in range(4):
                q = 4 * part + j
                at = 16 * g + 2 * q
                own = flat[2 * j * n : (2 * j + 1) * n]
                put(at, own + jnp.where(edge, pltpu.roll(even, (248 - 16 * q) % 128, 1), 0.0))
                own = flat[(2 * j + 1) * n : (2 * j + 2) * n]
                put(at + 1, own + jnp.where(edge, pltpu.roll(odd, (240 - 16 * q) % 128, 1), 0.0))
        return carry

    lax.fori_loop(0, groups, one, 0)


def mix_levels(parts, pair):
    high, low = split(pair)
    both = jnp.dot(parts, jnp.concatenate([high, low], axis=0), preferred_element_type=F32)
    half = both.shape[0] // 2
    return both[:half] + both[half:]


def fold_rows(x):
    return jnp.sum(x.reshape(-1, 8, 128), axis=0)


def ones_at(index, labels, groups):
    return jnp.concatenate(
        [
            jnp.where(index == labels[pl.ds(g, 1), :], 1.0, 0.0).astype(BF16)
            for g in range(groups)
        ],
        axis=1,
    )


def level_parts(v):
    high = v.astype(BF16).astype(F32)
    both = jnp.concatenate([high, v - high], axis=0)
    return jnp.concatenate([both, both], axis=1).astype(BF16)


def fused_kernel(
    nx, ny, most,
    control, inn, wt, owner_in, level_in, row_in, azimuth_in, spread_in, vertical_in, east_in, north_in,
    near, halo, total_out,
    lanes_v, spread, vertical, total_v, ext, tbuf, lift, state, right, left, low, high,
    windbuf, reflbuf, geobuf, wind, refl, geo, rows_v, rows_rhs, slot_v, band_s, inner_s,
    vert, vert_back, bands, east, north,
    m, waves, rhs, label_v, parts, ones_v,
    cell_s,
    fill_sem, rim_sem, edge_sem, row_sem, own_sem, sum_sem, load_sem, label_sem, put_sem, ready,
):
    fields, a, b, w = control.shape
    tiles = nx * ny
    slots = tiles * most
    rows = inn.shape[0]
    groups = rows // 128
    pitch = b + 8
    ix = lax.axis_index("gx")
    iy = lax.axis_index("gy")
    me = ix * ny + iy
    up_x, down_x = jnp.minimum(ix + 1, nx - 1), jnp.maximum(ix - 1, 0)
    up_y, down_y = jnp.minimum(iy + 1, ny - 1), jnp.maximum(iy - 1, 0)
    has_up_x, has_down_x = ix < nx - 1, ix > 0
    has_up_y, has_down_y = iy < ny - 1, iy > 0

    def place(t):
        return {"gx": t // ny, "gy": lax.rem(t, ny)}

    def fill(f):
        return pltpu.make_async_copy(
            control.at[f], ext.at[f, :, pl.ds(8, b)], fill_sem.at[f]
        )

    def load(k):
        src = (inn, wt)[k % 2]
        return pltpu.make_async_copy(src.at[:, k // 2], rows_v.at[k], load_sem.at[k])

    small = (
        (owner_in, lanes_v.at[0]),
        (level_in, lanes_v.at[1]),
        (row_in, lanes_v.at[2]),
        (azimuth_in, lanes_v.at[3]),
        (spread_in, spread),
        (vertical_in, vertical),
        (east_in, east),
        (north_in, north),
    )

    def fetch(k):
        return pltpu.make_async_copy(small[k][0], small[k][1], load_sem.at[4 + k])

    for k in range(len(small)):
        fetch(k).start()
    for k in range(4):
        load(k).start()
    for f in range(fields):
        fill(f).start()
    owner, level, row, azimuth = (lanes_v.at[k] for k in range(4))

    barrier = pltpu.get_barrier_semaphore()

    for axis, at, n in (("gx", ix, nx), ("gy", iy, ny)):
        for j in range(1, n):
            pl.semaphore_signal(
                barrier, inc=1, device_id={axis: lax.rem(at + j, n)}, device_id_type=MESH
            )

    pl.semaphore_wait(barrier, nx + ny - 2)
    for j in range(1, ny):
        pl.semaphore_signal(
            ready, inc=1, device_id={"gy": lax.rem(iy + j, ny)}, device_id_type=MESH
        )

    def remote(src, dst, sems, sweep, which, f, axis, target):
        return pltpu.make_async_remote_copy(
            src_ref=src,
            dst_ref=dst,
            send_sem=sems.at[0, sweep, which, f],
            recv_sem=sems.at[1, sweep, which, f],
            device_id={axis: target},
            device_id_type=MESH,
        )

    def rim_up(f, sweep):
        return remote(right.at[sweep, f], low.at[sweep, f], rim_sem, sweep, 0, f, "gx", up_x)

    def rim_down(f, sweep):
        return remote(left.at[sweep, f], high.at[sweep, f], rim_sem, sweep, 1, f, "gx", down_x)

    def edge_up(f, sweep):
        if sweep == 0:
            src, dst = control.at[f, :, pl.ds(b - 8, 8)], ext.at[f, :, pl.ds(0, 8)]
        else:
            src, dst = tbuf.at[f, :, pl.ds(b - 8, 8)], halo.at[f, :, pl.ds(0, 8)]
        return remote(src, dst, edge_sem, sweep, 0, f, "gy", up_y)

    def edge_down(f, sweep):
        if sweep == 0:
            src, dst = control.at[f, :, pl.ds(0, 8)], ext.at[f, :, pl.ds(b + 8, 8)]
        else:
            src, dst = tbuf.at[f, :, pl.ds(0, 8)], halo.at[f, :, pl.ds(8, 8)]
        return remote(src, dst, edge_sem, sweep, 1, f, "gy", down_y)

    def start_edges(f, sweep):
        @pl.when(has_up_y)
        def _():
            edge_up(f, sweep).start()

        @pl.when(has_down_y)
        def _():
            edge_down(f, sweep).start()

    def wait_edges(f, sweep):
        @pl.when(has_down_y)
        def _():
            edge_up(f, sweep).wait_recv()

        @pl.when(has_up_y)
        def _():
            edge_down(f, sweep).wait_recv()

    def start_rims(f, sweep):
        @pl.when(has_up_x)
        def _():
            rim_up(f, sweep).start()

        @pl.when(has_down_x)
        def _():
            rim_down(f, sweep).start()

    def wait_rims(f, sweep):
        @pl.when(has_down_x)
        def _():
            rim_up(f, sweep).wait_recv()

        @pl.when(has_up_x)
        def _():
            rim_down(f, sweep).wait_recv()

    kinds = (wind, refl, geo)

    def block(ref, kind, t):
        if kind == 2:
            return ref.at[pl.ds(t, 1)]
        return ref.at[:, pl.ds(pl.multiple_of(t * most, most), most)]

    def landing(kind, t):
        return block((windbuf, reflbuf, geobuf)[kind], kind, t)

    def row_copy(kind, j):
        t = lax.rem(me + j, tiles)
        return pltpu.make_async_remote_copy(
            src_ref=block(kinds[kind], kind, t),
            dst_ref=landing(kind, me),
            send_sem=row_sem.at[0, kind, j],
            recv_sem=row_sem.at[1, kind, j],
            device_id=place(t),
            device_id_type=MESH,
        )

    def row_arrival(kind, j):
        t = lax.rem(me + tiles - j, tiles)
        return pltpu.make_async_remote_copy(
            src_ref=block(kinds[kind], kind, t),
            dst_ref=landing(kind, t),
            send_sem=row_sem.at[0, kind, j],
            recv_sem=row_sem.at[1, kind, j],
            device_id=place(t),
            device_id_type=MESH,
        )

    def own_rows(kind):
        return pltpu.make_async_copy(
            block(kinds[kind], kind, me), landing(kind, me), own_sem.at[kind]
        )

    def start_rows(kind, first=1, last=tiles):
        def one(j, carry):
            row_copy(kind, j).start()
            return carry

        lax.fori_loop(first, last, one, 0)
        if first == 1:
            own_rows(kind).start()

    def wait_rows(kind):
        def one(j, carry):
            row_arrival(kind, j).wait_recv()
            return carry

        lax.fori_loop(1, tiles, one, 0)
        own_rows(kind).wait()

    for f in range(fields):
        start_edges(f, 0)

    for k in range(len(small)):
        fetch(k).wait()

    tile_index = lax.broadcasted_iota(I32, (tiles, 128), 0)
    member = ones_at(tile_index, owner, groups)
    before = jnp.concatenate(
        [
            jnp.where(
                lax.broadcasted_iota(I32, (rows, 128), 0)
                < lax.broadcasted_iota(I32, (rows, 128), 1) + 128 * g,
                1.0,
                0.0,
            ).astype(BF16)
            for g in range(groups)
        ],
        axis=1,
    )
    ahead = jnp.dot(member, before, preferred_element_type=F32)
    ranks = []
    for g in range(groups):
        here = jnp.where(tile_index == owner[pl.ds(g, 1), :], ahead[:, 128 * g : 128 * g + 128], 0.0)
        ranks.append(jnp.sum(here, axis=0, keepdims=True).astype(I32))
        slot_v[pl.ds(g, 1), :] = owner[pl.ds(g, 1), :] * most + ranks[g]
    k_index = lax.broadcasted_iota(I32, (128, 128), 0)
    told = []
    for g in range(groups):
        total = jnp.zeros((128, 128), F32)
        values = (
            level[pl.ds(g, 1), :],
            row[pl.ds(g, 1), :],
            azimuth[pl.ds(g, 1), :] - 180,
        )
        for part, value in enumerate(values):
            total = jnp.where(k_index == ranks[g] + part * most, value.astype(F32), total)
        told.append(total.astype(BF16))
    geo[...] = lax.dot_general(
        member,
        jnp.concatenate(told, axis=1),
        (((1,), (1,)), ((), ())),
        preferred_element_type=F32,
    ).astype(I32)
    pl.semaphore_wait(ready, ny - 1)
    start_rows(2)

    def pack(kind):
        target = kinds[kind]
        for k in range(2):
            one, two = split(rows_v[2 * kind + k])
            rows_rhs[kind, :, k * w : (k + 1) * w] = one
            rows_rhs[kind, :, (2 + k) * w : (3 + k) * w] = two

        def one(i, carry):
            index = lax.broadcasted_iota(I32, (256, 128), 0) + i * 256
            r = jnp.dot(
                ones_at(index, slot_v, groups), rows_rhs[kind], preferred_element_type=F32
            )
            at = pl.ds(pl.multiple_of(i * 256, 256), 256)
            target[0, at, :] = r[:, :w] + r[:, 2 * w : 3 * w]
            target[1, at, :] = r[:, w : 2 * w] + r[:, 3 * w :]
            return carry

        lax.fori_loop(0, slots // 256, one, 0)

    for k in range(4):
        load(k).wait()
    pack(0)

    @pl.when(jnp.logical_not(has_down_x))
    def _():
        low[...] = jnp.zeros_like(low)

    @pl.when(jnp.logical_not(has_up_x))
    def _():
        high[...] = jnp.zeros_like(high)

    @pl.when(jnp.logical_not(has_down_y))
    def _():
        ext[:, :, 0:8] = jnp.zeros((fields, a, 8, w), F32)

    @pl.when(jnp.logical_not(has_up_y))
    def _():
        ext[:, :, b + 8 :] = jnp.zeros((fields, a, 8, w), F32)

    for f in range(fields):
        band_s[f] = north_band(north, f, b, 8)
        inner_s[f] = north_band(north, f, b, 0)
        vert[f] = level_parts(vertical[f])
        vert_back[f] = level_parts(vertical[f].T)
        bands[f, 0] = main_band(east, f)
        bands[f, 1] = rim_band(east, f, 0)
        bands[f, 2] = rim_band(east, f, 8)

    total_square = jnp.zeros((8, w), F32)
    for f in range(fields):
        fill(f).wait()

        def square(i, total):
            v = ext[f, i, pl.ds(8, b), :]
            return total + fold_rows(v * v)

        total_square = lax.fori_loop(0, a, square, total_square)
    parts[0, ix, 0] = total_square

    def forward_north(f, carry):
        wait_edges(f, 0)
        band = band_s[f]

        def one(i, c):
            for j in range(8):
                p = 16 * i + 2 * j
                r = north_times(band, jnp.concatenate([ext[f, p], ext[f, p + 1]], axis=1))
                tbuf[f, p] = r[:, :w]
                tbuf[f, p + 1] = r[:, w:]
            return c

        lax.fori_loop(0, a // 16, one, 0)

        def put_right(g, v):
            right[0, f, g] = v

        def put_left(g, v):
            left[0, f, g] = v

        pack_rims(lambda s: tbuf[f, s], put_right, put_left, a // 16, b)
        start_rims(f, 0)
        return carry

    def forward_east(f, carry):
        wait_rims(f, 0)

        def put(s, v):
            lift[f, pl.ds(pl.multiple_of(s * pitch, 8), b), :] = v

        east_filter(
            lambda s, at, count: tbuf[f, s], low.at[0], high.at[0], put, bands, f, a // 16, ((0, b),)
        )
        v = vert[f]

        def one(p, c):
            for j in range(8):
                y = p * 16 + 2 * j
                x = jnp.concatenate(
                    [lift[f, pl.ds(y, a, stride=pitch), :], lift[f, pl.ds(y + 1, a, stride=pitch), :]],
                    axis=1,
                )
                r = mix_levels(v, x)
                at = pl.multiple_of(y * a, 8)
                state[f, pl.ds(at, a), :] = r[:, :w] * spread[f, pl.ds(y, 1), :]
                at = pl.multiple_of(y * a + a, 8)
                state[f, pl.ds(at, a), :] = r[:, w:] * spread[f, pl.ds(y + 1, 1), :]
            return c

        lax.fori_loop(0, b // 16, one, 0)
        return carry

    forward_north(0, 0)
    forward_north(1, 0)
    start_rows(0)
    pack(1)
    forward_east(0, 0)
    forward_north(2, 0)
    lax.fori_loop(1, fields, forward_east, 0)
    start_rows(1, 1, tiles // 3)

    wait_rows(2)
    per = 128 // most
    lane = lax.broadcasted_iota(I32, (8, 128), 1)

    def label(part):
        total = jnp.zeros((8, 128), I32)
        for q in range(per):
            piece = geobuf[pl.ds(q, 8, stride=per), :]
            shift = ((q - part) * most) % 128
            piece = pltpu.roll(piece, shift, 1) if shift else piece
            total = jnp.where((lane >= q * most) & (lane < (q + 1) * most), piece, total)
        return total

    cell = label(1) * a + label(0)
    angle = (label(2) + 180).astype(F32) * (2.0 * math.pi / 360.0)
    label_v[...] = cell
    to_cells = pltpu.make_async_copy(label_v, cell_s, label_sem.at[0])
    to_cells.start()
    for k, wave in enumerate((jnp.cos(angle), jnp.sin(angle))):
        for g in range(8):
            waves[k, g * 128 : (g + 1) * 128, :] = jnp.broadcast_to(
                wave[g : g + 1], (128, 128)
            ).T
    to_cells.wait()

    def pick(i, carry):
        block_at, first = i // 8, lax.rem(i, 8) * 16
        for j in range(16):
            at = jnp.clip(cell_s[block_at, first + j], 0, a * b - 1)
            for f in range(fields):
                m[f, pl.ds(i * 16 + j, 1), :] = state[f, pl.ds(at, 1), :]
        return carry

    lax.fori_loop(0, slots // 16, pick, 0)

    def mark(i, carry):
        index = lax.broadcasted_iota(I32, (256, 128), 0) + i * 256
        ones_v[pl.ds(pl.multiple_of(i * 256, 256), 256), :] = ones_at(index, label_v, slots // 128)
        return carry

    lax.fori_loop(0, a * b // 256, mark, 0)
    wait_rows(0)
    start_rows(1, tiles // 3, 2 * tiles // 3)

    def weigh_wind(i, total):
        at = pl.ds(pl.multiple_of(i * 16, 16), 16)
        d = waves[0, at, :] * m[0, at, :] + waves[1, at, :] * m[1, at, :] - windbuf[0, at, :]
        v = windbuf[1, at, :] * d
        for j in range(2):
            one, two = split(v * waves[j, at, :])
            rhs[j, at, 0:w] = one
            rhs[j, at, w : 2 * w] = two
        return total + fold_rows(v * d)

    def weigh_refl(i, total):
        at = pl.ds(pl.multiple_of(i * 16, 16), 16)
        d = m[2, at, :] - reflbuf[0, at, :]
        v = reflbuf[1, at, :] * d
        one, two = split(v)
        rhs[2, at, 0:w] = one
        rhs[2, at, w : 2 * w] = two
        return total + fold_rows(v * d)

    def lower(f):
        many = 16
        chunk = many * a
        v = vert_back[f]

        def one(i, carry):
            at = pl.ds(pl.multiple_of(i * chunk, chunk), chunk)
            r = jnp.dot(ones_v[at, :], rhs[f], preferred_element_type=F32)
            grown = r[:, :w] + r[:, w:]
            for j in range(many // 2):
                y = i * many + 2 * j
                x = jnp.concatenate(
                    [grown[2 * j * a : (2 * j + 1) * a], grown[(2 * j + 1) * a : (2 * j + 2) * a]],
                    axis=1,
                )
                t = mix_levels(v, x)
                lift[f, pl.ds(y, a, stride=pitch), :] = t[:, :w] * spread[f, pl.ds(y, 1), :]
                lift[f, pl.ds(y + 1, a, stride=pitch), :] = t[:, w:] * spread[f, pl.ds(y + 1, 1), :]
            return carry

        lax.fori_loop(0, b // many, one, 0)

    def back_rims(f):
        def put_right(g, v):
            right[1, f, g] = v

        def put_left(g, v):
            left[1, f, g] = v

        def get(s):
            return lift[f, pl.ds(pl.multiple_of(s * pitch, 8), b), :]

        pack_rims(get, put_right, put_left, a // 16, b)
        start_rims(f, 1)

    def back_get(f):
        def get(s, at, count):
            return lift[f, pl.ds(pl.multiple_of(s * pitch + at, 8), count), :]

        return get

    def back_edges(f):
        wait_rims(f, 1)

        def put(s, v):
            tbuf[f, s, 0:8, :] = v[0:8]
            tbuf[f, s, b - 8 : b, :] = v[8:16]

        spans = ((0, 8), (b - 8, 8))
        east_filter(back_get(f), low.at[1], high.at[1], put, bands, f, a // 16, spans)
        start_edges(f, 1)

    def back_east(f):
        def put(s, v):
            tbuf[f, s, 8 : b - 8, :] = v

        east_filter(back_get(f), low.at[1], high.at[1], put, bands, f, a // 16, ((8, b - 16),))

    def keep(f):
        return pltpu.make_async_copy(ext.at[f, :, pl.ds(8, b)], near.at[f], put_sem.at[0, f])

    def blank(f, side):
        return pltpu.make_async_copy(
            ext.at[f, :, pl.ds(side * (b + 8), 8)],
            halo.at[f, :, pl.ds(8 * side, 8)],
            put_sem.at[1 + side, f],
        )

    def blanks(act):
        for side, there in ((0, has_down_y), (1, has_up_y)):

            @pl.when(jnp.logical_not(there))
            def _():
                for f in range(fields):
                    act(blank(f, side))

    def back_inner(f, carry):
        band = inner_s[f]

        def one(i, c):
            for j in range(8):
                p = 16 * i + 2 * j
                r = north_times(band, jnp.concatenate([tbuf[f, p], tbuf[f, p + 1]], axis=1))
                at = pl.ds(8, b)
                ext[f, p, at, :] = ext[f, p, at, :] + r[:, :w]
                ext[f, p + 1, at, :] = ext[f, p + 1, at, :] + r[:, w:]
            return c

        lax.fori_loop(0, a // 16, one, 0)
        keep(f).start()
        return carry

    blanks(lambda copy: copy.start())
    observed = lax.fori_loop(0, slots // 16, weigh_wind, jnp.zeros((8, w), F32))

    def each(part, first, last):
        def one(f, carry):
            part(f)
            return carry

        lax.fori_loop(first, last, one, 0)

    def scatter(f):
        lower(f)
        back_rims(f)

    each(scatter, 0, 2)
    start_rows(1, 2 * tiles // 3, tiles)
    each(back_edges, 0, 2)
    wait_rows(1)
    observed = lax.fori_loop(0, slots // 16, weigh_refl, observed)
    parts[0, ix, 1] = observed

    def share(axis, slot, peer, row):
        return pltpu.make_async_remote_copy(
            src_ref=parts.at[row, slot],
            dst_ref=parts.at[row, slot],
            send_sem=sum_sem.at[0, row, peer],
            recv_sem=sum_sem.at[1, row, slot],
            device_id={axis: peer},
            device_id_type=MESH,
        )

    def arrival(axis, peer, row):
        return pltpu.make_async_remote_copy(
            src_ref=parts.at[row, peer],
            dst_ref=parts.at[row, peer],
            send_sem=sum_sem.at[0, row, peer],
            recv_sem=sum_sem.at[1, row, peer],
            device_id={axis: peer},
            device_id_type=MESH,
        )

    for j in range(1, nx):
        share("gx", ix, lax.rem(ix + j, nx), 0).start()
    scatter(2)
    each(back_east, 0, 2)
    back_inner(0, 0)
    for j in range(1, nx):
        arrival("gx", lax.rem(ix + j, nx), 0).wait_recv()
    row_sum = parts[0, 0]
    for j in range(1, nx):
        row_sum = row_sum + parts[0, j]
    parts[1, iy] = row_sum
    for j in range(1, ny):
        share("gy", iy, lax.rem(iy + j, ny), 1).start()
    back_edges(2)
    back_inner(1, 0)
    back_east(2)
    for j in range(1, ny):
        arrival("gy", lax.rem(iy + j, ny), 1).wait_recv()
    all_sum = parts[1, 0]
    for j in range(1, ny):
        all_sum = all_sum + parts[1, j]
    total_v[...] = all_sum
    totals = pltpu.make_async_copy(total_v, total_out, label_sem.at[1])
    totals.start()
    back_inner(2, 0)
    for f in range(fields):
        wait_edges(f, 1)
        keep(f).wait()
    blanks(lambda copy: copy.wait())
    totals.wait()

    for j in range(1, nx):
        share("gx", ix, lax.rem(ix + j, nx), 0).wait_send()
    for j in range(1, ny):
        share("gy", iy, lax.rem(iy + j, ny), 1).wait_send()

    for kind in range(3):

        def sent(j, carry):
            row_copy(kind, j).wait_send()
            return carry

        lax.fori_loop(1, tiles, sent, 0)

    for sweep in range(2):
        for f in range(fields):

            @pl.when(has_up_x)
            def _():
                rim_up(f, sweep).wait_send()

            @pl.when(has_down_x)
            def _():
                rim_down(f, sweep).wait_send()

            @pl.when(has_up_y)
            def _():
                edge_up(f, sweep).wait_send()

            @pl.when(has_down_y)
            def _():
                edge_down(f, sweep).wait_send()


def fused(
    control, inn, wt, owner, level, row, azimuth, spread, vertical, east, north, most
):
    f, a, b, w = control.shape
    nx, ny = lax.axis_size("gx"), lax.axis_size("gy")
    tiles = nx * ny
    slots = tiles * most
    rows = inn.shape[0]
    anywhere = pl.BlockSpec(memory_space=pl.ANY)
    rim = pltpu.VMEM((2, f, a // 16, b, w), F32)
    gates = pltpu.VMEM((2, slots, w), F32)
    told = pltpu.VMEM((tiles, 128), I32)
    dma = pltpu.SemaphoreType.DMA
    return pl.pallas_call(
        functools.partial(fused_kernel, nx, ny, most),
        in_specs=[anywhere] * 11,
        out_specs=(anywhere, anywhere, anywhere),
        out_shape=(
            jax.ShapeDtypeStruct((f, a, b, w), F32),
            jax.ShapeDtypeStruct((f, a, 16, w), F32),
            jax.ShapeDtypeStruct((2, 8, w), F32),
        ),
        scratch_shapes=[
            pltpu.VMEM((4, rows // 128, 128), I32),
            pltpu.VMEM((f, b, w), F32),
            pltpu.VMEM((f, a, a), F32),
            pltpu.VMEM((2, 8, w), F32),
            pltpu.VMEM((f, a, b + 16, w), F32),
            pltpu.VMEM((f, a, b, w), F32),
            pltpu.VMEM((f, a * (b + 8), w), F32),
            pltpu.VMEM((f, a * b, w), F32),
            rim,
            rim,
            rim,
            rim,
            gates,
            gates,
            told,
            gates,
            gates,
            told,
            pltpu.VMEM((4, rows, w), F32),
            pltpu.VMEM((2, rows, 4 * w), BF16),
            pltpu.VMEM((rows // 128, 128), I32),
            pltpu.VMEM((f, b, 3 * (b + 16)), BF16),
            pltpu.VMEM((f, b, 3 * b), BF16),
            pltpu.VMEM((f, 2 * a, 2 * a), BF16),
            pltpu.VMEM((f, 2 * a, 2 * a), BF16),
            pltpu.VMEM((f, 3, 2 * w, 2 * w), BF16),
            pltpu.SMEM(east.shape, F32),
            pltpu.SMEM(north.shape, F32),
            pltpu.VMEM((f, slots, w), F32),
            gates,
            pltpu.VMEM((f, slots, 2 * w), BF16),
            pltpu.VMEM((8, 128), I32),
            pltpu.VMEM((2, max(nx, ny), 2, 8, w), F32),
            pltpu.VMEM((a * b, slots), BF16),
            pltpu.SMEM((8, 128), I32),
            dma((f,)),
            dma((2, 2, 2, f)),
            dma((2, 2, 2, f)),
            dma((2, 3, tiles)),
            dma((3,)),
            dma((2, 2, max(nx, ny))),
            dma((12,)),
            dma((2,)),
            dma((3, f)),
            pltpu.SemaphoreType.REGULAR,
        ],
        compiler_params=pltpu.CompilerParams(
            vmem_limit_bytes=VMEM_BYTES, collective_id=0, has_side_effects=True
        ),
        name="fused",
    )(control, inn, wt, owner, level, row, azimuth, spread, vertical, east, north)


def final_kernel(
    scales, near, halo, totals, north_in, out, cost,
    buf, halo_v, totals_v, north, in_sem, out_sem, halo_sem, total_sem,
):
    fields, a, b, w = out.shape
    parts = in_sem.shape[1]
    zs = a // parts

    def rim(f):
        return pltpu.make_async_copy(halo.at[f], halo_v.at[f], halo_sem.at[f])

    def fetch(f, p):
        at = pl.ds(p * zs, zs)
        return pltpu.make_async_copy(near.at[f, at], buf.at[f, at], in_sem.at[f, p])

    def put(f, p):
        at = pl.ds(p * zs, zs)
        return pltpu.make_async_copy(buf.at[f, at], out.at[f, at], out_sem.at[f, p])

    total = pltpu.make_async_copy(totals, totals_v, total_sem.at[0])
    taps_in = pltpu.make_async_copy(north_in, north, total_sem.at[1])
    taps_in.start()
    for f in range(fields):
        rim(f).start()
        for p in range(parts):
            fetch(f, p).start()
    total.start()
    r = lax.broadcasted_iota(I32, (16, 48), 0)
    c = lax.broadcasted_iota(I32, (16, 48), 1)
    j = c & 15
    distance = jnp.where(r < 8, r + 8 - j, 8 + j - r)
    fits = ((r >> 3) == (j >> 3)) & (distance <= 8)
    taps_in.wait()

    for f in range(fields):
        taps = taps_at(north, f, distance, fits)
        high = taps.astype(BF16).astype(F32)
        band = jnp.where(c >= 32, taps - high, high).astype(BF16)
        rim(f).wait()
        for part in range(parts):
            fetch(f, part).wait()
            for i in range(zs // 8):
                first = part * zs + i * 8
                x = jnp.concatenate([halo_v[f, first + z] for z in range(8)], axis=1)
                t = north_times(band, x)
                for z in range(8):
                    here = t[:, z * w : (z + 1) * w]
                    buf[f, first + z, 0:8] = buf[f, first + z, 0:8] + here[0:8]
                    buf[f, first + z, b - 8 : b] = buf[f, first + z, b - 8 : b] + here[8:16]
            put(f, part).start()
    total.wait()
    for k in range(2):
        cost[k] = jnp.sum(totals_v[k]) * scales[k]
    for f in range(fields):
        for p in range(parts):
            put(f, p).wait()


def final(scales, near, halo, totals, north):
    f, a, b, w = near.shape
    smem = pl.BlockSpec(memory_space=pltpu.SMEM)
    anywhere = pl.BlockSpec(memory_space=pl.ANY)
    return pl.pallas_call(
        functools.partial(final_kernel, scales),
        in_specs=[anywhere] * 4,
        out_specs=(anywhere, smem),
        out_shape=(
            jax.ShapeDtypeStruct(near.shape, F32),
            jax.ShapeDtypeStruct((2,), F32),
        ),
        scratch_shapes=[
            pltpu.VMEM((f, a, b, w), F32),
            pltpu.VMEM((f, a, 16, w), F32),
            pltpu.VMEM(totals.shape, F32),
            pltpu.SMEM(north.shape, F32),
            pltpu.SemaphoreType.DMA((f, 4)),
            pltpu.SemaphoreType.DMA((f, 4)),
            pltpu.SemaphoreType.DMA((f,)),
            pltpu.SemaphoreType.DMA((2,)),
        ],
        compiler_params=pltpu.CompilerParams(vmem_limit_bytes=VMEM_BYTES),
        name="final",
    )(near, halo, totals, north)


def body(
    control, spread, kernel_east, kernel_north, vertical,
    tile_owner, gate_level, tile_row, beam_azimuth, innovation, obs_weight,
):
    tiles = lax.axis_size("gx") * lax.axis_size("gy")
    most = 2 * tile_owner.shape[0] // tiles
    lanes = [x.reshape(-1, 128) for x in (tile_owner, gate_level, tile_row, beam_azimuth)]
    near, halo, totals = fused(
        control, innovation, obs_weight, *lanes, spread, vertical, kernel_east, kernel_north, most
    )
    scales = [0.5 / (control.size * tiles), 0.5 / (innovation.size * tiles)]
    return final(scales, near, halo, totals, kernel_north)


def solution(mesh):
    both = ("gx", "gy")
    placed = (
        P(None, None, "gy", "gx"),
        P(None, "gy", "gx"),
        P(),
        P(),
        P(),
        P(both),
        P(both),
        P(both),
        P(both),
        P(both, None, None),
        P(both, None, None),
    )
    return jax.shard_map(
        body,
        mesh=mesh,
        in_specs=placed,
        out_specs=(P(None, None, "gy", "gx"), P()),
        check_vma=False,
    )
```

```python
import functools
import math

import jax
import jax.numpy as jnp
from jax import lax
from jax.experimental import pallas as pl
from jax.experimental.pallas import tpu as pltpu
from jax.sharding import PartitionSpec as P

F32 = jnp.float32
BF16 = jnp.bfloat16
I32 = jnp.int32
VMEM_BYTES = 58 * 1024 * 1024
MESH = pl.DeviceIdType.MESH


def split(value):
    high = value.astype(BF16)
    low = (value - high.astype(F32)).astype(BF16)
    return high, low


def doubled(weights):
    high, low = split(weights)
    row = jnp.concatenate([high, low], axis=1)
    return jnp.concatenate([row, row], axis=0)


def times(rows, weights):
    high, low = split(rows)
    both = jnp.dot(
        jnp.concatenate([high, low], axis=1), weights, preferred_element_type=F32
    )
    half = both.shape[1] // 2
    return both[:, :half] + both[:, half:]


def taps_at(kernel_ref, f, distance, allowed):
    total = jnp.zeros(distance.shape, F32)
    for d in range(kernel_ref.shape[1]):
        total = jnp.where(distance == d, kernel_ref[f, d], total)
    return jnp.where(allowed, total, 0.0)


def main_band(kernel_ref, f):
    r = lax.broadcasted_iota(I32, (128, 128), 0)
    c = lax.broadcasted_iota(I32, (128, 128), 1)
    return doubled(taps_at(kernel_ref, f, jnp.abs(r - c), jnp.abs(r - c) <= 8))


def rim_band(kernel_ref, f, offset):
    r = (lax.broadcasted_iota(I32, (128, 128), 0) + (128 - offset)) & 127
    c = (lax.broadcasted_iota(I32, (128, 128), 1) + (128 - offset)) & 127
    distance = jnp.abs(r - c)
    fits = ((r >> 4) == (c >> 4)) & ((r & 8) != (c & 8)) & (distance <= 8)
    return doubled(taps_at(kernel_ref, f, distance, fits))


def north_band(kernel_ref, f, ys, rim):
    reach = ys + 2 * rim
    r = lax.broadcasted_iota(I32, (ys, 3 * reach), 0)
    c = lax.broadcasted_iota(I32, (ys, 3 * reach), 1)
    j = jnp.where(c >= reach, c - reach, c)
    j = jnp.where(c >= 2 * reach, c - 2 * reach, j)
    distance = jnp.abs(r + rim - j)
    taps = taps_at(kernel_ref, f, distance, distance <= 8)
    high = taps.astype(BF16).astype(F32)
    return jnp.where(c >= 2 * reach, taps - high, high).astype(BF16)


def north_times(band, x):
    high, low = split(x)
    return jnp.dot(
        band, jnp.concatenate([high, low, high], axis=0), preferred_element_type=F32
    )


def pack_rims(get, put_right, put_left, groups, b):
    lane = lax.broadcasted_iota(I32, (b, 128), 1)
    first = (lane & 8) == 0

    def one(g, carry):
        even = jnp.zeros((b, 128), F32)
        odd = jnp.zeros((b, 128), F32)
        for q in range(8):
            even = jnp.where(
                (lane >> 4) == q, pltpu.roll(get(16 * g + 2 * q), (16 * q + 8) % 128, 1), even
            )
            odd = jnp.where(
                (((lane + 120) & 127) >> 4) == q,
                pltpu.roll(get(16 * g + 2 * q + 1), (16 * q + 16) % 128, 1),
                odd,
            )
        put_right(g, jnp.where(first, even, odd))
        put_left(g, jnp.where(first, odd, even))
        return carry

    lax.fori_loop(0, groups, one, 0)


def east_filter(get, low_ref, high_ref, put, bands, f, groups, spans):
    n = sum(count for _, count in spans)
    lane = lax.broadcasted_iota(I32, (n, 128), 1)
    first = (lane & 8) == 0
    edge = (lane < 8) | (lane >= 120)

    def side(ref, g):
        return jnp.concatenate([ref[f, g, at : at + count, :] for at, count in spans], axis=0)

    def one(g, carry):
        low = side(low_ref, g)
        high = side(high_ref, g)
        even = times(jnp.where(first, low, high), bands[f, 1])
        odd = times(jnp.where(first, high, low), bands[f, 2])
        for part in range(2):
            many = jnp.concatenate(
                [get(16 * g + 8 * part + j, *span) for j in range(8) for span in spans], axis=0
            )
            flat = times(many, bands[f, 0])
            for j in range(4):
                q = 4 * part + j
                at = 16 * g + 2 * q
                own = flat[2 * j * n : (2 * j + 1) * n]
                put(at, own + jnp.where(edge, pltpu.roll(even, (248 - 16 * q) % 128, 1), 0.0))
                own = flat[(2 * j + 1) * n : (2 * j + 2) * n]
                put(at + 1, own + jnp.where(edge, pltpu.roll(odd, (240 - 16 * q) % 128, 1), 0.0))
        return carry

    lax.fori_loop(0, groups, one, 0)


def mix_levels(parts, pair):
    high, low = split(pair)
    both = jnp.dot(parts, jnp.concatenate([high, low], axis=0), preferred_element_type=F32)
    half = both.shape[0] // 2
    return both[:half] + both[half:]


def fold_rows(x):
    return jnp.sum(x.reshape(-1, 8, 128), axis=0)


def ones_at(index, labels, groups):
    return jnp.concatenate(
        [
            jnp.where(index == labels[pl.ds(g, 1), :], 1.0, 0.0).astype(BF16)
            for g in range(groups)
        ],
        axis=1,
    )


def level_parts(v):
    high = v.astype(BF16).astype(F32)
    both = jnp.concatenate([high, v - high], axis=0)
    return jnp.concatenate([both, both], axis=1).astype(BF16)


def fused_kernel(
    nx, ny, most,
    control, inn, wt, owner_in, level_in, row_in, azimuth_in, spread_in, vertical_in, east_in, north_in,
    near, halo, total_out,
    lanes_v, spread, vertical, total_v, ext, tbuf, lift, state, right, left, low, high,
    windbuf, reflbuf, geobuf, wind, refl, geo, rows_v, rows_rhs, slot_v, band_s, inner_s,
    vert, vert_back, bands, east, north,
    m, waves, rhs, label_v, parts, ones_v,
    cell_s,
    fill_sem, rim_sem, edge_sem, row_sem, own_sem, sum_sem, load_sem, label_sem, put_sem, ready,
):
    fields, a, b, w = control.shape
    tiles = nx * ny
    slots = tiles * most
    rows = inn.shape[0]
    groups = rows // 128
    pitch = b + 8
    ix = lax.axis_index("gx")
    iy = lax.axis_index("gy")
    me = ix * ny + iy
    up_x, down_x = jnp.minimum(ix + 1, nx - 1), jnp.maximum(ix - 1, 0)
    up_y, down_y = jnp.minimum(iy + 1, ny - 1), jnp.maximum(iy - 1, 0)
    has_up_x, has_down_x = ix < nx - 1, ix > 0
    has_up_y, has_down_y = iy < ny - 1, iy > 0

    def place(t):
        return {"gx": t // ny, "gy": lax.rem(t, ny)}

    def fill(f):
        return pltpu.make_async_copy(
            control.at[f], ext.at[f, :, pl.ds(8, b)], fill_sem.at[f]
        )

    def load(k):
        src = (inn, wt)[k % 2]
        return pltpu.make_async_copy(src.at[:, k // 2], rows_v.at[k], load_sem.at[k])

    small = (
        (owner_in, lanes_v.at[0]),
        (level_in, lanes_v.at[1]),
        (row_in, lanes_v.at[2]),
        (azimuth_in, lanes_v.at[3]),
        (spread_in, spread),
        (vertical_in, vertical),
        (east_in, east),
        (north_in, north),
    )

    def fetch(k):
        return pltpu.make_async_copy(small[k][0], small[k][1], load_sem.at[4 + k])

    for k in range(len(small)):
        fetch(k).start()
    for k in range(4):
        load(k).start()
    for f in range(fields):
        fill(f).start()
    owner, level, row, azimuth = (lanes_v.at[k] for k in range(4))

    barrier = pltpu.get_barrier_semaphore()

    for axis, at, n in (("gx", ix, nx), ("gy", iy, ny)):
        for j in range(1, n):
            pl.semaphore_signal(
                barrier, inc=1, device_id={axis: lax.rem(at + j, n)}, device_id_type=MESH
            )

    pl.semaphore_wait(barrier, nx + ny - 2)
    for j in range(1, ny):
        pl.semaphore_signal(
            ready, inc=1, device_id={"gy": lax.rem(iy + j, ny)}, device_id_type=MESH
        )

    def remote(src, dst, sems, sweep, which, f, axis, target):
        return pltpu.make_async_remote_copy(
            src_ref=src,
            dst_ref=dst,
            send_sem=sems.at[0, sweep, which, f],
            recv_sem=sems.at[1, sweep, which, f],
            device_id={axis: target},
            device_id_type=MESH,
        )

    def rim_up(f, sweep):
        return remote(right.at[sweep, f], low.at[sweep, f], rim_sem, sweep, 0, f, "gx", up_x)

    def rim_down(f, sweep):
        return remote(left.at[sweep, f], high.at[sweep, f], rim_sem, sweep, 1, f, "gx", down_x)

    def edge_up(f, sweep):
        if sweep == 0:
            src, dst = control.at[f, :, pl.ds(b - 8, 8)], ext.at[f, :, pl.ds(0, 8)]
        else:
            src, dst = tbuf.at[f, :, pl.ds(b - 8, 8)], halo.at[f, :, pl.ds(0, 8)]
        return remote(src, dst, edge_sem, sweep, 0, f, "gy", up_y)

    def edge_down(f, sweep):
        if sweep == 0:
            src, dst = control.at[f, :, pl.ds(0, 8)], ext.at[f, :, pl.ds(b + 8, 8)]
        else:
            src, dst = tbuf.at[f, :, pl.ds(0, 8)], halo.at[f, :, pl.ds(8, 8)]
        return remote(src, dst, edge_sem, sweep, 1, f, "gy", down_y)

    def start_edges(f, sweep):
        @pl.when(has_up_y)
        def _():
            edge_up(f, sweep).start()

        @pl.when(has_down_y)
        def _():
            edge_down(f, sweep).start()

    def wait_edges(f, sweep):
        @pl.when(has_down_y)
        def _():
            edge_up(f, sweep).wait_recv()

        @pl.when(has_up_y)
        def _():
            edge_down(f, sweep).wait_recv()

    def start_rims(f, sweep):
        @pl.when(has_up_x)
        def _():
            rim_up(f, sweep).start()

        @pl.when(has_down_x)
        def _():
            rim_down(f, sweep).start()

    def wait_rims(f, sweep):
        @pl.when(has_down_x)
        def _():
            rim_up(f, sweep).wait_recv()

        @pl.when(has_up_x)
        def _():
            rim_down(f, sweep).wait_recv()

    kinds = (wind, refl, geo)

    def block(ref, kind, t):
        if kind == 2:
            return ref.at[pl.ds(t, 1)]
        return ref.at[:, pl.ds(pl.multiple_of(t * most, most), most)]

    def landing(kind, t):
        return block((windbuf, reflbuf, geobuf)[kind], kind, t)

    def row_copy(kind, j):
        t = lax.rem(me + j, tiles)
        return pltpu.make_async_remote_copy(
            src_ref=block(kinds[kind], kind, t),
            dst_ref=landing(kind, me),
            send_sem=row_sem.at[0, kind, j],
            recv_sem=row_sem.at[1, kind, j],
            device_id=place(t),
            device_id_type=MESH,
        )

    def row_arrival(kind, j):
        t = lax.rem(me + tiles - j, tiles)
        return pltpu.make_async_remote_copy(
            src_ref=block(kinds[kind], kind, t),
            dst_ref=landing(kind, t),
            send_sem=row_sem.at[0, kind, j],
            recv_sem=row_sem.at[1, kind, j],
            device_id=place(t),
            device_id_type=MESH,
        )

    def own_rows(kind):
        return pltpu.make_async_copy(
            block(kinds[kind], kind, me), landing(kind, me), own_sem.at[kind]
        )

    def start_rows(kind, first=1, last=tiles):
        def one(j, carry):
            row_copy(kind, j).start()
            return carry

        lax.fori_loop(first, last, one, 0)
        if first == 1:
            own_rows(kind).start()

    def wait_rows(kind):
        def one(j, carry):
            row_arrival(kind, j).wait_recv()
            return carry

        lax.fori_loop(1, tiles, one, 0)
        own_rows(kind).wait()

    for f in range(fields):
        start_edges(f, 0)

    for k in range(len(small)):
        fetch(k).wait()

    tile_index = lax.broadcasted_iota(I32, (tiles, 128), 0)
    member = ones_at(tile_index, owner, groups)
    before = jnp.concatenate(
        [
            jnp.where(
                lax.broadcasted_iota(I32, (rows, 128), 0)
                < lax.broadcasted_iota(I32, (rows, 128), 1) + 128 * g,
                1.0,
                0.0,
            ).astype(BF16)
            for g in range(groups)
        ],
        axis=1,
    )
    ahead = jnp.dot(member, before, preferred_element_type=F32)
    ranks = []
    for g in range(groups):
        here = jnp.where(tile_index == owner[pl.ds(g, 1), :], ahead[:, 128 * g : 128 * g + 128], 0.0)
        ranks.append(jnp.sum(here, axis=0, keepdims=True).astype(I32))
        slot_v[pl.ds(g, 1), :] = owner[pl.ds(g, 1), :] * most + ranks[g]
    k_index = lax.broadcasted_iota(I32, (128, 128), 0)
    told = []
    for g in range(groups):
        total = jnp.zeros((128, 128), F32)
        values = (
            level[pl.ds(g, 1), :],
            row[pl.ds(g, 1), :],
            azimuth[pl.ds(g, 1), :] - 180,
        )
        for part, value in enumerate(values):
            total = jnp.where(k_index == ranks[g] + part * most, value.astype(F32), total)
        told.append(total.astype(BF16))
    geo[...] = lax.dot_general(
        member,
        jnp.concatenate(told, axis=1),
        (((1,), (1,)), ((), ())),
        preferred_element_type=F32,
    ).astype(I32)
    pl.semaphore_wait(ready, ny - 1)
    start_rows(2)

    def pack(kind):
        target = kinds[kind]
        for k in range(2):
            one, two = split(rows_v[2 * kind + k])
            rows_rhs[kind, :, k * w : (k + 1) * w] = one
            rows_rhs[kind, :, (2 + k) * w : (3 + k) * w] = two

        def one(i, carry):
            index = lax.broadcasted_iota(I32, (256, 128), 0) + i * 256
            r = jnp.dot(
                ones_at(index, slot_v, groups), rows_rhs[kind], preferred_element_type=F32
            )
            at = pl.ds(pl.multiple_of(i * 256, 256), 256)
            target[0, at, :] = r[:, :w] + r[:, 2 * w : 3 * w]
            target[1, at, :] = r[:, w : 2 * w] + r[:, 3 * w :]
            return carry

        lax.fori_loop(0, slots // 256, one, 0)

    for k in range(4):
        load(k).wait()
    pack(0)

    @pl.when(jnp.logical_not(has_down_x))
    def _():
        low[...] = jnp.zeros_like(low)

    @pl.when(jnp.logical_not(has_up_x))
    def _():
        high[...] = jnp.zeros_like(high)

    @pl.when(jnp.logical_not(has_down_y))
    def _():
        ext[:, :, 0:8] = jnp.zeros((fields, a, 8, w), F32)

    @pl.when(jnp.logical_not(has_up_y))
    def _():
        ext[:, :, b + 8 :] = jnp.zeros((fields, a, 8, w), F32)

    for f in range(fields):
        band_s[f] = north_band(north, f, b, 8)
        inner_s[f] = north_band(north, f, b, 0)
        vert[f] = level_parts(vertical[f])
        vert_back[f] = level_parts(vertical[f].T)
        bands[f, 0] = main_band(east, f)
        bands[f, 1] = rim_band(east, f, 0)
        bands[f, 2] = rim_band(east, f, 8)

    total_square = jnp.zeros((8, w), F32)
    for f in range(fields):
        fill(f).wait()

        def square(i, total):
            v = ext[f, i, pl.ds(8, b), :]
            return total + fold_rows(v * v)

        total_square = lax.fori_loop(0, a, square, total_square)
    parts[0, ix, 0] = total_square

    def forward_north(f, carry):
        wait_edges(f, 0)
        band = band_s[f]

        def one(i, c):
            for j in range(8):
                p = 16 * i + 2 * j
                r = north_times(band, jnp.concatenate([ext[f, p], ext[f, p + 1]], axis=1))
                tbuf[f, p] = r[:, :w]
                tbuf[f, p + 1] = r[:, w:]
            return c

        lax.fori_loop(0, a // 16, one, 0)

        def put_right(g, v):
            right[0, f, g] = v

        def put_left(g, v):
            left[0, f, g] = v

        pack_rims(lambda s: tbuf[f, s], put_right, put_left, a // 16, b)
        start_rims(f, 0)
        return carry

    def forward_east(f, carry):
        wait_rims(f, 0)

        def put(s, v):
            lift[f, pl.ds(pl.multiple_of(s * pitch, 8), b), :] = v

        east_filter(
            lambda s, at, count: tbuf[f, s], low.at[0], high.at[0], put, bands, f, a // 16, ((0, b),)
        )
        v = vert[f]

        def one(p, c):
            for j in range(8):
                y = p * 16 + 2 * j
                x = jnp.concatenate(
                    [lift[f, pl.ds(y, a, stride=pitch), :], lift[f, pl.ds(y + 1, a, stride=pitch), :]],
                    axis=1,
                )
                r = mix_levels(v, x)
                at = pl.multiple_of(y * a, 8)
                state[f, pl.ds(at, a), :] = r[:, :w] * spread[f, pl.ds(y, 1), :]
                at = pl.multiple_of(y * a + a, 8)
                state[f, pl.ds(at, a), :] = r[:, w:] * spread[f, pl.ds(y + 1, 1), :]
            return c

        lax.fori_loop(0, b // 16, one, 0)
        return carry

    forward_north(0, 0)
    forward_north(1, 0)
    start_rows(0)
    pack(1)
    forward_east(0, 0)
    forward_north(2, 0)
    lax.fori_loop(1, fields, forward_east, 0)
    start_rows(1, 1, tiles // 3)

    wait_rows(2)
    per = 128 // most
    lane = lax.broadcasted_iota(I32, (8, 128), 1)

    def label(part):
        total = jnp.zeros((8, 128), I32)
        for q in range(per):
            piece = geobuf[pl.ds(q, 8, stride=per), :]
            shift = ((q - part) * most) % 128
            piece = pltpu.roll(piece, shift, 1) if shift else piece
            total = jnp.where((lane >= q * most) & (lane < (q + 1) * most), piece, total)
        return total

    cell = label(1) * a + label(0)
    angle = (label(2) + 180).astype(F32) * (2.0 * math.pi / 360.0)
    label_v[...] = cell
    to_cells = pltpu.make_async_copy(label_v, cell_s, label_sem.at[0])
    to_cells.start()
    for k, wave in enumerate((jnp.cos(angle), jnp.sin(angle))):
        for g in range(8):
            waves[k, g * 128 : (g + 1) * 128, :] = jnp.broadcast_to(
                wave[g : g + 1], (128, 128)
            ).T
    to_cells.wait()

    def pick(i, carry):
        block_at, first = i // 8, lax.rem(i, 8) * 16
        for j in range(16):
            at = jnp.clip(cell_s[block_at, first + j], 0, a * b - 1)
            for f in range(fields):
                m[f, pl.ds(i * 16 + j, 1), :] = state[f, pl.ds(at, 1), :]
        return carry

    lax.fori_loop(0, slots // 16, pick, 0)

    def mark(i, carry):
        index = lax.broadcasted_iota(I32, (256, 128), 0) + i * 256
        ones_v[pl.ds(pl.multiple_of(i * 256, 256), 256), :] = ones_at(index, label_v, slots // 128)
        return carry

    lax.fori_loop(0, a * b // 256, mark, 0)
    wait_rows(0)
    start_rows(1, tiles // 3, 2 * tiles // 3)

    def weigh_wind(i, total):
        at = pl.ds(pl.multiple_of(i * 16, 16), 16)
        d = waves[0, at, :] * m[0, at, :] + waves[1, at, :] * m[1, at, :] - windbuf[0, at, :]
        v = windbuf[1, at, :] * d
        for j in range(2):
            one, two = split(v * waves[j, at, :])
            rhs[j, at, 0:w] = one
            rhs[j, at, w : 2 * w] = two
        return total + fold_rows(v * d)

    def weigh_refl(i, total):
        at = pl.ds(pl.multiple_of(i * 16, 16), 16)
        d = m[2, at, :] - reflbuf[0, at, :]
        v = reflbuf[1, at, :] * d
        one, two = split(v)
        rhs[2, at, 0:w] = one
        rhs[2, at, w : 2 * w] = two
        return total + fold_rows(v * d)

    def lower(f):
        many = 16
        chunk = many * a
        v = vert_back[f]

        def one(i, carry):
            at = pl.ds(pl.multiple_of(i * chunk, chunk), chunk)
            r = jnp.dot(ones_v[at, :], rhs[f], preferred_element_type=F32)
            grown = r[:, :w] + r[:, w:]
            for j in range(many // 2):
                y = i * many + 2 * j
                x = jnp.concatenate(
                    [grown[2 * j * a : (2 * j + 1) * a], grown[(2 * j + 1) * a : (2 * j + 2) * a]],
                    axis=1,
                )
                t = mix_levels(v, x)
                lift[f, pl.ds(y, a, stride=pitch), :] = t[:, :w] * spread[f, pl.ds(y, 1), :]
                lift[f, pl.ds(y + 1, a, stride=pitch), :] = t[:, w:] * spread[f, pl.ds(y + 1, 1), :]
            return carry

        lax.fori_loop(0, b // many, one, 0)

    def back_rims(f):
        def put_right(g, v):
            right[1, f, g] = v

        def put_left(g, v):
            left[1, f, g] = v

        def get(s):
            return lift[f, pl.ds(pl.multiple_of(s * pitch, 8), b), :]

        pack_rims(get, put_right, put_left, a // 16, b)
        start_rims(f, 1)

    def back_get(f):
        def get(s, at, count):
            return lift[f, pl.ds(pl.multiple_of(s * pitch + at, 8), count), :]

        return get

    def back_edges(f):
        wait_rims(f, 1)

        def put(s, v):
            tbuf[f, s, 0:8, :] = v[0:8]
            tbuf[f, s, b - 8 : b, :] = v[8:16]

        spans = ((0, 8), (b - 8, 8))
        east_filter(back_get(f), low.at[1], high.at[1], put, bands, f, a // 16, spans)
        start_edges(f, 1)

    def back_east(f):
        def put(s, v):
            tbuf[f, s, 8 : b - 8, :] = v

        east_filter(back_get(f), low.at[1], high.at[1], put, bands, f, a // 16, ((8, b - 16),))

    def keep(f):
        return pltpu.make_async_copy(ext.at[f, :, pl.ds(8, b)], near.at[f], put_sem.at[0, f])

    def blank(f, side):
        return pltpu.make_async_copy(
            ext.at[f, :, pl.ds(side * (b + 8), 8)],
            halo.at[f, :, pl.ds(8 * side, 8)],
            put_sem.at[1 + side, f],
        )

    def blanks(act):
        for side, there in ((0, has_down_y), (1, has_up_y)):

            @pl.when(jnp.logical_not(there))
            def _():
                for f in range(fields):
                    act(blank(f, side))

    def back_inner(f, carry):
        band = inner_s[f]

        def one(i, c):
            for j in range(8):
                p = 16 * i + 2 * j
                r = north_times(band, jnp.concatenate([tbuf[f, p], tbuf[f, p + 1]], axis=1))
                at = pl.ds(8, b)
                ext[f, p, at, :] = ext[f, p, at, :] + r[:, :w]
                ext[f, p + 1, at, :] = ext[f, p + 1, at, :] + r[:, w:]
            return c

        lax.fori_loop(0, a // 16, one, 0)
        keep(f).start()
        return carry

    blanks(lambda copy: copy.start())
    observed = lax.fori_loop(0, slots // 16, weigh_wind, jnp.zeros((8, w), F32))

    def each(part, first, last):
        def one(f, carry):
            part(f)
            return carry

        lax.fori_loop(first, last, one, 0)

    def scatter(f):
        lower(f)
        back_rims(f)

    def scatter_wind(f):
        scatter(f)

        @pl.when(f == 0)
        def _():
            start_rows(1, 2 * tiles // 3, tiles)

    each(scatter_wind, 0, 2)
    each(back_edges, 0, 2)
    wait_rows(1)
    observed = lax.fori_loop(0, slots // 16, weigh_refl, observed)
    parts[0, ix, 1] = observed

    def share(axis, slot, peer, row):
        return pltpu.make_async_remote_copy(
            src_ref=parts.at[row, slot],
            dst_ref=parts.at[row, slot],
            send_sem=sum_sem.at[0, row, peer],
            recv_sem=sum_sem.at[1, row, slot],
            device_id={axis: peer},
            device_id_type=MESH,
        )

    def arrival(axis, peer, row):
        return pltpu.make_async_remote_copy(
            src_ref=parts.at[row, peer],
            dst_ref=parts.at[row, peer],
            send_sem=sum_sem.at[0, row, peer],
            recv_sem=sum_sem.at[1, row, peer],
            device_id={axis: peer},
            device_id_type=MESH,
        )

    for j in range(1, nx):
        share("gx", ix, lax.rem(ix + j, nx), 0).start()
    scatter(2)
    each(back_east, 0, 2)
    back_inner(0, 0)
    for j in range(1, nx):
        arrival("gx", lax.rem(ix + j, nx), 0).wait_recv()
    row_sum = parts[0, 0]
    for j in range(1, nx):
        row_sum = row_sum + parts[0, j]
    parts[1, iy] = row_sum
    for j in range(1, ny):
        share("gy", iy, lax.rem(iy + j, ny), 1).start()
    back_edges(2)
    back_inner(1, 0)
    back_east(2)
    for j in range(1, ny):
        arrival("gy", lax.rem(iy + j, ny), 1).wait_recv()
    all_sum = parts[1, 0]
    for j in range(1, ny):
        all_sum = all_sum + parts[1, j]
    total_v[...] = all_sum
    totals = pltpu.make_async_copy(total_v, total_out, label_sem.at[1])
    totals.start()
    back_inner(2, 0)
    for f in range(fields):
        wait_edges(f, 1)
        keep(f).wait()
    blanks(lambda copy: copy.wait())
    totals.wait()

    for j in range(1, nx):
        share("gx", ix, lax.rem(ix + j, nx), 0).wait_send()
    for j in range(1, ny):
        share("gy", iy, lax.rem(iy + j, ny), 1).wait_send()

    for kind in range(3):

        def sent(j, carry):
            row_copy(kind, j).wait_send()
            return carry

        lax.fori_loop(1, tiles, sent, 0)

    for sweep in range(2):
        for f in range(fields):

            @pl.when(has_up_x)
            def _():
                rim_up(f, sweep).wait_send()

            @pl.when(has_down_x)
            def _():
                rim_down(f, sweep).wait_send()

            @pl.when(has_up_y)
            def _():
                edge_up(f, sweep).wait_send()

            @pl.when(has_down_y)
            def _():
                edge_down(f, sweep).wait_send()


def fused(
    control, inn, wt, owner, level, row, azimuth, spread, vertical, east, north, most
):
    f, a, b, w = control.shape
    nx, ny = lax.axis_size("gx"), lax.axis_size("gy")
    tiles = nx * ny
    slots = tiles * most
    rows = inn.shape[0]
    anywhere = pl.BlockSpec(memory_space=pl.ANY)
    rim = pltpu.VMEM((2, f, a // 16, b, w), F32)
    gates = pltpu.VMEM((2, slots, w), F32)
    told = pltpu.VMEM((tiles, 128), I32)
    dma = pltpu.SemaphoreType.DMA
    return pl.pallas_call(
        functools.partial(fused_kernel, nx, ny, most),
        in_specs=[anywhere] * 11,
        out_specs=(anywhere, anywhere, anywhere),
        out_shape=(
            jax.ShapeDtypeStruct((f, a, b, w), F32),
            jax.ShapeDtypeStruct((f, a, 16, w), F32),
            jax.ShapeDtypeStruct((2, 8, w), F32),
        ),
        scratch_shapes=[
            pltpu.VMEM((4, rows // 128, 128), I32),
            pltpu.VMEM((f, b, w), F32),
            pltpu.VMEM((f, a, a), F32),
            pltpu.VMEM((2, 8, w), F32),
            pltpu.VMEM((f, a, b + 16, w), F32),
            pltpu.VMEM((f, a, b, w), F32),
            pltpu.VMEM((f, a * (b + 8), w), F32),
            pltpu.VMEM((f, a * b, w), F32),
            rim,
            rim,
            rim,
            rim,
            gates,
            gates,
            told,
            gates,
            gates,
            told,
            pltpu.VMEM((4, rows, w), F32),
            pltpu.VMEM((2, rows, 4 * w), BF16),
            pltpu.VMEM((rows // 128, 128), I32),
            pltpu.VMEM((f, b, 3 * (b + 16)), BF16),
            pltpu.VMEM((f, b, 3 * b), BF16),
            pltpu.VMEM((f, 2 * a, 2 * a), BF16),
            pltpu.VMEM((f, 2 * a, 2 * a), BF16),
            pltpu.VMEM((f, 3, 2 * w, 2 * w), BF16),
            pltpu.SMEM(east.shape, F32),
            pltpu.SMEM(north.shape, F32),
            pltpu.VMEM((f, slots, w), F32),
            gates,
            pltpu.VMEM((f, slots, 2 * w), BF16),
            pltpu.VMEM((8, 128), I32),
            pltpu.VMEM((2, max(nx, ny), 2, 8, w), F32),
            pltpu.VMEM((a * b, slots), BF16),
            pltpu.SMEM((8, 128), I32),
            dma((f,)),
            dma((2, 2, 2, f)),
            dma((2, 2, 2, f)),
            dma((2, 3, tiles)),
            dma((3,)),
            dma((2, 2, max(nx, ny))),
            dma((12,)),
            dma((2,)),
            dma((3, f)),
            pltpu.SemaphoreType.REGULAR,
        ],
        compiler_params=pltpu.CompilerParams(
            vmem_limit_bytes=VMEM_BYTES, collective_id=0, has_side_effects=True
        ),
        name="fused",
    )(control, inn, wt, owner, level, row, azimuth, spread, vertical, east, north)


def final_kernel(
    scales, near, halo, totals, north_in, out, cost,
    buf, halo_v, totals_v, north, in_sem, out_sem, halo_sem, total_sem,
):
    fields, a, b, w = out.shape
    parts = in_sem.shape[1]
    zs = a // parts

    def rim(f):
        return pltpu.make_async_copy(halo.at[f], halo_v.at[f], halo_sem.at[f])

    def fetch(f, p):
        at = pl.ds(p * zs, zs)
        return pltpu.make_async_copy(near.at[f, at], buf.at[f, at], in_sem.at[f, p])

    def put(f, p):
        at = pl.ds(p * zs, zs)
        return pltpu.make_async_copy(buf.at[f, at], out.at[f, at], out_sem.at[f, p])

    total = pltpu.make_async_copy(totals, totals_v, total_sem.at[0])
    taps_in = pltpu.make_async_copy(north_in, north, total_sem.at[1])
    taps_in.start()
    for f in range(fields):
        rim(f).start()
        for p in range(parts):
            fetch(f, p).start()
    total.start()
    r = lax.broadcasted_iota(I32, (16, 48), 0)
    c = lax.broadcasted_iota(I32, (16, 48), 1)
    j = c & 15
    distance = jnp.where(r < 8, r + 8 - j, 8 + j - r)
    fits = ((r >> 3) == (j >> 3)) & (distance <= 8)
    taps_in.wait()

    for f in range(fields):
        taps = taps_at(north, f, distance, fits)
        high = taps.astype(BF16).astype(F32)
        band = jnp.where(c >= 32, taps - high, high).astype(BF16)
        rim(f).wait()
        for part in range(parts):
            fetch(f, part).wait()
            for i in range(zs // 8):
                first = part * zs + i * 8
                x = jnp.concatenate([halo_v[f, first + z] for z in range(8)], axis=1)
                t = north_times(band, x)
                for z in range(8):
                    here = t[:, z * w : (z + 1) * w]
                    buf[f, first + z, 0:8] = buf[f, first + z, 0:8] + here[0:8]
                    buf[f, first + z, b - 8 : b] = buf[f, first + z, b - 8 : b] + here[8:16]
            put(f, part).start()
    total.wait()
    for k in range(2):
        cost[k] = jnp.sum(totals_v[k]) * scales[k]
    for f in range(fields):
        for p in range(parts):
            put(f, p).wait()


def final(scales, near, halo, totals, north):
    f, a, b, w = near.shape
    smem = pl.BlockSpec(memory_space=pltpu.SMEM)
    anywhere = pl.BlockSpec(memory_space=pl.ANY)
    return pl.pallas_call(
        functools.partial(final_kernel, scales),
        in_specs=[anywhere] * 4,
        out_specs=(anywhere, smem),
        out_shape=(
            jax.ShapeDtypeStruct(near.shape, F32),
            jax.ShapeDtypeStruct((2,), F32),
        ),
        scratch_shapes=[
            pltpu.VMEM((f, a, b, w), F32),
            pltpu.VMEM((f, a, 16, w), F32),
            pltpu.VMEM(totals.shape, F32),
            pltpu.SMEM(north.shape, F32),
            pltpu.SemaphoreType.DMA((f, 2)),
            pltpu.SemaphoreType.DMA((f, 2)),
            pltpu.SemaphoreType.DMA((f,)),
            pltpu.SemaphoreType.DMA((2,)),
        ],
        compiler_params=pltpu.CompilerParams(vmem_limit_bytes=VMEM_BYTES),
        name="final",
    )(near, halo, totals, north)


def body(
    control, spread, kernel_east, kernel_north, vertical,
    tile_owner, gate_level, tile_row, beam_azimuth, innovation, obs_weight,
):
    tiles = lax.axis_size("gx") * lax.axis_size("gy")
    most = 2 * tile_owner.shape[0] // tiles
    lanes = [x.reshape(-1, 128) for x in (tile_owner, gate_level, tile_row, beam_azimuth)]
    near, halo, totals = fused(
        control, innovation, obs_weight, *lanes, spread, vertical, kernel_east, kernel_north, most
    )
    scales = [0.5 / (control.size * tiles), 0.5 / (innovation.size * tiles)]
    return final(scales, near, halo, totals, kernel_north)


def solution(mesh):
    both = ("gx", "gy")
    placed = (
        P(None, None, "gy", "gx"),
        P(None, "gy", "gx"),
        P(),
        P(),
        P(),
        P(both),
        P(both),
        P(both),
        P(both),
        P(both, None, None),
        P(both, None, None),
    )
    return jax.shard_map(
        body,
        mesh=mesh,
        in_specs=placed,
        out_specs=(P(None, None, "gy", "gx"), P()),
        check_vma=False,
    )
```

```python
import functools
import math

import jax
import jax.numpy as jnp
from jax import lax
from jax.experimental import pallas as pl
from jax.experimental.pallas import tpu as pltpu
from jax.sharding import PartitionSpec as P

F32 = jnp.float32
BF16 = jnp.bfloat16
I32 = jnp.int32
VMEM_BYTES = 58 * 1024 * 1024
MESH = pl.DeviceIdType.MESH


def split(value):
    high = value.astype(BF16)
    low = (value - high.astype(F32)).astype(BF16)
    return high, low


def doubled(weights):
    high, low = split(weights)
    row = jnp.concatenate([high, low], axis=1)
    return jnp.concatenate([row, row], axis=0)


def times(rows, weights):
    high, low = split(rows)
    both = jnp.dot(
        jnp.concatenate([high, low], axis=1), weights, preferred_element_type=F32
    )
    half = both.shape[1] // 2
    return both[:, :half] + both[:, half:]


def taps_at(kernel_ref, f, distance, allowed):
    total = jnp.zeros(distance.shape, F32)
    for d in range(kernel_ref.shape[1]):
        total = jnp.where(distance == d, kernel_ref[f, d], total)
    return jnp.where(allowed, total, 0.0)


def main_band(kernel_ref, f):
    r = lax.broadcasted_iota(I32, (128, 128), 0)
    c = lax.broadcasted_iota(I32, (128, 128), 1)
    return doubled(taps_at(kernel_ref, f, jnp.abs(r - c), jnp.abs(r - c) <= 8))


def rim_band(kernel_ref, f, offset):
    r = (lax.broadcasted_iota(I32, (128, 128), 0) + (128 - offset)) & 127
    c = (lax.broadcasted_iota(I32, (128, 128), 1) + (128 - offset)) & 127
    distance = jnp.abs(r - c)
    fits = ((r >> 4) == (c >> 4)) & ((r & 8) != (c & 8)) & (distance <= 8)
    return doubled(taps_at(kernel_ref, f, distance, fits))


def north_band(kernel_ref, f, ys, rim):
    reach = ys + 2 * rim
    r = lax.broadcasted_iota(I32, (ys, 3 * reach), 0)
    c = lax.broadcasted_iota(I32, (ys, 3 * reach), 1)
    j = jnp.where(c >= reach, c - reach, c)
    j = jnp.where(c >= 2 * reach, c - 2 * reach, j)
    distance = jnp.abs(r + rim - j)
    taps = taps_at(kernel_ref, f, distance, distance <= 8)
    high = taps.astype(BF16).astype(F32)
    return jnp.where(c >= 2 * reach, taps - high, high).astype(BF16)


def north_times(band, x):
    high, low = split(x)
    return jnp.dot(
        band, jnp.concatenate([high, low, high], axis=0), preferred_element_type=F32
    )


def pack_rims(get, put_right, put_left, groups, b):
    lane = lax.broadcasted_iota(I32, (b, 128), 1)
    first = (lane & 8) == 0

    def one(g, carry):
        even = jnp.zeros((b, 128), F32)
        odd = jnp.zeros((b, 128), F32)
        for q in range(8):
            even = jnp.where(
                (lane >> 4) == q, pltpu.roll(get(16 * g + 2 * q), (16 * q + 8) % 128, 1), even
            )
            odd = jnp.where(
                (((lane + 120) & 127) >> 4) == q,
                pltpu.roll(get(16 * g + 2 * q + 1), (16 * q + 16) % 128, 1),
                odd,
            )
        put_right(g, jnp.where(first, even, odd))
        put_left(g, jnp.where(first, odd, even))
        return carry

    lax.fori_loop(0, groups, one, 0)


def east_filter(get, low_ref, high_ref, put, bands, f, groups, spans):
    n = sum(count for _, count in spans)
    lane = lax.broadcasted_iota(I32, (n, 128), 1)
    first = (lane & 8) == 0
    edge = (lane < 8) | (lane >= 120)

    def side(ref, g):
        return jnp.concatenate([ref[f, g, at : at + count, :] for at, count in spans], axis=0)

    def one(g, carry):
        low = side(low_ref, g)
        high = side(high_ref, g)
        even = times(jnp.where(first, low, high), bands[f, 1])
        odd = times(jnp.where(first, high, low), bands[f, 2])
        for part in range(2):
            many = jnp.concatenate(
                [get(16 * g + 8 * part + j, *span) for j in range(8) for span in spans], axis=0
            )
            flat = times(many, bands[f, 0])
            for j in range(4):
                q = 4 * part + j
                at = 16 * g + 2 * q
                own = flat[2 * j * n : (2 * j + 1) * n]
                put(at, own + jnp.where(edge, pltpu.roll(even, (248 - 16 * q) % 128, 1), 0.0))
                own = flat[(2 * j + 1) * n : (2 * j + 2) * n]
                put(at + 1, own + jnp.where(edge, pltpu.roll(odd, (240 - 16 * q) % 128, 1), 0.0))
        return carry

    lax.fori_loop(0, groups, one, 0)


def mix_levels(parts, pair):
    high, low = split(pair)
    both = jnp.dot(parts, jnp.concatenate([high, low], axis=0), preferred_element_type=F32)
    half = both.shape[0] // 2
    return both[:half] + both[half:]


def fold_rows(x):
    return jnp.sum(x.reshape(-1, 8, 128), axis=0)


def ones_at(index, labels, groups):
    return jnp.concatenate(
        [
            jnp.where(index == labels[pl.ds(g, 1), :], 1.0, 0.0).astype(BF16)
            for g in range(groups)
        ],
        axis=1,
    )


def level_parts(v):
    high = v.astype(BF16).astype(F32)
    both = jnp.concatenate([high, v - high], axis=0)
    return jnp.concatenate([both, both], axis=1).astype(BF16)


def fused_kernel(
    nx, ny, most,
    control, inn, wt, owner_in, level_in, row_in, azimuth_in, spread_in, vertical_in, east_in, north_in,
    near, halo, total_out,
    lanes_v, spread, vertical, total_v, ext, tbuf, lift, state, right, left, low, high,
    windbuf, reflbuf, geobuf, wind, refl, geo, rows_v, rows_rhs, slot_v, band_s, inner_s,
    vert, vert_back, bands, east, north,
    m, waves, rhs, label_v, parts, ones_v,
    cell_s,
    fill_sem, rim_sem, edge_sem, row_sem, own_sem, sum_sem, load_sem, label_sem, put_sem, ready,
):
    fields, a, b, w = control.shape
    tiles = nx * ny
    slots = tiles * most
    rows = inn.shape[0]
    groups = rows // 128
    pitch = b + 8
    ix = lax.axis_index("gx")
    iy = lax.axis_index("gy")
    me = ix * ny + iy
    up_x, down_x = jnp.minimum(ix + 1, nx - 1), jnp.maximum(ix - 1, 0)
    up_y, down_y = jnp.minimum(iy + 1, ny - 1), jnp.maximum(iy - 1, 0)
    has_up_x, has_down_x = ix < nx - 1, ix > 0
    has_up_y, has_down_y = iy < ny - 1, iy > 0

    def place(t):
        return {"gx": t // ny, "gy": lax.rem(t, ny)}

    def fill(f):
        return pltpu.make_async_copy(
            control.at[f], ext.at[f, :, pl.ds(8, b)], fill_sem.at[f]
        )

    def load(k):
        src = (inn, wt)[k % 2]
        return pltpu.make_async_copy(src.at[:, k // 2], rows_v.at[k], load_sem.at[k])

    small = (
        (owner_in, lanes_v.at[0]),
        (level_in, lanes_v.at[1]),
        (row_in, lanes_v.at[2]),
        (azimuth_in, lanes_v.at[3]),
        (spread_in, spread),
        (vertical_in, vertical),
        (east_in, east),
        (north_in, north),
    )

    def fetch(k):
        return pltpu.make_async_copy(small[k][0], small[k][1], load_sem.at[4 + k])

    for k in range(len(small)):
        fetch(k).start()
    for k in range(4):
        load(k).start()
    for f in range(fields):
        fill(f).start()
    owner, level, row, azimuth = (lanes_v.at[k] for k in range(4))

    barrier = pltpu.get_barrier_semaphore()

    for axis, at, n in (("gx", ix, nx), ("gy", iy, ny)):
        for j in range(1, n):
            pl.semaphore_signal(
                barrier, inc=1, device_id={axis: lax.rem(at + j, n)}, device_id_type=MESH
            )

    pl.semaphore_wait(barrier, nx + ny - 2)
    for j in range(1, ny):
        pl.semaphore_signal(
            ready, inc=1, device_id={"gy": lax.rem(iy + j, ny)}, device_id_type=MESH
        )

    def remote(src, dst, sems, sweep, which, f, axis, target):
        return pltpu.make_async_remote_copy(
            src_ref=src,
            dst_ref=dst,
            send_sem=sems.at[0, sweep, which, f],
            recv_sem=sems.at[1, sweep, which, f],
            device_id={axis: target},
            device_id_type=MESH,
        )

    def rim_up(f, sweep):
        return remote(right.at[sweep, f], low.at[sweep, f], rim_sem, sweep, 0, f, "gx", up_x)

    def rim_down(f, sweep):
        return remote(left.at[sweep, f], high.at[sweep, f], rim_sem, sweep, 1, f, "gx", down_x)

    def edge_up(f, sweep):
        if sweep == 0:
            src, dst = control.at[f, :, pl.ds(b - 8, 8)], ext.at[f, :, pl.ds(0, 8)]
        else:
            src, dst = tbuf.at[f, :, pl.ds(b - 8, 8)], halo.at[f, :, pl.ds(0, 8)]
        return remote(src, dst, edge_sem, sweep, 0, f, "gy", up_y)

    def edge_down(f, sweep):
        if sweep == 0:
            src, dst = control.at[f, :, pl.ds(0, 8)], ext.at[f, :, pl.ds(b + 8, 8)]
        else:
            src, dst = tbuf.at[f, :, pl.ds(0, 8)], halo.at[f, :, pl.ds(8, 8)]
        return remote(src, dst, edge_sem, sweep, 1, f, "gy", down_y)

    def start_edges(f, sweep):
        @pl.when(has_up_y)
        def _():
            edge_up(f, sweep).start()

        @pl.when(has_down_y)
        def _():
            edge_down(f, sweep).start()

    def wait_edges(f, sweep):
        @pl.when(has_down_y)
        def _():
            edge_up(f, sweep).wait_recv()

        @pl.when(has_up_y)
        def _():
            edge_down(f, sweep).wait_recv()

    def start_rims(f, sweep):
        @pl.when(has_up_x)
        def _():
            rim_up(f, sweep).start()

        @pl.when(has_down_x)
        def _():
            rim_down(f, sweep).start()

    def wait_rims(f, sweep):
        @pl.when(has_down_x)
        def _():
            rim_up(f, sweep).wait_recv()

        @pl.when(has_up_x)
        def _():
            rim_down(f, sweep).wait_recv()

    kinds = (wind, refl, geo)

    def block(ref, kind, t):
        if kind == 2:
            return ref.at[pl.ds(t, 1)]
        return ref.at[:, pl.ds(pl.multiple_of(t * most, most), most)]

    def landing(kind, t):
        return block((windbuf, reflbuf, geobuf)[kind], kind, t)

    def row_copy(kind, j):
        t = lax.rem(me + j, tiles)
        return pltpu.make_async_remote_copy(
            src_ref=block(kinds[kind], kind, t),
            dst_ref=landing(kind, me),
            send_sem=row_sem.at[0, kind, j],
            recv_sem=row_sem.at[1, kind, j],
            device_id=place(t),
            device_id_type=MESH,
        )

    def row_arrival(kind, j):
        t = lax.rem(me + tiles - j, tiles)
        return pltpu.make_async_remote_copy(
            src_ref=block(kinds[kind], kind, t),
            dst_ref=landing(kind, t),
            send_sem=row_sem.at[0, kind, j],
            recv_sem=row_sem.at[1, kind, j],
            device_id=place(t),
            device_id_type=MESH,
        )

    def own_rows(kind):
        return pltpu.make_async_copy(
            block(kinds[kind], kind, me), landing(kind, me), own_sem.at[kind]
        )

    def start_rows(kind, first=1, last=tiles):
        def one(j, carry):
            row_copy(kind, j).start()
            return carry

        lax.fori_loop(first, last, one, 0)
        if first == 1:
            own_rows(kind).start()

    def wait_rows(kind):
        def one(j, carry):
            row_arrival(kind, j).wait_recv()
            return carry

        lax.fori_loop(1, tiles, one, 0)
        own_rows(kind).wait()

    for f in range(fields):
        start_edges(f, 0)

    for k in range(len(small)):
        fetch(k).wait()

    tile_index = lax.broadcasted_iota(I32, (tiles, 128), 0)
    member = ones_at(tile_index, owner, groups)
    before = jnp.concatenate(
        [
            jnp.where(
                lax.broadcasted_iota(I32, (rows, 128), 0)
                < lax.broadcasted_iota(I32, (rows, 128), 1) + 128 * g,
                1.0,
                0.0,
            ).astype(BF16)
            for g in range(groups)
        ],
        axis=1,
    )
    ahead = jnp.dot(member, before, preferred_element_type=F32)
    ranks = []
    for g in range(groups):
        here = jnp.where(tile_index == owner[pl.ds(g, 1), :], ahead[:, 128 * g : 128 * g + 128], 0.0)
        ranks.append(jnp.sum(here, axis=0, keepdims=True).astype(I32))
        slot_v[pl.ds(g, 1), :] = owner[pl.ds(g, 1), :] * most + ranks[g]
    k_index = lax.broadcasted_iota(I32, (128, 128), 0)
    told = []
    for g in range(groups):
        total = jnp.zeros((128, 128), F32)
        values = (
            level[pl.ds(g, 1), :],
            row[pl.ds(g, 1), :],
            azimuth[pl.ds(g, 1), :] - 180,
        )
        for part, value in enumerate(values):
            total = jnp.where(k_index == ranks[g] + part * most, value.astype(F32), total)
        told.append(total.astype(BF16))
    geo[...] = lax.dot_general(
        member,
        jnp.concatenate(told, axis=1),
        (((1,), (1,)), ((), ())),
        preferred_element_type=F32,
    ).astype(I32)
    pl.semaphore_wait(ready, ny - 1)
    start_rows(2)

    def pack(kind):
        target = kinds[kind]
        for k in range(2):
            one, two = split(rows_v[2 * kind + k])
            rows_rhs[kind, :, k * w : (k + 1) * w] = one
            rows_rhs[kind, :, (2 + k) * w : (3 + k) * w] = two

        def one(i, carry):
            index = lax.broadcasted_iota(I32, (256, 128), 0) + i * 256
            r = jnp.dot(
                ones_at(index, slot_v, groups), rows_rhs[kind], preferred_element_type=F32
            )
            at = pl.ds(pl.multiple_of(i * 256, 256), 256)
            target[0, at, :] = r[:, :w] + r[:, 2 * w : 3 * w]
            target[1, at, :] = r[:, w : 2 * w] + r[:, 3 * w :]
            return carry

        lax.fori_loop(0, slots // 256, one, 0)

    for k in range(4):
        load(k).wait()
    pack(0)

    @pl.when(jnp.logical_not(has_down_x))
    def _():
        low[...] = jnp.zeros_like(low)

    @pl.when(jnp.logical_not(has_up_x))
    def _():
        high[...] = jnp.zeros_like(high)

    @pl.when(jnp.logical_not(has_down_y))
    def _():
        ext[:, :, 0:8] = jnp.zeros((fields, a, 8, w), F32)

    @pl.when(jnp.logical_not(has_up_y))
    def _():
        ext[:, :, b + 8 :] = jnp.zeros((fields, a, 8, w), F32)

    for f in range(fields):
        band_s[f] = north_band(north, f, b, 8)
        inner_s[f] = north_band(north, f, b, 0)
        vert[f] = level_parts(vertical[f])
        vert_back[f] = level_parts(vertical[f].T)
        bands[f, 0] = main_band(east, f)
        bands[f, 1] = rim_band(east, f, 0)
        bands[f, 2] = rim_band(east, f, 8)

    total_square = jnp.zeros((8, w), F32)
    for f in range(fields):
        fill(f).wait()

        def square(i, total):
            v = ext[f, i, pl.ds(8, b), :]
            return total + fold_rows(v * v)

        total_square = lax.fori_loop(0, a, square, total_square)
    parts[0, ix, 0] = total_square

    def forward_north(f, carry):
        wait_edges(f, 0)
        band = band_s[f]

        def one(i, c):
            for j in range(8):
                p = 16 * i + 2 * j
                r = north_times(band, jnp.concatenate([ext[f, p], ext[f, p + 1]], axis=1))
                tbuf[f, p] = r[:, :w]
                tbuf[f, p + 1] = r[:, w:]
            return c

        lax.fori_loop(0, a // 16, one, 0)

        def put_right(g, v):
            right[0, f, g] = v

        def put_left(g, v):
            left[0, f, g] = v

        pack_rims(lambda s: tbuf[f, s], put_right, put_left, a // 16, b)
        start_rims(f, 0)
        return carry

    def forward_east(f, carry):
        wait_rims(f, 0)

        def put(s, v):
            lift[f, pl.ds(pl.multiple_of(s * pitch, 8), b), :] = v

        east_filter(
            lambda s, at, count: tbuf[f, s], low.at[0], high.at[0], put, bands, f, a // 16, ((0, b),)
        )
        v = vert[f]

        def one(p, c):
            for j in range(8):
                y = p * 16 + 2 * j
                x = jnp.concatenate(
                    [lift[f, pl.ds(y, a, stride=pitch), :], lift[f, pl.ds(y + 1, a, stride=pitch), :]],
                    axis=1,
                )
                r = mix_levels(v, x)
                at = pl.multiple_of(y * a, 8)
                state[f, pl.ds(at, a), :] = r[:, :w] * spread[f, pl.ds(y, 1), :]
                at = pl.multiple_of(y * a + a, 8)
                state[f, pl.ds(at, a), :] = r[:, w:] * spread[f, pl.ds(y + 1, 1), :]
            return c

        lax.fori_loop(0, b // 16, one, 0)
        return carry

    forward_north(0, 0)
    forward_north(1, 0)
    start_rows(0)
    pack(1)
    forward_east(0, 0)
    forward_north(2, 0)
    lax.fori_loop(1, fields, forward_east, 0)
    start_rows(1, 1, tiles // 3)

    wait_rows(2)
    per = 128 // most
    lane = lax.broadcasted_iota(I32, (8, 128), 1)

    def label(part):
        total = jnp.zeros((8, 128), I32)
        for q in range(per):
            piece = geobuf[pl.ds(q, 8, stride=per), :]
            shift = ((q - part) * most) % 128
            piece = pltpu.roll(piece, shift, 1) if shift else piece
            total = jnp.where((lane >= q * most) & (lane < (q + 1) * most), piece, total)
        return total

    cell = label(1) * a + label(0)
    angle = (label(2) + 180).astype(F32) * (2.0 * math.pi / 360.0)
    label_v[...] = cell
    to_cells = pltpu.make_async_copy(label_v, cell_s, label_sem.at[0])
    to_cells.start()
    for k, wave in enumerate((jnp.cos(angle), jnp.sin(angle))):
        for g in range(8):
            waves[k, g * 128 : (g + 1) * 128, :] = jnp.broadcast_to(
                wave[g : g + 1], (128, 128)
            ).T
    to_cells.wait()

    def pick(i, carry):
        block_at, first = i // 8, lax.rem(i, 8) * 16
        for j in range(16):
            at = jnp.clip(cell_s[block_at, first + j], 0, a * b - 1)
            for f in range(fields):
                m[f, pl.ds(i * 16 + j, 1), :] = state[f, pl.ds(at, 1), :]
        return carry

    lax.fori_loop(0, slots // 16, pick, 0)

    def mark(i, carry):
        index = lax.broadcasted_iota(I32, (256, 128), 0) + i * 256
        ones_v[pl.ds(pl.multiple_of(i * 256, 256), 256), :] = ones_at(index, label_v, slots // 128)
        return carry

    lax.fori_loop(0, a * b // 256, mark, 0)
    wait_rows(0)
    start_rows(1, tiles // 3, 2 * tiles // 3)

    def weigh_wind(i, total):
        at = pl.ds(pl.multiple_of(i * 16, 16), 16)
        d = waves[0, at, :] * m[0, at, :] + waves[1, at, :] * m[1, at, :] - windbuf[0, at, :]
        v = windbuf[1, at, :] * d
        for j in range(2):
            one, two = split(v * waves[j, at, :])
            rhs[j, at, 0:w] = one
            rhs[j, at, w : 2 * w] = two
        return total + fold_rows(v * d)

    def weigh_refl(i, total):
        at = pl.ds(pl.multiple_of(i * 16, 16), 16)
        d = m[2, at, :] - reflbuf[0, at, :]
        v = reflbuf[1, at, :] * d
        one, two = split(v)
        rhs[2, at, 0:w] = one
        rhs[2, at, w : 2 * w] = two
        return total + fold_rows(v * d)

    def lower(f):
        many = 16
        chunk = many * a
        v = vert_back[f]

        def one(i, carry):
            at = pl.ds(pl.multiple_of(i * chunk, chunk), chunk)
            r = jnp.dot(ones_v[at, :], rhs[f], preferred_element_type=F32)
            grown = r[:, :w] + r[:, w:]
            for j in range(many // 2):
                y = i * many + 2 * j
                x = jnp.concatenate(
                    [grown[2 * j * a : (2 * j + 1) * a], grown[(2 * j + 1) * a : (2 * j + 2) * a]],
                    axis=1,
                )
                t = mix_levels(v, x)
                lift[f, pl.ds(y, a, stride=pitch), :] = t[:, :w] * spread[f, pl.ds(y, 1), :]
                lift[f, pl.ds(y + 1, a, stride=pitch), :] = t[:, w:] * spread[f, pl.ds(y + 1, 1), :]
            return carry

        lax.fori_loop(0, b // many, one, 0)

    def back_rims(f):
        def put_right(g, v):
            right[1, f, g] = v

        def put_left(g, v):
            left[1, f, g] = v

        def get(s):
            return lift[f, pl.ds(pl.multiple_of(s * pitch, 8), b), :]

        pack_rims(get, put_right, put_left, a // 16, b)
        start_rims(f, 1)

    def back_get(f):
        def get(s, at, count):
            return lift[f, pl.ds(pl.multiple_of(s * pitch + at, 8), count), :]

        return get

    def back_edges(f):
        wait_rims(f, 1)

        def put(s, v):
            tbuf[f, s, 0:8, :] = v[0:8]
            tbuf[f, s, b - 8 : b, :] = v[8:16]

        spans = ((0, 8), (b - 8, 8))
        east_filter(back_get(f), low.at[1], high.at[1], put, bands, f, a // 16, spans)
        start_edges(f, 1)

    def back_east(f):
        def put(s, v):
            tbuf[f, s, 8 : b - 8, :] = v

        east_filter(back_get(f), low.at[1], high.at[1], put, bands, f, a // 16, ((8, b - 16),))

    def keep(f):
        return pltpu.make_async_copy(ext.at[f, :, pl.ds(8, b)], near.at[f], put_sem.at[0, f])

    def blank(f, side):
        return pltpu.make_async_copy(
            ext.at[f, :, pl.ds(side * (b + 8), 8)],
            halo.at[f, :, pl.ds(8 * side, 8)],
            put_sem.at[1 + side, f],
        )

    def blanks(act):
        for side, there in ((0, has_down_y), (1, has_up_y)):

            @pl.when(jnp.logical_not(there))
            def _():
                for f in range(fields):
                    act(blank(f, side))

    def back_inner(f, carry):
        band = inner_s[f]

        def one(i, c):
            for j in range(8):
                p = 16 * i + 2 * j
                r = north_times(band, jnp.concatenate([tbuf[f, p], tbuf[f, p + 1]], axis=1))
                at = pl.ds(8, b)
                ext[f, p, at, :] = ext[f, p, at, :] + r[:, :w]
                ext[f, p + 1, at, :] = ext[f, p + 1, at, :] + r[:, w:]
            return c

        lax.fori_loop(0, a // 16, one, 0)
        keep(f).start()
        return carry

    blanks(lambda copy: copy.start())
    observed = lax.fori_loop(0, slots // 16, weigh_wind, jnp.zeros((8, w), F32))

    def each(part, first, last):
        def one(f, carry):
            part(f)
            return carry

        lax.fori_loop(first, last, one, 0)

    def scatter(f):
        lower(f)
        back_rims(f)

    def scatter_wind(f):
        scatter(f)

        @pl.when(f == 0)
        def _():
            start_rows(1, 2 * tiles // 3, tiles)

    each(scatter_wind, 0, 2)
    each(back_edges, 0, 2)
    wait_rows(1)
    observed = lax.fori_loop(0, slots // 16, weigh_refl, observed)
    parts[0, ix, 1] = observed

    def share(axis, slot, peer, row):
        return pltpu.make_async_remote_copy(
            src_ref=parts.at[row, slot],
            dst_ref=parts.at[row, slot],
            send_sem=sum_sem.at[0, row, peer],
            recv_sem=sum_sem.at[1, row, slot],
            device_id={axis: peer},
            device_id_type=MESH,
        )

    def arrival(axis, peer, row):
        return pltpu.make_async_remote_copy(
            src_ref=parts.at[row, peer],
            dst_ref=parts.at[row, peer],
            send_sem=sum_sem.at[0, row, peer],
            recv_sem=sum_sem.at[1, row, peer],
            device_id={axis: peer},
            device_id_type=MESH,
        )

    for j in range(1, nx):
        share("gx", ix, lax.rem(ix + j, nx), 0).start()
    scatter(2)
    each(back_east, 0, 2)
    for j in range(1, nx):
        arrival("gx", lax.rem(ix + j, nx), 0).wait_recv()
    row_sum = parts[0, 0]
    for j in range(1, nx):
        row_sum = row_sum + parts[0, j]
    parts[1, iy] = row_sum
    for j in range(1, ny):
        share("gy", iy, lax.rem(iy + j, ny), 1).start()
    back_edges(2)
    lax.fori_loop(0, 2, back_inner, 0)
    back_east(2)
    for j in range(1, ny):
        arrival("gy", lax.rem(iy + j, ny), 1).wait_recv()
    all_sum = parts[1, 0]
    for j in range(1, ny):
        all_sum = all_sum + parts[1, j]
    total_v[...] = all_sum
    totals = pltpu.make_async_copy(total_v, total_out, label_sem.at[1])
    totals.start()
    back_inner(2, 0)
    for f in range(fields):
        wait_edges(f, 1)
        keep(f).wait()
    blanks(lambda copy: copy.wait())
    totals.wait()

    for j in range(1, nx):
        share("gx", ix, lax.rem(ix + j, nx), 0).wait_send()
    for j in range(1, ny):
        share("gy", iy, lax.rem(iy + j, ny), 1).wait_send()

    for kind in range(3):

        def sent(j, carry):
            row_copy(kind, j).wait_send()
            return carry

        lax.fori_loop(1, tiles, sent, 0)

    for sweep in range(2):
        for f in range(fields):

            @pl.when(has_up_x)
            def _():
                rim_up(f, sweep).wait_send()

            @pl.when(has_down_x)
            def _():
                rim_down(f, sweep).wait_send()

            @pl.when(has_up_y)
            def _():
                edge_up(f, sweep).wait_send()

            @pl.when(has_down_y)
            def _():
                edge_down(f, sweep).wait_send()


def fused(
    control, inn, wt, owner, level, row, azimuth, spread, vertical, east, north, most
):
    f, a, b, w = control.shape
    nx, ny = lax.axis_size("gx"), lax.axis_size("gy")
    tiles = nx * ny
    slots = tiles * most
    rows = inn.shape[0]
    anywhere = pl.BlockSpec(memory_space=pl.ANY)
    rim = pltpu.VMEM((2, f, a // 16, b, w), F32)
    gates = pltpu.VMEM((2, slots, w), F32)
    told = pltpu.VMEM((tiles, 128), I32)
    dma = pltpu.SemaphoreType.DMA
    return pl.pallas_call(
        functools.partial(fused_kernel, nx, ny, most),
        in_specs=[anywhere] * 11,
        out_specs=(anywhere, anywhere, anywhere),
        out_shape=(
            jax.ShapeDtypeStruct((f, a, b, w), F32),
            jax.ShapeDtypeStruct((f, a, 16, w), F32),
            jax.ShapeDtypeStruct((2, 8, w), F32),
        ),
        scratch_shapes=[
            pltpu.VMEM((4, rows // 128, 128), I32),
            pltpu.VMEM((f, b, w), F32),
            pltpu.VMEM((f, a, a), F32),
            pltpu.VMEM((2, 8, w), F32),
            pltpu.VMEM((f, a, b + 16, w), F32),
            pltpu.VMEM((f, a, b, w), F32),
            pltpu.VMEM((f, a * (b + 8), w), F32),
            pltpu.VMEM((f, a * b, w), F32),
            rim,
            rim,
            rim,
            rim,
            gates,
            gates,
            told,
            gates,
            gates,
            told,
            pltpu.VMEM((4, rows, w), F32),
            pltpu.VMEM((2, rows, 4 * w), BF16),
            pltpu.VMEM((rows // 128, 128), I32),
            pltpu.VMEM((f, b, 3 * (b + 16)), BF16),
            pltpu.VMEM((f, b, 3 * b), BF16),
            pltpu.VMEM((f, 2 * a, 2 * a), BF16),
            pltpu.VMEM((f, 2 * a, 2 * a), BF16),
            pltpu.VMEM((f, 3, 2 * w, 2 * w), BF16),
            pltpu.SMEM(east.shape, F32),
            pltpu.SMEM(north.shape, F32),
            pltpu.VMEM((f, slots, w), F32),
            gates,
            pltpu.VMEM((f, slots, 2 * w), BF16),
            pltpu.VMEM((8, 128), I32),
            pltpu.VMEM((2, max(nx, ny), 2, 8, w), F32),
            pltpu.VMEM((a * b, slots), BF16),
            pltpu.SMEM((8, 128), I32),
            dma((f,)),
            dma((2, 2, 2, f)),
            dma((2, 2, 2, f)),
            dma((2, 3, tiles)),
            dma((3,)),
            dma((2, 2, max(nx, ny))),
            dma((12,)),
            dma((2,)),
            dma((3, f)),
            pltpu.SemaphoreType.REGULAR,
        ],
        compiler_params=pltpu.CompilerParams(
            vmem_limit_bytes=VMEM_BYTES, collective_id=0, has_side_effects=True
        ),
        name="fused",
    )(control, inn, wt, owner, level, row, azimuth, spread, vertical, east, north)


def final_kernel(
    scales, near, halo, totals, north_in, out, cost,
    buf, halo_v, totals_v, north, in_sem, out_sem, halo_sem, total_sem,
):
    fields, a, b, w = out.shape
    parts = in_sem.shape[1]
    zs = a // parts

    def rim(f):
        return pltpu.make_async_copy(halo.at[f], halo_v.at[f], halo_sem.at[f])

    def fetch(f, p):
        at = pl.ds(p * zs, zs)
        return pltpu.make_async_copy(near.at[f, at], buf.at[f, at], in_sem.at[f, p])

    def put(f, p):
        at = pl.ds(p * zs, zs)
        return pltpu.make_async_copy(buf.at[f, at], out.at[f, at], out_sem.at[f, p])

    total = pltpu.make_async_copy(totals, totals_v, total_sem.at[0])
    taps_in = pltpu.make_async_copy(north_in, north, total_sem.at[1])
    taps_in.start()
    for f in range(fields):
        rim(f).start()
        for p in range(parts):
            fetch(f, p).start()
    total.start()
    r = lax.broadcasted_iota(I32, (16, 48), 0)
    c = lax.broadcasted_iota(I32, (16, 48), 1)
    j = c & 15
    distance = jnp.where(r < 8, r + 8 - j, 8 + j - r)
    fits = ((r >> 3) == (j >> 3)) & (distance <= 8)
    taps_in.wait()

    for f in range(fields):
        taps = taps_at(north, f, distance, fits)
        high = taps.astype(BF16).astype(F32)
        band = jnp.where(c >= 32, taps - high, high).astype(BF16)
        rim(f).wait()
        for part in range(parts):
            fetch(f, part).wait()
            for i in range(zs // 8):
                first = part * zs + i * 8
                x = jnp.concatenate([halo_v[f, first + z] for z in range(8)], axis=1)
                t = north_times(band, x)
                for z in range(8):
                    here = t[:, z * w : (z + 1) * w]
                    buf[f, first + z, 0:8] = buf[f, first + z, 0:8] + here[0:8]
                    buf[f, first + z, b - 8 : b] = buf[f, first + z, b - 8 : b] + here[8:16]
            put(f, part).start()
    total.wait()
    for k in range(2):
        cost[k] = jnp.sum(totals_v[k]) * scales[k]
    for f in range(fields):
        for p in range(parts):
            put(f, p).wait()


def final(scales, near, halo, totals, north):
    f, a, b, w = near.shape
    smem = pl.BlockSpec(memory_space=pltpu.SMEM)
    anywhere = pl.BlockSpec(memory_space=pl.ANY)
    return pl.pallas_call(
        functools.partial(final_kernel, scales),
        in_specs=[anywhere] * 4,
        out_specs=(anywhere, smem),
        out_shape=(
            jax.ShapeDtypeStruct(near.shape, F32),
            jax.ShapeDtypeStruct((2,), F32),
        ),
        scratch_shapes=[
            pltpu.VMEM((f, a, b, w), F32),
            pltpu.VMEM((f, a, 16, w), F32),
            pltpu.VMEM(totals.shape, F32),
            pltpu.SMEM(north.shape, F32),
            pltpu.SemaphoreType.DMA((f, 2)),
            pltpu.SemaphoreType.DMA((f, 2)),
            pltpu.SemaphoreType.DMA((f,)),
            pltpu.SemaphoreType.DMA((2,)),
        ],
        compiler_params=pltpu.CompilerParams(vmem_limit_bytes=VMEM_BYTES),
        name="final",
    )(near, halo, totals, north)


def body(
    control, spread, kernel_east, kernel_north, vertical,
    tile_owner, gate_level, tile_row, beam_azimuth, innovation, obs_weight,
):
    tiles = lax.axis_size("gx") * lax.axis_size("gy")
    most = 2 * tile_owner.shape[0] // tiles
    lanes = [x.reshape(-1, 128) for x in (tile_owner, gate_level, tile_row, beam_azimuth)]
    near, halo, totals = fused(
        control, innovation, obs_weight, *lanes, spread, vertical, kernel_east, kernel_north, most
    )
    scales = [0.5 / (control.size * tiles), 0.5 / (innovation.size * tiles)]
    return final(scales, near, halo, totals, kernel_north)


def solution(mesh):
    both = ("gx", "gy")
    placed = (
        P(None, None, "gy", "gx"),
        P(None, "gy", "gx"),
        P(),
        P(),
        P(),
        P(both),
        P(both),
        P(both),
        P(both),
        P(both, None, None),
        P(both, None, None),
    )
    return jax.shard_map(
        body,
        mesh=mesh,
        in_specs=placed,
        out_specs=(P(None, None, "gy", "gx"), P()),
        check_vma=False,
    )
```
